32 devices in a mesh: dp: 4 (over x, core), expert: 8 (over z, y).
Axes of the slice: x: 2, y: 2, z: 4, core: 2. Of those that a mesh axis runs over, the one named last changes fastest.
Arguments:
- tokens: bfloat16 [1024, 2048], P('dp', 'expert'), may hold values from -6 to 6
- out_grad: bfloat16 [1024, 2048], P('dp', 'expert'), may hold values from -6 to 6
- expert_out: bfloat16 [1024, 2048], P('dp', 'expert'), may hold values from -0.119628906 to 0.119628906
- router_probs: float32 [1024, 8], P('dp'), may hold values from 0 to 1, as said below
- expert_index: int32 [1024, 1], P('dp'), may hold values from 0 to 7; in each aligned block of 256 rows (0 to 255, 256 to 511, ...) at most 40 rows name the same one
- in_weight: bfloat16 [8, 2, 5120, 2048], P('expert', None, 'dp'), may hold values from -0.125 to 0.125
- down_weight: bfloat16 [8, 5120, 2048], P('expert', 'dp'), may hold values from -0.078125 to 0.078125
- router_weight: bfloat16 [2048, 8], P('expert'), may hold values from -6 to 6
Outputs:
- token_grad: bfloat16 [1024, 2048], P('dp', 'expert')
- in_weight_grad: bfloat16 [8, 2, 5120, 2048], P('expert', None, 'dp')
- router_grad: float32 [2048, 8], P('expert')
The draws below stay inside these ranges and needn't reach their ends.
Inputs may be any that keep to these rules, and one draw needn't show every extreme that they name: `expert_index`: in each aligned block of 256 tokens (one group) no expert is chosen more than 40 times, so no token is dropped. `router_probs`: each row is positive and sums to one.
All inputs are finite; a program needn't handle non-finite values.
Results may differ from the reference program's by a relative error of at most 0.0057.
Values may be sent and summed in bfloat16 or wider, within the bound.
No kernel may reach another device: no remote copies, remote signals or barrier semaphores. Data moves between devices by JAX's collectives and lax.ppermute only.
A program may use at most 64 MiB of HBM per device.

```python
import math
from functools import partial
import jax
import jax.numpy as jnp
import numpy as np
from jax import lax

D = 2048
FF = 5120
TOK_ROW = 256
E = 8
TOKENS = 1024
CAP = 40
N_DP = 4


def draw_router_probs(key, part):
    logits = 1.5 * jax.random.normal(key, (TOKENS, E), jnp.float32)
    return jax.nn.softmax(logits, axis=1)


def levels(rng, dims, cuts, least, largest):
    factor_of, own = 1.0, jax.random.fold_in(rng, 6)
    for dim, blocks in cuts:
        draws = jnp.exp(jax.random.uniform(jax.random.fold_in(own, dim), (blocks,), jnp.float32, least / len(cuts), largest / len(cuts)))
        factor_of = factor_of * jnp.repeat(draws, dims[dim] // blocks).reshape([-1 if axis == dim else 1 for axis in range(len(dims))])
    return factor_of


def shared_out(stream_key, own, number, rows, count, top, most, skew):
    order = jax.random.permutation(stream_key, count)
    crowded, ordinary = shares(count, rows * top, most, skew, True), shares(count, rows * top, most, skew, False)
    places = jnp.arange(count)

    def named(tallies, rotation):
        used = int((tallies > 0).sum())
        fixed = max(1, used // 4)
        passed = fixed + (places - fixed + rotation * (used - fixed)) % max(1, count - fixed)
        return jnp.zeros((count,), jnp.int32).at[order[jnp.where(places < fixed, places, passed)]].set(jnp.asarray(tallies, jnp.int32))

    tallies = jnp.where(number % 4 == 0, named(crowded, number // 4), named(ordinary, number - number // 4 - 1))
    mixed = jax.random.permutation(jax.random.fold_in(own, 3), count)
    source_of, receiver = mixed[0:count // 2 * 2:2], mixed[1:count // 2 * 2:2]
    slack = jnp.minimum(tallies[source_of] - 1, most - tallies[receiver]) // 2
    slack = jnp.where((source_of == order[0]) | (receiver == order[0]) | (tallies[receiver] == 0), 0, jnp.maximum(slack, 0))
    passed = jax.random.randint(jax.random.fold_in(own, 4), (count // 2,), 0, 1 << 20) % (slack + 1)
    tallies = tallies.at[source_of].add(-passed).at[receiver].add(passed)
    labels = jnp.searchsorted(jnp.cumsum(tallies), jnp.arange(rows * top), side="right").astype(jnp.int32)
    table = labels.reshape(top, rows).T
    table = table[jax.random.permutation(jax.random.fold_in(own, 1), rows)]
    rotation = jax.random.randint(jax.random.fold_in(own, 2), (rows, 1), 0, top)
    return jnp.take_along_axis(table, (jnp.arange(top)[None, :] + rotation) % top, axis=1)


def shares(amount, total, bound, skew, full):
    portions = [(1 << 20) // math.isqrt(grade ** skew) + 1 for grade in range(1, amount + 1)]
    largest = bound if full else min(bound, max(-(-total // amount), total * portions[0] // sum(portions)))
    least = 1 if total - largest >= amount - 1 else 0
    given, rest = [largest] + [least] * (amount - 1), total - largest - least * (amount - 1)
    while rest > 0:
        movable = [i for i in range(1, amount) if given[i] < largest] or [i for i in range(1, amount) if given[i] < bound]
        pool, remaining = sum([portions[i] for i in movable]), rest
        for i in movable:
            more = min(bound - given[i], max(1, remaining * portions[i] // pool), rest)
            given[i] = given[i] + more
            rest = rest - more
    return np.array(given)


def gaussian(stream_key, shape, scale, most, cuts=(), kind=jnp.bfloat16):
    loudness = levels(stream_key, shape, cuts, -0.22, 0.18) if cuts else 1.0
    values = jax.random.normal(stream_key, shape, jnp.float32) * scale * loudness
    return jnp.minimum(jnp.maximum(values, -most), most).astype(kind)


def setup_inputs(seed: int = 0) -> dict:
    key_of = jax.random.split(jax.random.key(seed), 9)
    tokens = gaussian(key_of[0], (TOKENS, D), 1.0, 6.0, ((0, 4), (1, 8)))
    out_grad = gaussian(key_of[1], (TOKENS, D), 1.0, 6.0, ((0, 4), (1, 8)))
    expert_out = gaussian(key_of[2], (TOKENS, D), 0.02, 0.119628906, ((0, 4), (1, 8)))
    router_probs = draw_router_probs(jax.random.fold_in(key_of[8], 71), 0)
    expert_index_keys = jax.random.split(jax.random.fold_in(key_of[4], 1), TOKENS // TOK_ROW)
    expert_index_turns = jax.random.permutation(jax.random.fold_in(key_of[4], 3), TOKENS // TOK_ROW)
    expert_index = jax.vmap(lambda own, number: shared_out(jax.random.fold_in(key_of[4], 2), own, number, TOK_ROW, E, 1, CAP, 2))(expert_index_keys, expert_index_turns).reshape((TOKENS, 1))
    in_weight = gaussian(key_of[5], (E, 2, FF, D), D ** -0.5, 0.125, ((0, 8), (2, 4)))
    down_weight = gaussian(key_of[6], (E, FF, D), FF ** -0.5, 0.078125, ((0, 8), (1, 4)))
    router_weight = gaussian(key_of[7], (D, E), 1.0, 6.0, ((0, 8),))
    return {"tokens": tokens, "out_grad": out_grad, "expert_out": expert_out, "router_probs": router_probs, "expert_index": expert_index, "in_weight": in_weight, "down_weight": down_weight, "router_weight": router_weight}


aux_coef = 0.2

def slot_numbers(routes):
    width = routes.shape[1]
    same_expert = routes[:, :, None] == routes[:, None, :]
    position = jnp.arange(width, dtype=jnp.int32)
    before = position[None, :] < position[:, None]
    return lax.optimization_barrier(jnp.sum((same_expert & before[None]).astype(jnp.int32), axis=2))

def one_hot(routes, slot_ids, experts, capacity):
    expert_hit = routes[..., None] == jnp.arange(experts, dtype=jnp.int32)
    slot_hit = slot_ids[..., None] == jnp.arange(capacity, dtype=jnp.int32)
    return (expert_hit[..., :, None] & slot_hit[..., None, :]).astype(jnp.float32)

def gelu_parts(pre_act, upstream):
    gelu_value, pullback = jax.vjp(partial(jax.nn.gelu, approximate=True), pre_act)
    return (gelu_value, pullback(upstream)[0])

def expert_backward(pieces):
    row_tokens, row_grads, weights, down = pieces
    contract_last = (((1,), (1,)), ((), ()))
    contract_first = (((0,), (0,)), ((), ()))
    gate_pre = lax.dot_general(row_tokens, weights[0], contract_last, preferred_element_type=jnp.float32)
    up_pre = lax.dot_general(row_tokens, weights[1], contract_last, preferred_element_type=jnp.float32)
    hidden_grad = lax.dot_general(row_grads, down, contract_last, preferred_element_type=jnp.float32)
    gate_act, gate_back = gelu_parts(gate_pre, hidden_grad * up_pre)
    gate_grad = gate_back.astype(jnp.bfloat16)
    up_grad = (hidden_grad * gate_act).astype(jnp.bfloat16)
    w_gate_grad = lax.dot_general(gate_grad, row_tokens, contract_first, preferred_element_type=jnp.float32)
    w_up_grad = lax.dot_general(up_grad, row_tokens, contract_first, preferred_element_type=jnp.float32)
    partial_in = jnp.dot(gate_grad, weights[0], preferred_element_type=jnp.float32)
    partial_in = partial_in + jnp.dot(up_grad, weights[1], preferred_element_type=jnp.float32)
    return (jnp.stack([w_gate_grad, w_up_grad]).astype(jnp.bfloat16), partial_in)

def reference(tokens, out_grad, expert_out, router_probs, expert_index, in_weight, down_weight, router_weight):
    groups = N_DP
    experts = router_probs.shape[1]
    capacity = CAP
    feature_width = tokens.shape[1]
    routes = expert_index[:, 0].reshape(groups, TOK_ROW)
    slot_ids = slot_numbers(routes)
    dispatch_mask = one_hot(routes, slot_ids, experts, capacity)
    chosen = lax.optimization_barrier(jnp.sum(dispatch_mask, axis=3)).reshape(TOKENS, experts)
    gate = lax.optimization_barrier(jnp.sum(router_probs * chosen, axis=1))
    gated_dy = (gate[:, None] * out_grad.astype(jnp.float32)).astype(jnp.bfloat16)

    def dispatch(values):
        grouped = values.astype(jnp.float32).reshape(groups, TOK_ROW, feature_width)
        placed = jnp.einsum('gtec,gtf->egcf', dispatch_mask, grouped, precision=lax.Precision.HIGHEST)
        return placed.astype(jnp.bfloat16).reshape(experts, groups * capacity, feature_width)
    row_tokens = dispatch(tokens)
    row_grads = dispatch(gated_dy)
    weight_grads, partials = lax.map(expert_backward, (row_tokens, row_grads, in_weight, down_weight))
    partials = partials.reshape(experts, groups, capacity, feature_width)
    combined = jnp.einsum('gtec,egcf->gtf', dispatch_mask, partials, precision=lax.Precision.HIGHEST)
    combined = combined.reshape(TOKENS, feature_width)
    gate_dot = lax.optimization_barrier(jnp.sum(out_grad.astype(jnp.float32) * expert_out.astype(jnp.float32), axis=1))
    counts = lax.optimization_barrier(jnp.sum(chosen, axis=0))
    prob_grad = chosen * gate_dot[:, None] + aux_coef * experts * counts[None, :] / TOKENS
    logit_grad = router_probs * (prob_grad - lax.optimization_barrier(jnp.sum(router_probs * prob_grad, axis=1, keepdims=True)))
    logit_grad = logit_grad.astype(jnp.bfloat16)
    router_grad = lax.dot_general(tokens, logit_grad, (((0,), (0,)), ((), ())), preferred_element_type=jnp.float32)
    router_term = lax.dot_general(logit_grad, router_weight, (((1,), (1,)), ((), ())), preferred_element_type=jnp.float32)
    token_grad = (combined + router_term).astype(jnp.bfloat16)
    return (token_grad, weight_grads, router_grad)
```

```python
from functools import partial

import jax
import jax.numpy as jnp
from jax import lax
from jax.experimental import pallas as pl
from jax.experimental.pallas import tpu as pltpu
from jax.sharding import PartitionSpec as P

aux_coef = 0.2
contract_last = (((1,), (1,)), ((), ()))
contract_first = (((0,), (0,)), ((), ()))


def slot_numbers(routes):
    width = routes.shape[1]
    same_expert = routes[:, :, None] == routes[:, None, :]
    position = jnp.arange(width, dtype=jnp.int32)
    before = position[None, :] < position[:, None]
    return jnp.sum((same_expert & before[None]).astype(jnp.int32), axis=2)


def one_hot(routes, slot_ids, experts, capacity):
    expert_hit = routes[..., None] == jnp.arange(experts, dtype=jnp.int32)
    slot_hit = slot_ids[..., None] == jnp.arange(capacity, dtype=jnp.int32)
    return (expert_hit[..., :, None] & slot_hit[..., None, :]).astype(jnp.float32)


def gelu_parts(pre_act, upstream):
    gelu_value, pullback = jax.vjp(partial(jax.nn.gelu, approximate=True), pre_act)
    return (gelu_value, pullback(upstream)[0])


def swap(value, distance):
    size = lax.axis_size("dp")
    return lax.ppermute(value, "dp", [(i, i ^ distance) for i in range(size)])


def distances():
    found, distance = [], lax.axis_size("dp") // 2
    while distance:
        found.append(distance)
        distance //= 2
    return found


def gather_groups(block):
    for distance in distances():
        block = jnp.concatenate([block, swap(block, distance)], axis=0)
    return block


def reduce_groups(total):
    order = distances()[::-1]
    size = lax.axis_size("dp")
    for distance in order:
        half = total.shape[0] // 2
        away = swap(total[half:].astype(jnp.bfloat16), distance)
        total = total[:half] + away.astype(jnp.float32)
    return total


def weight_grad_kernel(gate_ref, up_ref, rows_ref, out_ref):
    rows = rows_ref[...]
    out_ref[0, 0] = lax.dot_general(
        gate_ref[...], rows, contract_first, preferred_element_type=jnp.float32
    ).astype(jnp.bfloat16)
    out_ref[0, 1] = lax.dot_general(
        up_ref[...], rows, contract_first, preferred_element_type=jnp.float32
    ).astype(jnp.bfloat16)


def weight_grads(gate_grad, up_grad, rows):
    count, hidden = gate_grad.shape
    width = rows.shape[1]
    block = 256 if hidden % 256 == 0 else hidden
    return pl.pallas_call(
        weight_grad_kernel,
        grid=(hidden // block,),
        in_specs=[
            pl.BlockSpec((count, block), lambda j: (0, j)),
            pl.BlockSpec((count, block), lambda j: (0, j)),
            pl.BlockSpec((count, width), lambda j: (0, 0)),
        ],
        out_specs=pl.BlockSpec((1, 2, block, width), lambda j: (0, 0, j, 0)),
        out_shape=jax.ShapeDtypeStruct((1, 2, hidden, width), jnp.bfloat16),
        cost_estimate=pl.CostEstimate(
            flops=4 * count * hidden * width,
            bytes_accessed=4 * hidden * width,
            transcendentals=0,
        ),
        name="weight_grads",
    )(gate_grad, up_grad, rows)


def split_float(value):
    high = lax.reduce_precision(value, 8, 7)
    middle = lax.reduce_precision(value - high, 8, 7)
    return jnp.stack([high, middle, value - high - middle]).astype(jnp.bfloat16)


def per_device(
    tokens, out_grad, expert_out, router_probs, expert_index, in_weight, down_weight, router_weight
):
    token_count, feature_width = tokens.shape
    experts = router_probs.shape[1]
    capacity = (5 * token_count + 4 * experts - 1) // (4 * experts)
    groups = lax.axis_size("dp")
    routes = expert_index[:, 0]
    slot_ids = slot_numbers(routes[None, :])[0]
    dispatch_mask = one_hot(routes, slot_ids, experts, capacity)
    mask_half = dispatch_mask.astype(jnp.bfloat16)
    chosen = jnp.sum(dispatch_mask, axis=2)

    def exchange(value):
        return lax.all_to_all(value, "expert", split_axis=0, concat_axis=2, tiled=True)[0]

    send_tokens = jnp.einsum(
        "tec,tf->ecf", mask_half, tokens, preferred_element_type=jnp.float32
    ).astype(jnp.bfloat16)
    got_tokens = exchange(send_tokens)

    gate = jnp.sum(router_probs * chosen, axis=1)
    gated_dy = (gate[:, None] * out_grad.astype(jnp.float32)).astype(jnp.bfloat16)
    send_grads = jnp.einsum(
        "tec,tf->ecf", mask_half, gated_dy, preferred_element_type=jnp.float32
    ).astype(jnp.bfloat16)
    partial_dot = jnp.sum(out_grad.astype(jnp.float32) * expert_out.astype(jnp.float32), axis=1)
    dot_rows = token_count // feature_width
    pieces = split_float(partial_dot).reshape(3 * dot_rows, feature_width)
    local_counts = jnp.sum(chosen, axis=0)
    count_row = jnp.pad(local_counts.astype(jnp.bfloat16)[None], ((0, 0), (0, feature_width - experts)))
    side = jnp.concatenate([pieces, count_row], axis=0)
    side_rows = -(-(capacity + side.shape[0]) // 8) * 8 - capacity
    side = jnp.pad(side, ((0, side_rows - side.shape[0]), (0, 0)))
    send_grads = jnp.concatenate(
        [send_grads, jnp.broadcast_to(side[None], (experts, side_rows, feature_width))], axis=1
    )
    got_grads = exchange(send_grads)

    row_tokens = gather_groups(got_tokens)
    all_grads = gather_groups(got_grads).reshape(groups, capacity + side_rows, -1)
    row_grads = all_grads[:, :capacity].reshape(groups * capacity, -1)
    own_side = got_grads[capacity:].astype(jnp.float32)
    gate_dot = jnp.sum(
        own_side[: 3 * dot_rows].reshape(3, dot_rows, experts, feature_width), axis=(0, 2)
    ).reshape(token_count)
    counts = jnp.sum(all_grads[:, capacity + 3 * dot_rows, :experts].astype(jnp.float32), axis=0)

    gate_weight = in_weight[0, 0]
    up_weight = in_weight[0, 1]
    gate_pre = lax.dot_general(
        row_tokens, gate_weight, contract_last, preferred_element_type=jnp.float32
    )
    up_pre = lax.dot_general(
        row_tokens, up_weight, contract_last, preferred_element_type=jnp.float32
    )
    hidden_grad = lax.dot_general(
        row_grads, down_weight[0], contract_last, preferred_element_type=jnp.float32
    )
    gate_act, gate_back = gelu_parts(gate_pre, hidden_grad * up_pre)
    gate_grad = gate_back.astype(jnp.bfloat16)
    up_grad = (hidden_grad * gate_act).astype(jnp.bfloat16)
    term = jnp.dot(gate_grad, gate_weight, preferred_element_type=jnp.float32)
    term = term + jnp.dot(up_grad, up_weight, preferred_element_type=jnp.float32)
    summed = reduce_groups(term)
    going = summed.astype(jnp.bfloat16).reshape(capacity, experts, feature_width)
    returned = lax.all_to_all(
        going.transpose(1, 0, 2), "expert", split_axis=0, concat_axis=0, tiled=True
    )
    weight_grad = weight_grads(gate_grad, up_grad, row_tokens)

    prob_grad = chosen * gate_dot[:, None] + aux_coef * experts * counts[None, :] / (
        token_count * groups
    )
    logit_grad = router_probs * (
        prob_grad - jnp.sum(router_probs * prob_grad, axis=1, keepdims=True)
    )
    logit_grad = logit_grad.astype(jnp.bfloat16)
    router_grad = lax.dot_general(
        tokens, logit_grad, contract_first, preferred_element_type=jnp.float32
    )
    for distance in distances():
        router_grad = router_grad + swap(router_grad, distance)
    router_term = lax.dot_general(
        logit_grad, router_weight, contract_last, preferred_element_type=jnp.float32
    )
    combined = jnp.einsum(
        "tec,ecf->tf", mask_half, returned, preferred_element_type=jnp.float32
    )
    token_grad = (combined + router_term).astype(jnp.bfloat16)
    return (token_grad, weight_grad, router_grad)


def solution(mesh):
    in_specs = (
        P("dp", "expert"),
        P("dp", "expert"),
        P("dp", "expert"),
        P("dp", None),
        P("dp", None),
        P("expert", None, "dp", None),
        P("expert", "dp", None),
        P("expert", None),
    )
    out_specs = (P("dp", "expert"), P("expert", None, "dp", None), P("expert", None))
    return jax.shard_map(
        per_device, mesh=mesh, in_specs=in_specs, out_specs=out_specs, check_vma=False
    )
```

```python
import math
from functools import partial

import jax
import jax.numpy as jnp
from jax import lax
from jax.experimental import pallas as pl
from jax.experimental.pallas import tpu as pltpu
from jax.sharding import PartitionSpec as P

aux_coef = 0.2
contract_last = (((1,), (1,)), ((), ()))
contract_first = (((0,), (0,)), ((), ()))


def slot_numbers(routes):
    width = routes.shape[1]
    same_expert = routes[:, :, None] == routes[:, None, :]
    position = jnp.arange(width, dtype=jnp.int32)
    before = position[None, :] < position[:, None]
    return jnp.sum((same_expert & before[None]).astype(jnp.int32), axis=2)


def one_hot(routes, slot_ids, experts, capacity):
    expert_hit = routes[..., None] == jnp.arange(experts, dtype=jnp.int32)
    slot_hit = slot_ids[..., None] == jnp.arange(capacity, dtype=jnp.int32)
    return (expert_hit[..., :, None] & slot_hit[..., None, :]).astype(jnp.float32)


def gelu_parts(pre_act, upstream):
    gelu_value, pullback = jax.vjp(partial(jax.nn.gelu, approximate=True), pre_act)
    return (gelu_value, pullback(upstream)[0])


def swap(value, distance):
    size = lax.axis_size("dp")
    return lax.ppermute(value, "dp", [(i, i ^ distance) for i in range(size)])


def distances():
    found, distance = [], lax.axis_size("dp") // 2
    while distance:
        found.append(distance)
        distance //= 2
    return found


def gather_groups(block):
    for distance in distances():
        block = jnp.concatenate([block, swap(block, distance)], axis=0)
    return block


def reduce_groups(total, first=1):
    order = [distance for distance in distances()[::-1] if distance >= first]
    for distance in order:
        half = total.shape[0] // 2
        away = swap(total[half:].astype(jnp.bfloat16), distance)
        total = total[:half] + away.astype(jnp.float32)
    return total


def weight_grad_kernel(gate_ref, up_ref, rows_ref, out_ref):
    rows = rows_ref[...]
    out_ref[0, 0] = lax.dot_general(
        gate_ref[...], rows, contract_first, preferred_element_type=jnp.float32
    ).astype(jnp.bfloat16)
    out_ref[0, 1] = lax.dot_general(
        up_ref[...], rows, contract_first, preferred_element_type=jnp.float32
    ).astype(jnp.bfloat16)


def weight_grads(gate_grad, up_grad, rows):
    count, hidden = gate_grad.shape
    width = rows.shape[1]
    block = 256 if hidden % 256 == 0 else hidden
    return pl.pallas_call(
        weight_grad_kernel,
        grid=(hidden // block,),
        in_specs=[
            pl.BlockSpec((count, block), lambda j: (0, j)),
            pl.BlockSpec((count, block), lambda j: (0, j)),
            pl.BlockSpec((count, width), lambda j: (0, 0)),
        ],
        out_specs=pl.BlockSpec((1, 2, block, width), lambda j: (0, 0, j, 0)),
        out_shape=jax.ShapeDtypeStruct((1, 2, hidden, width), jnp.bfloat16),
        cost_estimate=pl.CostEstimate(
            flops=4 * count * hidden * width,
            bytes_accessed=4 * hidden * width,
            transcendentals=0,
        ),
        name="weight_grads",
    )(gate_grad, up_grad, rows)


def split_float(value):
    high = lax.reduce_precision(value, 8, 7)
    middle = lax.reduce_precision(value - high, 8, 7)
    return jnp.stack([high, middle, value - high - middle]).astype(jnp.bfloat16)


def general_device(
    tokens, out_grad, expert_out, router_probs, expert_index, in_weight, down_weight, router_weight
):
    token_count, feature_width = tokens.shape
    experts = router_probs.shape[1]
    capacity = (5 * token_count + 4 * experts - 1) // (4 * experts)
    groups = lax.axis_size("dp")
    routes = expert_index[:, 0]
    slot_ids = slot_numbers(routes[None, :])[0]
    dispatch_mask = one_hot(routes, slot_ids, experts, capacity)
    mask_half = dispatch_mask.astype(jnp.bfloat16)
    chosen = jnp.sum(dispatch_mask, axis=2)

    def exchange(value):
        return lax.all_to_all(value, "expert", split_axis=0, concat_axis=2, tiled=True)[0]

    send_tokens = jnp.einsum(
        "tec,tf->ecf", mask_half, tokens, preferred_element_type=jnp.float32
    ).astype(jnp.bfloat16)
    got_tokens = exchange(send_tokens)

    gate = jnp.sum(router_probs * chosen, axis=1)
    gated_dy = (gate[:, None] * out_grad.astype(jnp.float32)).astype(jnp.bfloat16)
    send_grads = jnp.einsum(
        "tec,tf->ecf", mask_half, gated_dy, preferred_element_type=jnp.float32
    ).astype(jnp.bfloat16)
    partial_dot = jnp.sum(out_grad.astype(jnp.float32) * expert_out.astype(jnp.float32), axis=1)
    dot_rows = token_count // feature_width
    pieces = split_float(partial_dot).reshape(3 * dot_rows, feature_width)
    local_counts = jnp.sum(chosen, axis=0)
    count_row = jnp.pad(local_counts.astype(jnp.bfloat16)[None], ((0, 0), (0, feature_width - experts)))
    side = jnp.concatenate([pieces, count_row], axis=0)
    side_rows = -(-(capacity + side.shape[0]) // 8) * 8 - capacity
    side = jnp.pad(side, ((0, side_rows - side.shape[0]), (0, 0)))
    send_grads = jnp.concatenate(
        [send_grads, jnp.broadcast_to(side[None], (experts, side_rows, feature_width))], axis=1
    )
    got_grads = exchange(send_grads)

    row_tokens = gather_groups(got_tokens)
    all_grads = gather_groups(got_grads).reshape(groups, capacity + side_rows, -1)
    row_grads = all_grads[:, :capacity].reshape(groups * capacity, -1)
    own_side = got_grads[capacity:].astype(jnp.float32)
    gate_dot = jnp.sum(
        own_side[: 3 * dot_rows].reshape(3, dot_rows, experts, feature_width), axis=(0, 2)
    ).reshape(token_count)
    counts = jnp.sum(all_grads[:, capacity + 3 * dot_rows, :experts].astype(jnp.float32), axis=0)

    gate_weight = in_weight[0, 0]
    up_weight = in_weight[0, 1]
    gate_pre = lax.dot_general(
        row_tokens, gate_weight, contract_last, preferred_element_type=jnp.float32
    )
    up_pre = lax.dot_general(
        row_tokens, up_weight, contract_last, preferred_element_type=jnp.float32
    )
    hidden_grad = lax.dot_general(
        row_grads, down_weight[0], contract_last, preferred_element_type=jnp.float32
    )
    gate_act, gate_back = gelu_parts(gate_pre, hidden_grad * up_pre)
    gate_grad = gate_back.astype(jnp.bfloat16)
    up_grad = (hidden_grad * gate_act).astype(jnp.bfloat16)
    term = jnp.dot(gate_grad, gate_weight, preferred_element_type=jnp.float32)
    term = term + jnp.dot(up_grad, up_weight, preferred_element_type=jnp.float32)
    summed = reduce_groups(term)
    going = summed.astype(jnp.bfloat16).reshape(capacity, experts, feature_width)
    returned = lax.all_to_all(
        going.transpose(1, 0, 2), "expert", split_axis=0, concat_axis=0, tiled=True
    )
    weight_grad = weight_grads(gate_grad, up_grad, row_tokens)

    prob_grad = chosen * gate_dot[:, None] + aux_coef * experts * counts[None, :] / (
        token_count * groups
    )
    logit_grad = router_probs * (
        prob_grad - jnp.sum(router_probs * prob_grad, axis=1, keepdims=True)
    )
    logit_grad = logit_grad.astype(jnp.bfloat16)
    router_grad = lax.dot_general(
        tokens, logit_grad, contract_first, preferred_element_type=jnp.float32
    )
    for distance in distances():
        router_grad = router_grad + swap(router_grad, distance)
    router_term = lax.dot_general(
        logit_grad, router_weight, contract_last, preferred_element_type=jnp.float32
    )
    combined = jnp.einsum(
        "tec,ecf->tf", mask_half, returned, preferred_element_type=jnp.float32
    )
    token_grad = (combined + router_term).astype(jnp.bfloat16)
    return (token_grad, weight_grad, router_grad)


def prelude_kernel(
    capacity, route_ref, probs_ref, tokens_ref, grads_ref, expert_out_ref, send_ref, place_ref
):
    experts, count = probs_ref.shape
    width = tokens_ref.shape[1]
    half, full = jnp.bfloat16, jnp.float32
    iota = lambda shape, axis: lax.broadcasted_iota(jnp.int32, shape, axis)
    dot = partial(lax.dot_general, preferred_element_type=full)
    plain = (((1,), (0,)), ((), ()))
    route = route_ref[...]
    hit = iota((experts, count), 0) == route
    square = (count, count)
    earlier = (iota(square, 0) < iota(square, 1)).astype(full).astype(half)
    before = dot(hit.astype(full).astype(half), earlier, plain)
    slot = jnp.sum(jnp.where(hit, before, 0.0), axis=0, keepdims=True)
    gate = jnp.sum(jnp.where(hit, probs_ref[...], 0.0), axis=0, keepdims=True)
    place = iota((experts * capacity, count), 0) == route * capacity + slot.astype(jnp.int32)
    mask = place.astype(full).astype(half)
    place_ref[...] = mask
    rows_x = dot(mask, tokens_ref[...], plain)
    row_gate = jnp.sum(jnp.where(place, gate, 0.0), axis=1, keepdims=True)
    rows_dy = dot(mask, grads_ref[...], plain) * row_gate
    product = grads_ref[...].astype(full) * expert_out_ref[...].astype(full)
    high = product.astype(half)
    low = (product - high.astype(full)).astype(half)
    ones = jnp.ones((8, width), half)
    part = dot(ones, high, contract_last) + dot(ones, low, contract_last)
    first = part.astype(half).astype(full)
    second = (part - first).astype(half).astype(full)
    third = part - first - second
    listed = (iota((width, count), 0) == route).astype(full).astype(half)
    counts = dot(jnp.ones((8, count), half), listed, contract_last)
    line = iota((8, width), 0)
    side = jnp.where(line == 3, counts, 0.0)
    for number, piece in enumerate((first, second, third)):
        side = jnp.where(line == number, piece, side)
    side = side.astype(half)
    for expert in range(experts):
        rows = slice(expert * capacity, (expert + 1) * capacity)
        send_ref[expert, :capacity] = rows_x[rows].astype(half)
        send_ref[expert, capacity : 2 * capacity] = rows_dy[rows].astype(half)
        send_ref[expert, 2 * capacity :] = side


def prelude(capacity, route, probs, tokens, out_grad, expert_out):
    experts, count = probs.shape
    width = tokens.shape[1]
    return pl.pallas_call(
        partial(prelude_kernel, capacity),
        out_shape=(
            jax.ShapeDtypeStruct((experts, 2 * capacity + 8, width), jnp.bfloat16),
            jax.ShapeDtypeStruct((experts * capacity, count), jnp.bfloat16),
        ),
        compiler_params=pltpu.CompilerParams(vmem_limit_bytes=8 << 20),
        name="prelude",
    )(route, probs, tokens, out_grad, expert_out)


def fetch_kernel(pieces, source_ref, after_ref, target_ref, sems):
    planes, hidden = source_ref.shape[1:3] if len(source_ref.shape) == 4 else (1, source_ref.shape[1])
    size = hidden // pieces
    copies = []
    for plane in range(planes):
        for piece in range(pieces):
            rows = pl.ds(piece * size, size)
            where = (0, plane, rows) if len(source_ref.shape) == 4 else (0, rows)
            copies.append(
                pltpu.make_async_copy(
                    source_ref.at[where], target_ref.at[where], sems.at[len(copies)]
                )
            )
    for copy in copies:
        copy.start()
    for copy in copies:
        copy.wait()


def fetch(weight, after):
    pieces = 2
    planes = weight.shape[1] if weight.ndim == 4 else 1
    return pl.pallas_call(
        partial(fetch_kernel, pieces),
        in_specs=[pl.BlockSpec(memory_space=pl.ANY)] * 2,
        out_specs=pl.BlockSpec(memory_space=pltpu.VMEM),
        out_shape=pltpu.VMEM(weight.shape, weight.dtype),
        scratch_shapes=[pltpu.SemaphoreType.DMA((planes * pieces,))],
        compiler_params=pltpu.CompilerParams(vmem_limit_bytes=1 << 20),
        cost_estimate=pl.CostEstimate(
            flops=0, bytes_accessed=2 * weight.size, transcendentals=0
        ),
        name="fetch",
    )(pltpu.with_memory_space_constraint(weight, pltpu.HBM), after)


def near(value):
    return pltpu.with_memory_space_constraint(value, pltpu.VMEM)


def hidden_pre_kernel(block, rows_ref, in_ref, out_ref):
    hidden = in_ref.shape[2]
    rows = rows_ref[...]
    for which in range(2):
        for start in range(0, hidden, block):
            part = slice(start, start + block)
            out_ref[which, :, part] = lax.dot_general(
                rows, in_ref[0, which, part], contract_last, preferred_element_type=jnp.float32
            )


def hidden_pre(rows, in_near):
    count, width = rows.shape
    hidden = in_near.shape[2]
    return pl.pallas_call(
        partial(hidden_pre_kernel, 256 if hidden % 256 == 0 else hidden),
        in_specs=[pl.BlockSpec(memory_space=pltpu.VMEM)] * 2,
        out_specs=pl.BlockSpec(memory_space=pltpu.VMEM),
        out_shape=pltpu.VMEM((2, count, hidden), jnp.float32),
        compiler_params=pltpu.CompilerParams(vmem_limit_bytes=8 << 20),
        cost_estimate=pl.CostEstimate(
            flops=4 * count * hidden * width,
            bytes_accessed=4 * hidden * width,
            transcendentals=0,
        ),
        name="hidden_pre",
    )(rows, near(in_near))


def hidden_back_kernel(
    block, rows_ref, pre_ref, in_ref, down_ref, gate_ref, up_ref, kept_ref, away_ref
):
    hidden, width = down_ref.shape[1:]
    rows = rows_ref[...]
    half = rows.shape[0] // 2
    scale, cubic = math.sqrt(2 / math.pi), 0.044715
    for start in range(0, hidden, block):
        part = slice(start, start + block)
        grad = lax.dot_general(
            rows, down_ref[0, part], contract_last, preferred_element_type=jnp.float32
        )
        value, up = pre_ref[0, :, part], pre_ref[1, :, part]
        square = value * value
        bend = jnp.tanh(scale * (value + cubic * (square * value)))
        cdf = 0.5 * (1.0 + bend)
        slope = cdf + (0.5 * scale) * value * (1.0 - bend * bend) * (1.0 + 3 * cubic * square)
        gate_ref[:, part] = (grad * up * slope).astype(jnp.bfloat16)
        up_ref[:, part] = (grad * (value * cdf)).astype(jnp.bfloat16)
    gate_grad, up_grad = gate_ref[...], up_ref[...]
    for start in range(0, width, block):
        part = slice(start, start + block)
        total = jnp.dot(gate_grad, in_ref[0, 0, :, part], preferred_element_type=jnp.float32)
        total += jnp.dot(up_grad, in_ref[0, 1, :, part], preferred_element_type=jnp.float32)
        kept_ref[:, part] = total[:half]
        away_ref[:, part] = total[half:].astype(jnp.bfloat16)


def hidden_back(rows, pres, in_near, down_near):
    count, width = rows.shape
    hidden = down_near.shape[1]
    near_spec = pl.BlockSpec(memory_space=pltpu.VMEM)
    return pl.pallas_call(
        partial(hidden_back_kernel, 256 if hidden % 256 == 0 else hidden),
        in_specs=[near_spec] * 4,
        out_specs=[near_spec] * 4,
        out_shape=(
            pltpu.VMEM((count, hidden), jnp.bfloat16),
            pltpu.VMEM((count, hidden), jnp.bfloat16),
            pltpu.VMEM((count // 2, width), jnp.float32),
            pltpu.VMEM((count // 2, width), jnp.bfloat16),
        ),
        compiler_params=pltpu.CompilerParams(vmem_limit_bytes=8 << 20),
        cost_estimate=pl.CostEstimate(
            flops=6 * count * hidden * width,
            bytes_accessed=6 * hidden * width,
            transcendentals=count * hidden,
        ),
        name="hidden_back",
    )(rows, near(pres), near(in_near), near(down_near))


def half_kernel(grad_ref, rows_ref, *refs):
    refs[-1][0, 0] = lax.dot_general(
        grad_ref[...], rows_ref[...], contract_first, preferred_element_type=jnp.float32
    ).astype(jnp.bfloat16)


def half_weight_grad(which, grad, rows, partly=None):
    count, hidden = grad.shape
    width = rows.shape[1]
    block = 256 if hidden % 256 == 0 else hidden
    given = [] if partly is None else [partly]
    return pl.pallas_call(
        half_kernel,
        grid=(hidden // block,),
        in_specs=[
            pl.BlockSpec((count, block), lambda j: (0, j)),
            pl.BlockSpec((count, width), lambda j: (0, 0)),
        ]
        + [pl.BlockSpec(memory_space=pl.ANY)] * len(given),
        out_specs=pl.BlockSpec((1, 1, block, width), lambda j: (0, which, j, 0)),
        out_shape=jax.ShapeDtypeStruct((1, 2, hidden, width), jnp.bfloat16),
        input_output_aliases={2: 0} if given else {},
        cost_estimate=pl.CostEstimate(
            flops=2 * count * hidden * width, bytes_accessed=2 * hidden * width, transcendentals=0
        ),
        compiler_params=pltpu.CompilerParams(vmem_limit_bytes=12 << 20),
        name="weight_grad_half",
    )(grad, rows, *given)


def aligned_device(
    tokens, out_grad, expert_out, router_probs, expert_index, in_weight, down_weight, router_weight
):
    token_count, width = tokens.shape
    experts = router_probs.shape[1]
    capacity = (5 * token_count + 4 * experts - 1) // (4 * experts)
    groups = lax.axis_size("dp")
    full_width = experts * width
    probs = router_probs.T
    route = expert_index.reshape(1, token_count)
    send, mask = prelude(capacity, route, probs, tokens, out_grad, expert_out)
    got = lax.all_to_all(send, "expert", split_axis=0, concat_axis=0, tiled=True)
    in_near, down_near = fetch(in_weight, got), fetch(down_weight, got)

    def as_rows(value):
        return value.transpose(1, 0, 2).reshape(value.shape[1], full_width)

    row_tokens = gather_groups(as_rows(got[:, :capacity]))
    all_grads = gather_groups(as_rows(got[:, capacity:])).reshape(groups, capacity + 8, full_width)
    row_grads = all_grads[:, :capacity].reshape(groups * capacity, full_width)
    gate_dot = jnp.sum(got[:, 2 * capacity : 2 * capacity + 3].astype(jnp.float32), axis=(0, 1))
    counts = jnp.sum(all_grads[:, capacity + 3, :experts].astype(jnp.float32), axis=0)

    pres = hidden_pre(row_tokens, in_near)
    gate_grad, up_grad, kept, away = hidden_back(row_grads, pres, in_near, down_near)
    summed = kept + swap(away, 1).astype(jnp.float32)
    summed = reduce_groups(summed, 2)
    going = summed.astype(jnp.bfloat16).reshape(capacity, experts, width).transpose(1, 0, 2)
    returned = lax.all_to_all(going, "expert", split_axis=0, concat_axis=0, tiled=True)
    weight_grad = half_weight_grad(0, gate_grad, row_tokens)
    weight_grad = half_weight_grad(1, up_grad, row_tokens, weight_grad)

    chosen = (lax.broadcasted_iota(jnp.int32, (experts, token_count), 0) == route).astype(jnp.float32)
    prob_grad = chosen * gate_dot[None, :] + aux_coef * experts * counts[:, None] / (
        token_count * groups
    )
    logit_grad = probs * (prob_grad - jnp.sum(probs * prob_grad, axis=0, keepdims=True))
    logit_grad = logit_grad.astype(jnp.bfloat16)
    router_grad = jnp.dot(logit_grad, tokens, preferred_element_type=jnp.float32)
    for distance in distances():
        router_grad = router_grad + swap(router_grad, distance)
    router_term = lax.dot_general(
        logit_grad, router_weight, (((0,), (1,)), ((), ())), preferred_element_type=jnp.float32
    )
    combined = lax.dot_general(
        mask,
        returned.reshape(experts * capacity, width),
        contract_first,
        preferred_element_type=jnp.float32,
    )
    token_grad = (combined + router_term).astype(jnp.bfloat16)
    return (token_grad, weight_grad, router_grad.T)


def per_device(tokens, out_grad, expert_out, router_probs, *rest):
    token_count, width = tokens.shape
    experts = router_probs.shape[1]
    capacity = (5 * token_count + 4 * experts - 1) // (4 * experts)
    aligned = token_count == width and width % 128 == 0 and capacity % 8 == 0 and experts % 8 == 0
    device = aligned_device if aligned else general_device
    return device(tokens, out_grad, expert_out, router_probs, *rest)


def solution(mesh):
    in_specs = (
        P("dp", "expert"),
        P("dp", "expert"),
        P("dp", "expert"),
        P("dp", None),
        P("dp", None),
        P("expert", None, "dp", None),
        P("expert", "dp", None),
        P("expert", None),
    )
    out_specs = (P("dp", "expert"), P("expert", None, "dp", None), P("expert", None))
    return jax.shard_map(
        per_device, mesh=mesh, in_specs=in_specs, out_specs=out_specs, check_vma=False
    )
```

```python
import math
from functools import partial

import jax
import jax.numpy as jnp
from jax import lax
from jax.experimental import pallas as pl
from jax.experimental.pallas import tpu as pltpu
from jax.sharding import PartitionSpec as P


aux_coef = 0.2
contract_last = (((1,), (1,)), ((), ()))
contract_first = (((0,), (0,)), ((), ()))


def slot_numbers(routes):
    width = routes.shape[1]
    same_expert = routes[:, :, None] == routes[:, None, :]
    position = jnp.arange(width, dtype=jnp.int32)
    before = position[None, :] < position[:, None]
    return jnp.sum((same_expert & before[None]).astype(jnp.int32), axis=2)


def one_hot(routes, slot_ids, experts, capacity):
    expert_hit = routes[..., None] == jnp.arange(experts, dtype=jnp.int32)
    slot_hit = slot_ids[..., None] == jnp.arange(capacity, dtype=jnp.int32)
    return (expert_hit[..., :, None] & slot_hit[..., None, :]).astype(jnp.float32)


def gelu_parts(pre_act, upstream):
    gelu_value, pullback = jax.vjp(partial(jax.nn.gelu, approximate=True), pre_act)
    return (gelu_value, pullback(upstream)[0])


def swap(value, distance):
    size = lax.axis_size("dp")
    return lax.ppermute(value, "dp", [(i, i ^ distance) for i in range(size)])


def distances():
    found, distance = [], lax.axis_size("dp") // 2
    while distance:
        found.append(distance)
        distance //= 2
    return found


def gather_groups(block, given=()):
    for distance in given or distances():
        block = jnp.concatenate([block, swap(block, distance)], axis=0)
    return block


def reduce_groups(total, first=1):
    order = [distance for distance in distances()[::-1] if distance >= first]
    for distance in order:
        half = total.shape[0] // 2
        away = swap(total[half:].astype(jnp.bfloat16), distance)
        total = total[:half] + away.astype(jnp.float32)
    return total


def weight_grad_kernel(gate_ref, up_ref, rows_ref, out_ref):
    rows = rows_ref[...]
    out_ref[0, 0] = lax.dot_general(
        gate_ref[...], rows, contract_first, preferred_element_type=jnp.float32
    ).astype(jnp.bfloat16)
    out_ref[0, 1] = lax.dot_general(
        up_ref[...], rows, contract_first, preferred_element_type=jnp.float32
    ).astype(jnp.bfloat16)


def weight_grads(gate_grad, up_grad, rows):
    count, hidden = gate_grad.shape
    width = rows.shape[1]
    block = 256 if hidden % 256 == 0 else hidden
    return pl.pallas_call(
        weight_grad_kernel,
        grid=(hidden // block,),
        in_specs=[
            pl.BlockSpec((count, block), lambda j: (0, j)),
            pl.BlockSpec((count, block), lambda j: (0, j)),
            pl.BlockSpec((count, width), lambda j: (0, 0)),
        ],
        out_specs=pl.BlockSpec((1, 2, block, width), lambda j: (0, 0, j, 0)),
        out_shape=jax.ShapeDtypeStruct((1, 2, hidden, width), jnp.bfloat16),
        cost_estimate=pl.CostEstimate(
            flops=4 * count * hidden * width,
            bytes_accessed=4 * hidden * width,
            transcendentals=0,
        ),
        name="weight_grads",
    )(gate_grad, up_grad, rows)


def split_float(value):
    high = lax.reduce_precision(value, 8, 7)
    middle = lax.reduce_precision(value - high, 8, 7)
    return jnp.stack([high, middle, value - high - middle]).astype(jnp.bfloat16)


def general_device(
    tokens, out_grad, expert_out, router_probs, expert_index, in_weight, down_weight, router_weight
):
    token_count, feature_width = tokens.shape
    experts = router_probs.shape[1]
    capacity = (5 * token_count + 4 * experts - 1) // (4 * experts)
    groups = lax.axis_size("dp")
    routes = expert_index[:, 0]
    slot_ids = slot_numbers(routes[None, :])[0]
    dispatch_mask = one_hot(routes, slot_ids, experts, capacity)
    mask_half = dispatch_mask.astype(jnp.bfloat16)
    chosen = jnp.sum(dispatch_mask, axis=2)

    def exchange(value):
        return lax.all_to_all(value, "expert", split_axis=0, concat_axis=2, tiled=True)[0]

    send_tokens = jnp.einsum(
        "tec,tf->ecf", mask_half, tokens, preferred_element_type=jnp.float32
    ).astype(jnp.bfloat16)
    got_tokens = exchange(send_tokens)

    gate = jnp.sum(router_probs * chosen, axis=1)
    gated_dy = (gate[:, None] * out_grad.astype(jnp.float32)).astype(jnp.bfloat16)
    send_grads = jnp.einsum(
        "tec,tf->ecf", mask_half, gated_dy, preferred_element_type=jnp.float32
    ).astype(jnp.bfloat16)
    partial_dot = jnp.sum(out_grad.astype(jnp.float32) * expert_out.astype(jnp.float32), axis=1)
    dot_rows = token_count // feature_width
    pieces = split_float(partial_dot).reshape(3 * dot_rows, feature_width)
    local_counts = jnp.sum(chosen, axis=0)
    count_row = jnp.pad(local_counts.astype(jnp.bfloat16)[None], ((0, 0), (0, feature_width - experts)))
    side = jnp.concatenate([pieces, count_row], axis=0)
    side_rows = -(-(capacity + side.shape[0]) // 8) * 8 - capacity
    side = jnp.pad(side, ((0, side_rows - side.shape[0]), (0, 0)))
    send_grads = jnp.concatenate(
        [send_grads, jnp.broadcast_to(side[None], (experts, side_rows, feature_width))], axis=1
    )
    got_grads = exchange(send_grads)

    row_tokens = gather_groups(got_tokens)
    all_grads = gather_groups(got_grads).reshape(groups, capacity + side_rows, -1)
    row_grads = all_grads[:, :capacity].reshape(groups * capacity, -1)
    own_side = got_grads[capacity:].astype(jnp.float32)
    gate_dot = jnp.sum(
        own_side[: 3 * dot_rows].reshape(3, dot_rows, experts, feature_width), axis=(0, 2)
    ).reshape(token_count)
    counts = jnp.sum(all_grads[:, capacity + 3 * dot_rows, :experts].astype(jnp.float32), axis=0)

    gate_weight = in_weight[0, 0]
    up_weight = in_weight[0, 1]
    gate_pre = lax.dot_general(
        row_tokens, gate_weight, contract_last, preferred_element_type=jnp.float32
    )
    up_pre = lax.dot_general(
        row_tokens, up_weight, contract_last, preferred_element_type=jnp.float32
    )
    hidden_grad = lax.dot_general(
        row_grads, down_weight[0], contract_last, preferred_element_type=jnp.float32
    )
    gate_act, gate_back = gelu_parts(gate_pre, hidden_grad * up_pre)
    gate_grad = gate_back.astype(jnp.bfloat16)
    up_grad = (hidden_grad * gate_act).astype(jnp.bfloat16)
    term = jnp.dot(gate_grad, gate_weight, preferred_element_type=jnp.float32)
    term = term + jnp.dot(up_grad, up_weight, preferred_element_type=jnp.float32)
    summed = reduce_groups(term)
    going = summed.astype(jnp.bfloat16).reshape(capacity, experts, feature_width)
    returned = lax.all_to_all(
        going.transpose(1, 0, 2), "expert", split_axis=0, concat_axis=0, tiled=True
    )
    weight_grad = weight_grads(gate_grad, up_grad, row_tokens)

    prob_grad = chosen * gate_dot[:, None] + aux_coef * experts * counts[None, :] / (
        token_count * groups
    )
    logit_grad = router_probs * (
        prob_grad - jnp.sum(router_probs * prob_grad, axis=1, keepdims=True)
    )
    logit_grad = logit_grad.astype(jnp.bfloat16)
    router_grad = lax.dot_general(
        tokens, logit_grad, contract_first, preferred_element_type=jnp.float32
    )
    for distance in distances():
        router_grad = router_grad + swap(router_grad, distance)
    router_term = lax.dot_general(
        logit_grad, router_weight, contract_last, preferred_element_type=jnp.float32
    )
    combined = jnp.einsum(
        "tec,ecf->tf", mask_half, returned, preferred_element_type=jnp.float32
    )
    token_grad = (combined + router_term).astype(jnp.bfloat16)
    return (token_grad, weight_grad, router_grad)


def prelude_kernel(
    capacity,
    route_hbm,
    probs_hbm,
    tokens_hbm,
    grads_hbm,
    expert_out_hbm,
    send_ref,
    place_ref,
    route_ref,
    probs_ref,
    tokens_ref,
    grads_ref,
    expert_out_ref,
    sems,
):
    sources = (route_hbm, probs_hbm, tokens_hbm, grads_hbm, expert_out_hbm)
    targets = (route_ref, probs_ref, tokens_ref, grads_ref, expert_out_ref)
    copies = [
        pltpu.make_async_copy(source, target, sems.at[number])
        for number, (source, target) in enumerate(zip(sources, targets))
    ]
    for copy in copies:
        copy.start()
    experts, count = probs_ref.shape
    width = tokens_ref.shape[1]
    half, full = jnp.bfloat16, jnp.float32
    iota = lambda shape, axis: lax.broadcasted_iota(jnp.int32, shape, axis)
    dot = partial(lax.dot_general, preferred_element_type=full)
    plain = (((1,), (0,)), ((), ()))
    square = (count, count)
    earlier = (iota(square, 0) < iota(square, 1)).astype(full).astype(half)
    copies[0].wait()
    route = route_ref[...]
    hit = iota((experts, count), 0) == route
    before = dot(hit.astype(full).astype(half), earlier, plain)
    slot = jnp.sum(jnp.where(hit, before, 0.0), axis=0, keepdims=True)
    place = iota((experts * capacity, count), 0) == route * capacity + slot.astype(jnp.int32)
    mask = place.astype(full).astype(half)
    place_ref[...] = mask
    copies[1].wait()
    gate = jnp.sum(jnp.where(hit, probs_ref[...], 0.0), axis=0, keepdims=True)
    row_gate = jnp.sum(jnp.where(place, gate, 0.0), axis=1, keepdims=True)
    copies[2].wait()
    rows_x = dot(mask, tokens_ref[...], plain)
    copies[3].wait()
    rows_dy = dot(mask, grads_ref[...], plain) * row_gate
    copies[4].wait()
    product = grads_ref[...].astype(full) * expert_out_ref[...].astype(full)
    high = product.astype(half)
    low = (product - high.astype(full)).astype(half)
    ones = jnp.ones((8, width), half)
    part = dot(ones, high, contract_last) + dot(ones, low, contract_last)
    first = part.astype(half).astype(full)
    second = (part - first).astype(half).astype(full)
    third = part - first - second
    listed = (iota((width, count), 0) == route).astype(full).astype(half)
    counts = dot(jnp.ones((8, count), half), listed, contract_last)
    line = iota((8, width), 0)
    side = jnp.where(line == 3, counts, 0.0)
    for number, piece in enumerate((first, second, third)):
        side = jnp.where(line == number, piece, side)
    side = side.astype(half)
    for expert in range(experts):
        rows = slice(expert * capacity, (expert + 1) * capacity)
        send_ref[expert, :capacity] = rows_x[rows].astype(half)
        send_ref[expert, capacity : 2 * capacity] = rows_dy[rows].astype(half)
        send_ref[expert, 2 * capacity :] = side


def far(value):
    return pltpu.with_memory_space_constraint(value, pltpu.HBM)


def near(value):
    return pltpu.with_memory_space_constraint(value, pltpu.VMEM)


def prelude(capacity, *args):
    experts, count = args[1].shape
    width = args[2].shape[1]
    return pl.pallas_call(
        partial(prelude_kernel, capacity),
        in_specs=[pl.BlockSpec(memory_space=pl.ANY)] * len(args),
        out_shape=(
            jax.ShapeDtypeStruct((experts, 2 * capacity + 8, width), jnp.bfloat16),
            jax.ShapeDtypeStruct((experts * capacity, count), jnp.bfloat16),
        ),
        scratch_shapes=[pltpu.VMEM(value.shape, value.dtype) for value in args]
        + [pltpu.SemaphoreType.DMA((len(args),))],
        compiler_params=pltpu.CompilerParams(vmem_limit_bytes=8 << 20),
        name="prelude",
    )(*[far(value) for value in args])


def fetch_kernel(pieces, source_ref, after_ref, target_ref, sems):
    planes, hidden = source_ref.shape[1:3]
    size = hidden // pieces
    copies = []
    for plane in range(planes):
        for piece in range(pieces):
            where = (0, plane, pl.ds(piece * size, size))
            copies.append(
                pltpu.make_async_copy(
                    source_ref.at[where], target_ref.at[where], sems.at[len(copies)]
                )
            )
    for copy in copies:
        copy.start()
    for copy in copies:
        copy.wait()


def fetch(weight, after):
    pieces = 4
    return pl.pallas_call(
        partial(fetch_kernel, pieces),
        in_specs=[pl.BlockSpec(memory_space=pl.ANY)] * 2,
        out_specs=pl.BlockSpec(memory_space=pltpu.VMEM),
        out_shape=pltpu.VMEM(weight.shape, weight.dtype),
        scratch_shapes=[pltpu.SemaphoreType.DMA((weight.shape[1] * pieces,))],
        compiler_params=pltpu.CompilerParams(vmem_limit_bytes=1 << 20),
        cost_estimate=pl.CostEstimate(
            flops=0, bytes_accessed=2 * weight.size, transcendentals=0
        ),
        name="fetch",
    )(far(weight), after)


def hidden_pre_kernel(which, rows_ref, in_ref, down_hbm, out_ref, down_ref, sems):
    size = down_ref.shape[0]
    piece = size // sems.shape[0]
    copies = [
        pltpu.make_async_copy(
            down_hbm.at[0, pl.ds(which * size + number * piece, piece)],
            down_ref.at[pl.ds(number * piece, piece)],
            sems.at[number],
        )
        for number in range(sems.shape[0])
    ]
    for copy in copies:
        copy.start()
    rows = rows_ref[...]
    for start in range(0, 2 * size, size):
        part = slice(start, start + size)
        out_ref[part] = lax.dot_general(
            in_ref[0, which, part], rows, contract_last, preferred_element_type=jnp.float32
        )
    for copy in copies:
        copy.wait()


def hidden_pre(which, rows, in_near, down_weight):
    count, width = rows.shape
    hidden = in_near.shape[2]
    near_spec = pl.BlockSpec(memory_space=pltpu.VMEM)
    return pl.pallas_call(
        partial(hidden_pre_kernel, which),
        in_specs=[near_spec] * 2 + [pl.BlockSpec(memory_space=pl.ANY)],
        out_specs=[near_spec] * 2,
        out_shape=(
            pltpu.VMEM((hidden, count), jnp.float32),
            pltpu.VMEM((hidden // 2, width), down_weight.dtype),
        ),
        scratch_shapes=[pltpu.SemaphoreType.DMA((4,))],
        compiler_params=pltpu.CompilerParams(vmem_limit_bytes=8 << 20),
        cost_estimate=pl.CostEstimate(
            flops=2 * count * hidden * width, bytes_accessed=2 * hidden * width, transcendentals=0
        ),
        name="hidden_pre",
    )(rows, near(in_near), far(down_weight))


def block_of(size, wanted):
    return wanted if size % wanted == 0 else size


def hidden_back_kernel(
    block,
    rows_ref,
    gate_pre_ref,
    up_pre_ref,
    in_ref,
    down_ref,
    other_ref,
    gate_ref,
    up_ref,
    kept_ref,
    away_ref,
):
    size, width = down_ref.shape
    rows = rows_ref[...]
    half = rows.shape[0] // 2
    scale, cubic = math.sqrt(2 / math.pi), 0.044715
    for number, weight_ref in enumerate((down_ref, other_ref)):
        part = slice(number * size, (number + 1) * size)
        grad = lax.dot_general(
            weight_ref[...], rows, contract_last, preferred_element_type=jnp.float32
        )
        value, up = gate_pre_ref[part], up_pre_ref[part]
        square = value * value
        bend = jnp.tanh(scale * (value + cubic * (square * value)))
        cdf = 0.5 * (1.0 + bend)
        slope = cdf + (0.5 * scale) * value * (1.0 - bend * bend) * (1.0 + 3 * cubic * square)
        gate_ref[part] = (grad * up * slope).astype(jnp.bfloat16)
        up_ref[part] = (grad * (value * cdf)).astype(jnp.bfloat16)
    gate_grad, up_grad = gate_ref[...].T, up_ref[...].T
    for start in range(0, width, block):
        part = slice(start, start + block)
        total = jnp.dot(gate_grad, in_ref[0, 0, :, part], preferred_element_type=jnp.float32)
        total += jnp.dot(up_grad, in_ref[0, 1, :, part], preferred_element_type=jnp.float32)
        kept_ref[:, part] = total[:half]
        away_ref[:, part] = total[half:].astype(jnp.bfloat16)


def hidden_back(rows, gate_pre, up_pre, in_near, downs):
    count, width = rows.shape
    hidden = in_near.shape[2]
    near_spec = pl.BlockSpec(memory_space=pltpu.VMEM)
    return pl.pallas_call(
        partial(hidden_back_kernel, block_of(width, 1024)),
        in_specs=[near_spec] * 6,
        out_specs=[near_spec] * 4,
        out_shape=(
            pltpu.VMEM((hidden, count), jnp.bfloat16),
            pltpu.VMEM((hidden, count), jnp.bfloat16),
            pltpu.VMEM((count // 2, width), jnp.float32),
            pltpu.VMEM((count // 2, width), jnp.bfloat16),
        ),
        compiler_params=pltpu.CompilerParams(vmem_limit_bytes=12 << 20),
        cost_estimate=pl.CostEstimate(
            flops=6 * count * hidden * width,
            bytes_accessed=6 * hidden * width,
            transcendentals=count * hidden,
        ),
        name="hidden_back",
    )(rows, near(gate_pre), near(up_pre), near(in_near), *map(near, downs))


def half_kernel(grad_ref, rows_ref, *refs):
    refs[-1][0, 0] = jnp.dot(
        grad_ref[...], rows_ref[...], preferred_element_type=jnp.float32
    ).astype(jnp.bfloat16)


def half_weight_grad(which, grad, rows, partly=None):
    hidden, count = grad.shape
    width = rows.shape[1]
    block = block_of(hidden, 640)
    given = [] if partly is None else [partly]
    return pl.pallas_call(
        half_kernel,
        grid=(hidden // block,),
        in_specs=[
            pl.BlockSpec((block, count), lambda j: (j, 0)),
            pl.BlockSpec((count, width), lambda j: (0, 0)),
        ]
        + [pl.BlockSpec(memory_space=pl.ANY)] * len(given),
        out_specs=pl.BlockSpec((1, 1, block, width), lambda j: (0, which, j, 0)),
        out_shape=jax.ShapeDtypeStruct((1, 2, hidden, width), jnp.bfloat16),
        input_output_aliases={2: 0} if given else {},
        compiler_params=pltpu.CompilerParams(vmem_limit_bytes=20 << 20),
        cost_estimate=pl.CostEstimate(
            flops=2 * count * hidden * width, bytes_accessed=2 * hidden * width, transcendentals=0
        ),
        name="weight_grad_half",
    )(grad, rows, *given)


def aligned_device(
    tokens, out_grad, expert_out, router_probs, expert_index, in_weight, down_weight, router_weight
):
    token_count, width = tokens.shape
    experts = router_probs.shape[1]
    capacity = (5 * token_count + 4 * experts - 1) // (4 * experts)
    groups = lax.axis_size("dp")
    full_width = experts * width
    probs = router_probs.T
    route = expert_index.reshape(1, token_count)
    send, mask = prelude(capacity, route, probs, tokens, out_grad, expert_out)
    got = lax.all_to_all(send, "expert", split_axis=0, concat_axis=0, tiled=True)
    in_near = fetch(in_weight, got)

    def as_rows(value):
        return value.transpose(1, 0, 2).reshape(value.shape[1], full_width)

    row_tokens, all_grads = as_rows(got[:, :capacity]), as_rows(got[:, capacity:])
    first, last = distances()[:-1], distances()[-1:]
    row_tokens = gather_groups(row_tokens, first)
    all_grads = gather_groups(all_grads, first)
    row_tokens = gather_groups(row_tokens, last)
    all_grads = gather_groups(all_grads, last).reshape(groups, capacity + 8, full_width)
    gate_pre, first_down = hidden_pre(0, row_tokens, in_near, down_weight)
    up_pre, second_down = hidden_pre(1, row_tokens, in_near, down_weight)
    row_grads = all_grads[:, :capacity].reshape(groups * capacity, full_width)
    gate_dot = jnp.sum(got[:, 2 * capacity : 2 * capacity + 3].astype(jnp.float32), axis=(0, 1))
    counts = jnp.sum(all_grads[:, capacity + 3, :experts].astype(jnp.float32), axis=0)

    gate_grad, up_grad, kept, away = hidden_back(
        row_grads, gate_pre, up_pre, in_near, (first_down, second_down)
    )
    summed = kept + swap(away, 1).astype(jnp.float32)
    summed = reduce_groups(summed, 2)
    going = summed.astype(jnp.bfloat16).reshape(capacity, experts, width).transpose(1, 0, 2)
    returned = lax.all_to_all(going, "expert", split_axis=0, concat_axis=0, tiled=True)
    weight_grad = half_weight_grad(0, gate_grad, row_tokens)
    weight_grad = half_weight_grad(1, up_grad, row_tokens, weight_grad)

    chosen = (lax.broadcasted_iota(jnp.int32, (experts, token_count), 0) == route).astype(jnp.float32)
    prob_grad = chosen * gate_dot[None, :] + aux_coef * experts * counts[:, None] / (
        token_count * groups
    )
    logit_grad = probs * (prob_grad - jnp.sum(probs * prob_grad, axis=0, keepdims=True))
    logit_grad = logit_grad.astype(jnp.bfloat16)
    router_grad = jnp.dot(logit_grad, tokens, preferred_element_type=jnp.float32)
    for distance in distances():
        router_grad = router_grad + swap(router_grad, distance)
    router_term = lax.dot_general(
        logit_grad, router_weight, (((0,), (1,)), ((), ())), preferred_element_type=jnp.float32
    )
    combined = lax.dot_general(
        mask,
        returned.reshape(experts * capacity, width),
        contract_first,
        preferred_element_type=jnp.float32,
    )
    token_grad = (combined + router_term).astype(jnp.bfloat16)
    return (token_grad, weight_grad, router_grad.T)


def per_device(tokens, out_grad, expert_out, router_probs, *rest):
    token_count, width = tokens.shape
    experts = router_probs.shape[1]
    capacity = (5 * token_count + 4 * experts - 1) // (4 * experts)
    aligned = token_count == width and width % 128 == 0 and capacity % 8 == 0 and experts % 8 == 0
    if not aligned:
        return general_device(tokens, out_grad, expert_out, router_probs, *rest)
    return aligned_device(tokens, out_grad, expert_out, router_probs, *rest)


def solution(mesh):
    in_specs = (
        P("dp", "expert"),
        P("dp", "expert"),
        P("dp", "expert"),
        P("dp", None),
        P("dp", None),
        P("expert", None, "dp", None),
        P("expert", "dp", None),
        P("expert", None),
    )
    out_specs = (P("dp", "expert"), P("expert", None, "dp", None), P("expert", None))
    return jax.shard_map(
        per_device, mesh=mesh, in_specs=in_specs, out_specs=out_specs, check_vma=False
    )
```

```python
import math
from functools import partial

import jax
import jax.numpy as jnp
from jax import lax
from jax.experimental import pallas as pl
from jax.experimental.pallas import tpu as pltpu
from jax.sharding import PartitionSpec as P


aux_coef = 0.2
contract_last = (((1,), (1,)), ((), ()))
contract_first = (((0,), (0,)), ((), ()))


def slot_numbers(routes):
    width = routes.shape[1]
    same_expert = routes[:, :, None] == routes[:, None, :]
    position = jnp.arange(width, dtype=jnp.int32)
    before = position[None, :] < position[:, None]
    return jnp.sum((same_expert & before[None]).astype(jnp.int32), axis=2)


def one_hot(routes, slot_ids, experts, capacity):
    expert_hit = routes[..., None] == jnp.arange(experts, dtype=jnp.int32)
    slot_hit = slot_ids[..., None] == jnp.arange(capacity, dtype=jnp.int32)
    return (expert_hit[..., :, None] & slot_hit[..., None, :]).astype(jnp.float32)


def gelu_parts(pre_act, upstream):
    gelu_value, pullback = jax.vjp(partial(jax.nn.gelu, approximate=True), pre_act)
    return (gelu_value, pullback(upstream)[0])


def swap(value, distance):
    size = lax.axis_size("dp")
    return lax.ppermute(value, "dp", [(i, i ^ distance) for i in range(size)])


def distances():
    found, distance = [], lax.axis_size("dp") // 2
    while distance:
        found.append(distance)
        distance //= 2
    return found


def gather_groups(block, given=()):
    for distance in given or distances():
        block = jnp.concatenate([block, swap(block, distance)], axis=0)
    return block


def reduce_groups(total, first=1):
    order = [distance for distance in distances()[::-1] if distance >= first]
    for distance in order:
        half = total.shape[0] // 2
        away = swap(total[half:].astype(jnp.bfloat16), distance)
        total = total[:half] + away.astype(jnp.float32)
    return total


def weight_grad_kernel(gate_ref, up_ref, rows_ref, out_ref):
    rows = rows_ref[...]
    out_ref[0, 0] = lax.dot_general(
        gate_ref[...], rows, contract_first, preferred_element_type=jnp.float32
    ).astype(jnp.bfloat16)
    out_ref[0, 1] = lax.dot_general(
        up_ref[...], rows, contract_first, preferred_element_type=jnp.float32
    ).astype(jnp.bfloat16)


def weight_grads(gate_grad, up_grad, rows):
    count, hidden = gate_grad.shape
    width = rows.shape[1]
    block = 256 if hidden % 256 == 0 else hidden
    return pl.pallas_call(
        weight_grad_kernel,
        grid=(hidden // block,),
        in_specs=[
            pl.BlockSpec((count, block), lambda j: (0, j)),
            pl.BlockSpec((count, block), lambda j: (0, j)),
            pl.BlockSpec((count, width), lambda j: (0, 0)),
        ],
        out_specs=pl.BlockSpec((1, 2, block, width), lambda j: (0, 0, j, 0)),
        out_shape=jax.ShapeDtypeStruct((1, 2, hidden, width), jnp.bfloat16),
        cost_estimate=pl.CostEstimate(
            flops=4 * count * hidden * width,
            bytes_accessed=4 * hidden * width,
            transcendentals=0,
        ),
        name="weight_grads",
    )(gate_grad, up_grad, rows)


def split_float(value):
    high = lax.reduce_precision(value, 8, 7)
    middle = lax.reduce_precision(value - high, 8, 7)
    return jnp.stack([high, middle, value - high - middle]).astype(jnp.bfloat16)


def general_device(
    tokens, out_grad, expert_out, router_probs, expert_index, in_weight, down_weight, router_weight
):
    token_count, feature_width = tokens.shape
    experts = router_probs.shape[1]
    capacity = (5 * token_count + 4 * experts - 1) // (4 * experts)
    groups = lax.axis_size("dp")
    routes = expert_index[:, 0]
    slot_ids = slot_numbers(routes[None, :])[0]
    dispatch_mask = one_hot(routes, slot_ids, experts, capacity)
    mask_half = dispatch_mask.astype(jnp.bfloat16)
    chosen = jnp.sum(dispatch_mask, axis=2)

    def exchange(value):
        return lax.all_to_all(value, "expert", split_axis=0, concat_axis=2, tiled=True)[0]

    send_tokens = jnp.einsum(
        "tec,tf->ecf", mask_half, tokens, preferred_element_type=jnp.float32
    ).astype(jnp.bfloat16)
    got_tokens = exchange(send_tokens)

    gate = jnp.sum(router_probs * chosen, axis=1)
    gated_dy = (gate[:, None] * out_grad.astype(jnp.float32)).astype(jnp.bfloat16)
    send_grads = jnp.einsum(
        "tec,tf->ecf", mask_half, gated_dy, preferred_element_type=jnp.float32
    ).astype(jnp.bfloat16)
    partial_dot = jnp.sum(out_grad.astype(jnp.float32) * expert_out.astype(jnp.float32), axis=1)
    dot_rows = token_count // feature_width
    pieces = split_float(partial_dot).reshape(3 * dot_rows, feature_width)
    local_counts = jnp.sum(chosen, axis=0)
    count_row = jnp.pad(local_counts.astype(jnp.bfloat16)[None], ((0, 0), (0, feature_width - experts)))
    side = jnp.concatenate([pieces, count_row], axis=0)
    side_rows = -(-(capacity + side.shape[0]) // 8) * 8 - capacity
    side = jnp.pad(side, ((0, side_rows - side.shape[0]), (0, 0)))
    send_grads = jnp.concatenate(
        [send_grads, jnp.broadcast_to(side[None], (experts, side_rows, feature_width))], axis=1
    )
    got_grads = exchange(send_grads)

    row_tokens = gather_groups(got_tokens)
    all_grads = gather_groups(got_grads).reshape(groups, capacity + side_rows, -1)
    row_grads = all_grads[:, :capacity].reshape(groups * capacity, -1)
    own_side = got_grads[capacity:].astype(jnp.float32)
    gate_dot = jnp.sum(
        own_side[: 3 * dot_rows].reshape(3, dot_rows, experts, feature_width), axis=(0, 2)
    ).reshape(token_count)
    counts = jnp.sum(all_grads[:, capacity + 3 * dot_rows, :experts].astype(jnp.float32), axis=0)

    gate_weight = in_weight[0, 0]
    up_weight = in_weight[0, 1]
    gate_pre = lax.dot_general(
        row_tokens, gate_weight, contract_last, preferred_element_type=jnp.float32
    )
    up_pre = lax.dot_general(
        row_tokens, up_weight, contract_last, preferred_element_type=jnp.float32
    )
    hidden_grad = lax.dot_general(
        row_grads, down_weight[0], contract_last, preferred_element_type=jnp.float32
    )
    gate_act, gate_back = gelu_parts(gate_pre, hidden_grad * up_pre)
    gate_grad = gate_back.astype(jnp.bfloat16)
    up_grad = (hidden_grad * gate_act).astype(jnp.bfloat16)
    term = jnp.dot(gate_grad, gate_weight, preferred_element_type=jnp.float32)
    term = term + jnp.dot(up_grad, up_weight, preferred_element_type=jnp.float32)
    summed = reduce_groups(term)
    going = summed.astype(jnp.bfloat16).reshape(capacity, experts, feature_width)
    returned = lax.all_to_all(
        going.transpose(1, 0, 2), "expert", split_axis=0, concat_axis=0, tiled=True
    )
    weight_grad = weight_grads(gate_grad, up_grad, row_tokens)

    prob_grad = chosen * gate_dot[:, None] + aux_coef * experts * counts[None, :] / (
        token_count * groups
    )
    logit_grad = router_probs * (
        prob_grad - jnp.sum(router_probs * prob_grad, axis=1, keepdims=True)
    )
    logit_grad = logit_grad.astype(jnp.bfloat16)
    router_grad = lax.dot_general(
        tokens, logit_grad, contract_first, preferred_element_type=jnp.float32
    )
    for distance in distances():
        router_grad = router_grad + swap(router_grad, distance)
    router_term = lax.dot_general(
        logit_grad, router_weight, contract_last, preferred_element_type=jnp.float32
    )
    combined = jnp.einsum(
        "tec,ecf->tf", mask_half, returned, preferred_element_type=jnp.float32
    )
    token_grad = (combined + router_term).astype(jnp.bfloat16)
    return (token_grad, weight_grad, router_grad)


def prelude_kernel(
    capacity,
    route_hbm,
    probs_hbm,
    tokens_hbm,
    grads_hbm,
    expert_out_hbm,
    send_ref,
    place_ref,
    route_ref,
    probs_ref,
    tokens_ref,
    grads_ref,
    expert_out_ref,
    sems,
):
    sources = (route_hbm, probs_hbm, tokens_hbm, grads_hbm, expert_out_hbm)
    targets = (route_ref, probs_ref, tokens_ref, grads_ref, expert_out_ref)
    copies = [
        pltpu.make_async_copy(source, target, sems.at[number])
        for number, (source, target) in enumerate(zip(sources, targets))
    ]
    for copy in copies:
        copy.start()
    experts, count = probs_ref.shape
    width = tokens_ref.shape[1]
    half, full = jnp.bfloat16, jnp.float32
    iota = lambda shape, axis: lax.broadcasted_iota(jnp.int32, shape, axis)
    dot = partial(lax.dot_general, preferred_element_type=full)
    plain = (((1,), (0,)), ((), ()))
    square = (count, count)
    earlier = (iota(square, 0) < iota(square, 1)).astype(full).astype(half)
    copies[0].wait()
    route = route_ref[...]
    hit = iota((experts, count), 0) == route
    before = dot(hit.astype(full).astype(half), earlier, plain)
    slot = jnp.sum(jnp.where(hit, before, 0.0), axis=0, keepdims=True)
    place = iota((experts * capacity, count), 0) == route * capacity + slot.astype(jnp.int32)
    mask = place.astype(full).astype(half)
    place_ref[...] = mask
    copies[1].wait()
    gate = jnp.sum(jnp.where(hit, probs_ref[...], 0.0), axis=0, keepdims=True)
    row_gate = jnp.sum(jnp.where(place, gate, 0.0), axis=1, keepdims=True)
    copies[2].wait()
    rows_x = dot(mask, tokens_ref[...], plain)
    copies[3].wait()
    rows_dy = dot(mask, grads_ref[...], plain) * row_gate
    copies[4].wait()
    product = grads_ref[...].astype(full) * expert_out_ref[...].astype(full)
    high = product.astype(half)
    low = (product - high.astype(full)).astype(half)
    ones = jnp.ones((8, width), half)
    part = dot(ones, high, contract_last) + dot(ones, low, contract_last)
    first = part.astype(half).astype(full)
    second = (part - first).astype(half).astype(full)
    third = part - first - second
    listed = (iota((width, count), 0) == route).astype(full).astype(half)
    counts = dot(jnp.ones((8, count), half), listed, contract_last)
    line = iota((8, width), 0)
    side = jnp.where(line == 3, counts, 0.0)
    for number, piece in enumerate((first, second, third)):
        side = jnp.where(line == number, piece, side)
    side = side.astype(half)
    for expert in range(experts):
        rows = slice(expert * capacity, (expert + 1) * capacity)
        send_ref[expert, :capacity] = rows_x[rows].astype(half)
        send_ref[expert, capacity : 2 * capacity] = rows_dy[rows].astype(half)
        send_ref[expert, 2 * capacity :] = side


def far(value):
    return pltpu.with_memory_space_constraint(value, pltpu.HBM)


def near(value):
    return pltpu.with_memory_space_constraint(value, pltpu.VMEM)


def prelude(capacity, *args):
    experts, count = args[1].shape
    width = args[2].shape[1]
    return pl.pallas_call(
        partial(prelude_kernel, capacity),
        in_specs=[pl.BlockSpec(memory_space=pl.ANY)] * len(args),
        out_shape=(
            jax.ShapeDtypeStruct((experts, 2 * capacity + 8, width), jnp.bfloat16),
            jax.ShapeDtypeStruct((experts * capacity, count), jnp.bfloat16),
        ),
        scratch_shapes=[pltpu.VMEM(value.shape, value.dtype) for value in args]
        + [pltpu.SemaphoreType.DMA((len(args),))],
        compiler_params=pltpu.CompilerParams(vmem_limit_bytes=8 << 20),
        name="prelude",
    )(*[far(value) for value in args])


def fetch_kernel(pieces, source_ref, after_ref, target_ref, sems):
    planes, hidden = source_ref.shape[1:3]
    size = hidden // pieces
    copies = []
    for plane in range(planes):
        for piece in range(pieces):
            where = (0, plane, pl.ds(piece * size, size))
            copies.append(
                pltpu.make_async_copy(
                    source_ref.at[where], target_ref.at[where], sems.at[len(copies)]
                )
            )
    for copy in copies:
        copy.start()
    for copy in copies:
        copy.wait()


def fetch(weight, after):
    pieces = 4
    return pl.pallas_call(
        partial(fetch_kernel, pieces),
        in_specs=[pl.BlockSpec(memory_space=pl.ANY)] * 2,
        out_specs=pl.BlockSpec(memory_space=pltpu.VMEM),
        out_shape=pltpu.VMEM(weight.shape, weight.dtype),
        scratch_shapes=[pltpu.SemaphoreType.DMA((weight.shape[1] * pieces,))],
        compiler_params=pltpu.CompilerParams(vmem_limit_bytes=1 << 20),
        cost_estimate=pl.CostEstimate(
            flops=0, bytes_accessed=2 * weight.size, transcendentals=0
        ),
        name="fetch",
    )(far(weight), after)


def pre_activation(which, rows_ref, in_ref, out_ref):
    rows = rows_ref[...]
    size = in_ref.shape[2] // 2
    for start in (0, size):
        part = slice(start, start + size)
        out_ref[part] = lax.dot_general(
            in_ref[0, which, part], rows, contract_last, preferred_element_type=jnp.float32
        )


def gate_pre_kernel(rows_ref, in_ref, down_hbm, out_ref, down_ref, sems):
    pieces = sems.shape[0]
    size = down_ref.shape[1] // pieces
    copies = []
    for piece in range(pieces):
        where = (0, pl.ds(piece * size, size))
        copies.append(
            pltpu.make_async_copy(down_hbm.at[where], down_ref.at[where], sems.at[piece])
        )
    for copy in copies:
        copy.start()
    pre_activation(0, rows_ref, in_ref, out_ref)
    for copy in copies:
        copy.wait()


def hidden_pre(which, rows, in_near, down_weight=None):
    count, width = rows.shape
    hidden = in_near.shape[2]
    near_spec = pl.BlockSpec(memory_space=pltpu.VMEM)
    out = pltpu.VMEM((hidden, count), jnp.float32)
    settings = dict(
        compiler_params=pltpu.CompilerParams(vmem_limit_bytes=8 << 20),
        cost_estimate=pl.CostEstimate(
            flops=2 * count * hidden * width, bytes_accessed=2 * hidden * width, transcendentals=0
        ),
    )
    if down_weight is None:
        return pl.pallas_call(
            partial(pre_activation, which),
            in_specs=[near_spec] * 2,
            out_specs=near_spec,
            out_shape=out,
            name="hidden_pre",
            **settings,
        )(rows, near(in_near))
    return pl.pallas_call(
        gate_pre_kernel,
        in_specs=[near_spec] * 2 + [pl.BlockSpec(memory_space=pl.ANY)],
        out_specs=[near_spec] * 2,
        out_shape=(out, pltpu.VMEM(down_weight.shape, down_weight.dtype)),
        scratch_shapes=[pltpu.SemaphoreType.DMA((4,))],
        name="gate_pre",
        **settings,
    )(rows, near(in_near), far(down_weight))


def block_of(size, wanted):
    return wanted if size % wanted == 0 else size


def hidden_back_kernel(
    block,
    rows_ref,
    gate_pre_ref,
    up_pre_ref,
    in_ref,
    down_ref,
    gate_ref,
    up_ref,
    kept_ref,
    away_ref,
):
    size, width = down_ref.shape[1] // 2, down_ref.shape[2]
    rows = rows_ref[...]
    half = rows.shape[0] // 2
    scale, cubic = math.sqrt(2 / math.pi), 0.044715
    for start in (0, size):
        part = slice(start, start + size)
        grad = lax.dot_general(
            down_ref[0, part], rows, contract_last, preferred_element_type=jnp.float32
        )
        value, up = gate_pre_ref[part], up_pre_ref[part]
        square = value * value
        bend = jnp.tanh(scale * (value + cubic * (square * value)))
        cdf = 0.5 * (1.0 + bend)
        slope = cdf + (0.5 * scale) * value * (1.0 - bend * bend) * (1.0 + 3 * cubic * square)
        gate_ref[part] = (grad * up * slope).astype(jnp.bfloat16)
        up_ref[part] = (grad * (value * cdf)).astype(jnp.bfloat16)
    gate_grad, up_grad = gate_ref[...].T, up_ref[...].T
    for start in range(0, width, block):
        part = slice(start, start + block)
        total = jnp.dot(gate_grad, in_ref[0, 0, :, part], preferred_element_type=jnp.float32)
        total += jnp.dot(up_grad, in_ref[0, 1, :, part], preferred_element_type=jnp.float32)
        kept_ref[:, part] = total[:half]
        away_ref[:, part] = total[half:].astype(jnp.bfloat16)


def hidden_back(rows, gate_pre, up_pre, in_near, down_near):
    count, width = rows.shape
    hidden = in_near.shape[2]
    near_spec = pl.BlockSpec(memory_space=pltpu.VMEM)
    return pl.pallas_call(
        partial(hidden_back_kernel, block_of(width, 1024)),
        in_specs=[near_spec] * 5,
        out_specs=[near_spec] * 4,
        out_shape=(
            pltpu.VMEM((hidden, count), jnp.bfloat16),
            pltpu.VMEM((hidden, count), jnp.bfloat16),
            pltpu.VMEM((count // 2, width), jnp.float32),
            pltpu.VMEM((count // 2, width), jnp.bfloat16),
        ),
        compiler_params=pltpu.CompilerParams(vmem_limit_bytes=12 << 20),
        cost_estimate=pl.CostEstimate(
            flops=6 * count * hidden * width,
            bytes_accessed=6 * hidden * width,
            transcendentals=count * hidden,
        ),
        name="hidden_back",
    )(rows, near(gate_pre), near(up_pre), near(in_near), near(down_near))


def half_kernel(grad_ref, rows_ref, *refs):
    refs[-1][0, 0] = jnp.dot(
        grad_ref[...], rows_ref[...], preferred_element_type=jnp.float32
    ).astype(jnp.bfloat16)


def half_weight_grad(which, grad, rows, partly=None):
    hidden, count = grad.shape
    width = rows.shape[1]
    block = block_of(hidden, 640)
    given = [] if partly is None else [partly]
    return pl.pallas_call(
        half_kernel,
        grid=(hidden // block,),
        in_specs=[
            pl.BlockSpec((block, count), lambda j: (j, 0)),
            pl.BlockSpec((count, width), lambda j: (0, 0)),
        ]
        + [pl.BlockSpec(memory_space=pl.ANY)] * len(given),
        out_specs=pl.BlockSpec((1, 1, block, width), lambda j: (0, which, j, 0)),
        out_shape=jax.ShapeDtypeStruct((1, 2, hidden, width), jnp.bfloat16),
        input_output_aliases={2: 0} if given else {},
        compiler_params=pltpu.CompilerParams(vmem_limit_bytes=20 << 20),
        cost_estimate=pl.CostEstimate(
            flops=2 * count * hidden * width, bytes_accessed=2 * hidden * width, transcendentals=0
        ),
        name="weight_grad_half",
    )(grad, rows, *given)


def aligned_device(
    tokens, out_grad, expert_out, router_probs, expert_index, in_weight, down_weight, router_weight
):
    token_count, width = tokens.shape
    experts = router_probs.shape[1]
    capacity = (5 * token_count + 4 * experts - 1) // (4 * experts)
    groups = lax.axis_size("dp")
    full_width = experts * width
    probs = router_probs.T
    route = expert_index.reshape(1, token_count)
    send, mask = prelude(capacity, route, probs, tokens, out_grad, expert_out)
    got = lax.all_to_all(send, "expert", split_axis=0, concat_axis=0, tiled=True)
    in_near = fetch(in_weight, got)

    def as_rows(value):
        return value.transpose(1, 0, 2).reshape(value.shape[1], full_width)

    row_tokens, all_grads = as_rows(got[:, :capacity]), as_rows(got[:, capacity:])
    first, last = distances()[:-1], distances()[-1:]
    row_tokens = gather_groups(row_tokens, first)
    all_grads = gather_groups(all_grads, first)
    row_tokens = gather_groups(row_tokens, last)
    all_grads = gather_groups(all_grads, last).reshape(groups, capacity + 8, full_width)
    gate_pre, down_near = hidden_pre(0, row_tokens, in_near, down_weight)
    up_pre = hidden_pre(1, row_tokens, in_near)
    row_grads = all_grads[:, :capacity].reshape(groups * capacity, full_width)
    gate_dot = jnp.sum(got[:, 2 * capacity : 2 * capacity + 3].astype(jnp.float32), axis=(0, 1))
    counts = jnp.sum(all_grads[:, capacity + 3, :experts].astype(jnp.float32), axis=0)

    gate_grad, up_grad, kept, away = hidden_back(
        row_grads, gate_pre, up_pre, in_near, down_near
    )
    summed = kept + swap(away, 1).astype(jnp.float32)
    summed = reduce_groups(summed, 2)
    going = summed.astype(jnp.bfloat16).reshape(capacity, experts, width).transpose(1, 0, 2)
    returned = lax.all_to_all(going, "expert", split_axis=0, concat_axis=0, tiled=True)
    weight_grad = half_weight_grad(0, gate_grad, row_tokens)
    weight_grad = half_weight_grad(1, up_grad, row_tokens, weight_grad)

    chosen = (lax.broadcasted_iota(jnp.int32, (experts, token_count), 0) == route).astype(jnp.float32)
    prob_grad = chosen * gate_dot[None, :] + aux_coef * experts * counts[:, None] / (
        token_count * groups
    )
    logit_grad = probs * (prob_grad - jnp.sum(probs * prob_grad, axis=0, keepdims=True))
    logit_grad = logit_grad.astype(jnp.bfloat16)
    router_grad = jnp.dot(logit_grad, tokens, preferred_element_type=jnp.float32)
    for distance in distances()[::-1]:
        router_grad = router_grad + swap(router_grad, distance)
    router_term = lax.dot_general(
        logit_grad, router_weight, (((0,), (1,)), ((), ())), preferred_element_type=jnp.float32
    )
    combined = lax.dot_general(
        mask,
        returned.reshape(experts * capacity, width),
        contract_first,
        preferred_element_type=jnp.float32,
    )
    token_grad = (combined + router_term).astype(jnp.bfloat16)
    return (token_grad, weight_grad, router_grad.T)


def per_device(tokens, out_grad, expert_out, router_probs, *rest):
    token_count, width = tokens.shape
    experts = router_probs.shape[1]
    capacity = (5 * token_count + 4 * experts - 1) // (4 * experts)
    aligned = token_count == width and width % 128 == 0 and capacity % 8 == 0 and experts % 8 == 0
    if not aligned:
        return general_device(tokens, out_grad, expert_out, router_probs, *rest)
    return aligned_device(tokens, out_grad, expert_out, router_probs, *rest)


def solution(mesh):
    in_specs = (
        P("dp", "expert"),
        P("dp", "expert"),
        P("dp", "expert"),
        P("dp", None),
        P("dp", None),
        P("expert", None, "dp", None),
        P("expert", "dp", None),
        P("expert", None),
    )
    out_specs = (P("dp", "expert"), P("expert", None, "dp", None), P("expert", None))
    return jax.shard_map(
        per_device, mesh=mesh, in_specs=in_specs, out_specs=out_specs, check_vma=False
    )
```

```python
import math
from functools import partial

import jax
import jax.numpy as jnp
from jax import lax
from jax.experimental import pallas as pl
from jax.experimental.pallas import tpu as pltpu
from jax.sharding import PartitionSpec as P


aux_coef = 0.2
contract_last = (((1,), (1,)), ((), ()))
contract_first = (((0,), (0,)), ((), ()))


def slot_numbers(routes):
    width = routes.shape[1]
    same_expert = routes[:, :, None] == routes[:, None, :]
    position = jnp.arange(width, dtype=jnp.int32)
    before = position[None, :] < position[:, None]
    return jnp.sum((same_expert & before[None]).astype(jnp.int32), axis=2)


def one_hot(routes, slot_ids, experts, capacity):
    expert_hit = routes[..., None] == jnp.arange(experts, dtype=jnp.int32)
    slot_hit = slot_ids[..., None] == jnp.arange(capacity, dtype=jnp.int32)
    return (expert_hit[..., :, None] & slot_hit[..., None, :]).astype(jnp.float32)


def gelu_parts(pre_act, upstream):
    gelu_value, pullback = jax.vjp(partial(jax.nn.gelu, approximate=True), pre_act)
    return (gelu_value, pullback(upstream)[0])


def swap(value, distance):
    size = lax.axis_size("dp")
    return lax.ppermute(value, "dp", [(i, i ^ distance) for i in range(size)])


def distances():
    found, distance = [], lax.axis_size("dp") // 2
    while distance:
        found.append(distance)
        distance //= 2
    return found


def gather_groups(block, given=()):
    for distance in given or distances():
        block = jnp.concatenate([block, swap(block, distance)], axis=0)
    return block


def reduce_groups(total, first=1):
    order = [distance for distance in distances()[::-1] if distance >= first]
    for distance in order:
        half = total.shape[0] // 2
        away = swap(total[half:].astype(jnp.bfloat16), distance)
        total = total[:half] + away.astype(jnp.float32)
    return total


def weight_grad_kernel(gate_ref, up_ref, rows_ref, out_ref):
    rows = rows_ref[...]
    out_ref[0, 0] = lax.dot_general(
        gate_ref[...], rows, contract_first, preferred_element_type=jnp.float32
    ).astype(jnp.bfloat16)
    out_ref[0, 1] = lax.dot_general(
        up_ref[...], rows, contract_first, preferred_element_type=jnp.float32
    ).astype(jnp.bfloat16)


def weight_grads(gate_grad, up_grad, rows):
    count, hidden = gate_grad.shape
    width = rows.shape[1]
    block = 256 if hidden % 256 == 0 else hidden
    return pl.pallas_call(
        weight_grad_kernel,
        grid=(hidden // block,),
        in_specs=[
            pl.BlockSpec((count, block), lambda j: (0, j)),
            pl.BlockSpec((count, block), lambda j: (0, j)),
            pl.BlockSpec((count, width), lambda j: (0, 0)),
        ],
        out_specs=pl.BlockSpec((1, 2, block, width), lambda j: (0, 0, j, 0)),
        out_shape=jax.ShapeDtypeStruct((1, 2, hidden, width), jnp.bfloat16),
        cost_estimate=pl.CostEstimate(
            flops=4 * count * hidden * width,
            bytes_accessed=4 * hidden * width,
            transcendentals=0,
        ),
        name="weight_grads",
    )(gate_grad, up_grad, rows)


def split_float(value):
    high = lax.reduce_precision(value, 8, 7)
    middle = lax.reduce_precision(value - high, 8, 7)
    return jnp.stack([high, middle, value - high - middle]).astype(jnp.bfloat16)


def general_device(
    tokens, out_grad, expert_out, router_probs, expert_index, in_weight, down_weight, router_weight
):
    token_count, feature_width = tokens.shape
    experts = router_probs.shape[1]
    capacity = (5 * token_count + 4 * experts - 1) // (4 * experts)
    groups = lax.axis_size("dp")
    routes = expert_index[:, 0]
    slot_ids = slot_numbers(routes[None, :])[0]
    dispatch_mask = one_hot(routes, slot_ids, experts, capacity)
    mask_half = dispatch_mask.astype(jnp.bfloat16)
    chosen = jnp.sum(dispatch_mask, axis=2)

    def exchange(value):
        return lax.all_to_all(value, "expert", split_axis=0, concat_axis=2, tiled=True)[0]

    send_tokens = jnp.einsum(
        "tec,tf->ecf", mask_half, tokens, preferred_element_type=jnp.float32
    ).astype(jnp.bfloat16)
    got_tokens = exchange(send_tokens)

    gate = jnp.sum(router_probs * chosen, axis=1)
    gated_dy = (gate[:, None] * out_grad.astype(jnp.float32)).astype(jnp.bfloat16)
    send_grads = jnp.einsum(
        "tec,tf->ecf", mask_half, gated_dy, preferred_element_type=jnp.float32
    ).astype(jnp.bfloat16)
    partial_dot = jnp.sum(out_grad.astype(jnp.float32) * expert_out.astype(jnp.float32), axis=1)
    dot_rows = token_count // feature_width
    pieces = split_float(partial_dot).reshape(3 * dot_rows, feature_width)
    local_counts = jnp.sum(chosen, axis=0)
    count_row = jnp.pad(local_counts.astype(jnp.bfloat16)[None], ((0, 0), (0, feature_width - experts)))
    side = jnp.concatenate([pieces, count_row], axis=0)
    side_rows = -(-(capacity + side.shape[0]) // 8) * 8 - capacity
    side = jnp.pad(side, ((0, side_rows - side.shape[0]), (0, 0)))
    send_grads = jnp.concatenate(
        [send_grads, jnp.broadcast_to(side[None], (experts, side_rows, feature_width))], axis=1
    )
    got_grads = exchange(send_grads)

    row_tokens = gather_groups(got_tokens)
    all_grads = gather_groups(got_grads).reshape(groups, capacity + side_rows, -1)
    row_grads = all_grads[:, :capacity].reshape(groups * capacity, -1)
    own_side = got_grads[capacity:].astype(jnp.float32)
    gate_dot = jnp.sum(
        own_side[: 3 * dot_rows].reshape(3, dot_rows, experts, feature_width), axis=(0, 2)
    ).reshape(token_count)
    counts = jnp.sum(all_grads[:, capacity + 3 * dot_rows, :experts].astype(jnp.float32), axis=0)

    gate_weight = in_weight[0, 0]
    up_weight = in_weight[0, 1]
    gate_pre = lax.dot_general(
        row_tokens, gate_weight, contract_last, preferred_element_type=jnp.float32
    )
    up_pre = lax.dot_general(
        row_tokens, up_weight, contract_last, preferred_element_type=jnp.float32
    )
    hidden_grad = lax.dot_general(
        row_grads, down_weight[0], contract_last, preferred_element_type=jnp.float32
    )
    gate_act, gate_back = gelu_parts(gate_pre, hidden_grad * up_pre)
    gate_grad = gate_back.astype(jnp.bfloat16)
    up_grad = (hidden_grad * gate_act).astype(jnp.bfloat16)
    term = jnp.dot(gate_grad, gate_weight, preferred_element_type=jnp.float32)
    term = term + jnp.dot(up_grad, up_weight, preferred_element_type=jnp.float32)
    summed = reduce_groups(term)
    going = summed.astype(jnp.bfloat16).reshape(capacity, experts, feature_width)
    returned = lax.all_to_all(
        going.transpose(1, 0, 2), "expert", split_axis=0, concat_axis=0, tiled=True
    )
    weight_grad = weight_grads(gate_grad, up_grad, row_tokens)

    prob_grad = chosen * gate_dot[:, None] + aux_coef * experts * counts[None, :] / (
        token_count * groups
    )
    logit_grad = router_probs * (
        prob_grad - jnp.sum(router_probs * prob_grad, axis=1, keepdims=True)
    )
    logit_grad = logit_grad.astype(jnp.bfloat16)
    router_grad = lax.dot_general(
        tokens, logit_grad, contract_first, preferred_element_type=jnp.float32
    )
    for distance in distances():
        router_grad = router_grad + swap(router_grad, distance)
    router_term = lax.dot_general(
        logit_grad, router_weight, contract_last, preferred_element_type=jnp.float32
    )
    combined = jnp.einsum(
        "tec,ecf->tf", mask_half, returned, preferred_element_type=jnp.float32
    )
    token_grad = (combined + router_term).astype(jnp.bfloat16)
    return (token_grad, weight_grad, router_grad)


def prelude_kernel(
    capacity,
    route_hbm,
    probs_hbm,
    tokens_hbm,
    grads_hbm,
    expert_out_hbm,
    send_ref,
    place_ref,
    route_ref,
    probs_ref,
    tokens_ref,
    grads_ref,
    expert_out_ref,
    sems,
):
    sources = (route_hbm, probs_hbm, tokens_hbm, grads_hbm, expert_out_hbm)
    targets = (route_ref, probs_ref, tokens_ref, grads_ref, expert_out_ref)
    copies = [
        pltpu.make_async_copy(source, target, sems.at[number])
        for number, (source, target) in enumerate(zip(sources, targets))
    ]
    for copy in copies:
        copy.start()
    experts, count = probs_ref.shape
    width = tokens_ref.shape[1]
    half, full = jnp.bfloat16, jnp.float32
    iota = lambda shape, axis: lax.broadcasted_iota(jnp.int32, shape, axis)
    dot = partial(lax.dot_general, preferred_element_type=full)
    plain = (((1,), (0,)), ((), ()))
    square = (count, count)
    earlier = (iota(square, 0) < iota(square, 1)).astype(full).astype(half)
    copies[0].wait()
    route = route_ref[...]
    hit = iota((experts, count), 0) == route
    before = dot(hit.astype(full).astype(half), earlier, plain)
    slot = jnp.sum(jnp.where(hit, before, 0.0), axis=0, keepdims=True)
    place = iota((experts * capacity, count), 0) == route * capacity + slot.astype(jnp.int32)
    mask = place.astype(full).astype(half)
    place_ref[...] = mask
    copies[1].wait()
    gate = jnp.sum(jnp.where(hit, probs_ref[...], 0.0), axis=0, keepdims=True)
    row_gate = jnp.sum(jnp.where(place, gate, 0.0), axis=1, keepdims=True)
    copies[2].wait()
    rows_x = dot(mask, tokens_ref[...], plain)
    copies[3].wait()
    rows_dy = dot(mask, grads_ref[...], plain) * row_gate
    copies[4].wait()
    product = grads_ref[...].astype(full) * expert_out_ref[...].astype(full)
    high = product.astype(half)
    low = (product - high.astype(full)).astype(half)
    ones = jnp.ones((8, width), half)
    part = dot(ones, high, contract_last) + dot(ones, low, contract_last)
    first = part.astype(half).astype(full)
    second = (part - first).astype(half).astype(full)
    third = part - first - second
    listed = (iota((width, count), 0) == route).astype(full).astype(half)
    counts = dot(jnp.ones((8, count), half), listed, contract_last)
    line = iota((8, width), 0)
    side = jnp.where(line == 3, counts, 0.0)
    for number, piece in enumerate((first, second, third)):
        side = jnp.where(line == number, piece, side)
    side = side.astype(half)
    for expert in range(experts):
        rows = slice(expert * capacity, (expert + 1) * capacity)
        send_ref[expert, :capacity] = rows_x[rows].astype(half)
        send_ref[expert, capacity : 2 * capacity] = rows_dy[rows].astype(half)
        send_ref[expert, 2 * capacity :] = side


def far(value):
    return pltpu.with_memory_space_constraint(value, pltpu.HBM)


def near(value):
    return pltpu.with_memory_space_constraint(value, pltpu.VMEM)


def prelude(capacity, *args):
    experts, count = args[1].shape
    width = args[2].shape[1]
    return pl.pallas_call(
        partial(prelude_kernel, capacity),
        in_specs=[pl.BlockSpec(memory_space=pl.ANY)] * len(args),
        out_shape=(
            jax.ShapeDtypeStruct((experts, 2 * capacity + 8, width), jnp.bfloat16),
            jax.ShapeDtypeStruct((experts * capacity, count), jnp.bfloat16),
        ),
        scratch_shapes=[pltpu.VMEM(value.shape, value.dtype) for value in args]
        + [pltpu.SemaphoreType.DMA((len(args),))],
        compiler_params=pltpu.CompilerParams(vmem_limit_bytes=8 << 20),
        name="prelude",
    )(*[far(value) for value in args])


def fetch_kernel(pieces, source_ref, after_ref, target_ref, sems):
    planes, hidden = source_ref.shape[1:3]
    size = hidden // pieces
    copies = []
    for plane in range(planes):
        for piece in range(pieces):
            where = (0, plane, pl.ds(piece * size, size))
            copies.append(
                pltpu.make_async_copy(
                    source_ref.at[where], target_ref.at[where], sems.at[len(copies)]
                )
            )
    for copy in copies:
        copy.start()
    for copy in copies:
        copy.wait()


def fetch(weight, after):
    pieces = 4
    return pl.pallas_call(
        partial(fetch_kernel, pieces),
        in_specs=[pl.BlockSpec(memory_space=pl.ANY)] * 2,
        out_specs=pl.BlockSpec(memory_space=pltpu.VMEM),
        out_shape=pltpu.VMEM(weight.shape, weight.dtype),
        scratch_shapes=[pltpu.SemaphoreType.DMA((weight.shape[1] * pieces,))],
        compiler_params=pltpu.CompilerParams(vmem_limit_bytes=1 << 20),
        cost_estimate=pl.CostEstimate(
            flops=0, bytes_accessed=2 * weight.size, transcendentals=0
        ),
        name="fetch",
    )(far(weight), after)


def pre_activation(which, rows_ref, in_ref, out_ref):
    rows = rows_ref[...]
    size = in_ref.shape[2] // 2
    for start in (0, size):
        part = slice(start, start + size)
        out_ref[part] = lax.dot_general(
            in_ref[0, which, part], rows, contract_last, preferred_element_type=jnp.float32
        )


def gate_pre_kernel(rows_ref, in_ref, down_hbm, out_ref, down_ref, sems):
    pieces = sems.shape[0]
    size = down_ref.shape[1] // pieces
    copies = []
    for piece in range(pieces):
        where = (0, pl.ds(piece * size, size))
        copies.append(
            pltpu.make_async_copy(down_hbm.at[where], down_ref.at[where], sems.at[piece])
        )
    for copy in copies:
        copy.start()
    pre_activation(0, rows_ref, in_ref, out_ref)
    for copy in copies:
        copy.wait()


def hidden_pre(which, rows, in_near, down_weight=None):
    count, width = rows.shape
    hidden = in_near.shape[2]
    near_spec = pl.BlockSpec(memory_space=pltpu.VMEM)
    out = pltpu.VMEM((hidden, count), jnp.float32)
    settings = dict(
        compiler_params=pltpu.CompilerParams(vmem_limit_bytes=8 << 20),
        cost_estimate=pl.CostEstimate(
            flops=2 * count * hidden * width, bytes_accessed=2 * hidden * width, transcendentals=0
        ),
    )
    if down_weight is None:
        return pl.pallas_call(
            partial(pre_activation, which),
            in_specs=[near_spec] * 2,
            out_specs=near_spec,
            out_shape=out,
            name="hidden_pre",
            **settings,
        )(rows, near(in_near))
    return pl.pallas_call(
        gate_pre_kernel,
        in_specs=[near_spec] * 2 + [pl.BlockSpec(memory_space=pl.ANY)],
        out_specs=[near_spec] * 2,
        out_shape=(out, pltpu.VMEM(down_weight.shape, down_weight.dtype)),
        scratch_shapes=[pltpu.SemaphoreType.DMA((4,))],
        name="gate_pre",
        **settings,
    )(rows, near(in_near), far(down_weight))


def block_of(size, wanted):
    return wanted if size % wanted == 0 else size


def input_grads(rows, in_ref, first, kept_ref, away_ref, block):
    half = kept_ref.shape[0]
    for start in range(0, kept_ref.shape[1], block):
        part, columns = slice(start, start + block), slice(first + start, first + start + block)
        total = jnp.dot(rows[0], in_ref[0, 0, :, columns], preferred_element_type=jnp.float32)
        total += jnp.dot(rows[1], in_ref[0, 1, :, columns], preferred_element_type=jnp.float32)
        kept_ref[:, part] = total[:half]
        away_ref[:, part] = total[half:].astype(jnp.bfloat16)


def hidden_back_kernel(
    block,
    rows_ref,
    gate_pre_ref,
    up_pre_ref,
    in_ref,
    down_ref,
    gate_ref,
    up_ref,
    gate_rows_ref,
    up_rows_ref,
    kept_ref,
    away_ref,
):
    size = down_ref.shape[1] // 2
    rows = rows_ref[...]
    scale, cubic = math.sqrt(2 / math.pi), 0.044715
    for start in (0, size):
        part = slice(start, start + size)
        grad = lax.dot_general(
            down_ref[0, part], rows, contract_last, preferred_element_type=jnp.float32
        )
        value, up = gate_pre_ref[part], up_pre_ref[part]
        square = value * value
        bend = jnp.tanh(scale * (value + cubic * (square * value)))
        cdf = 0.5 * (1.0 + bend)
        slope = cdf + (0.5 * scale) * value * (1.0 - bend * bend) * (1.0 + 3 * cubic * square)
        gate_ref[part] = (grad * up * slope).astype(jnp.bfloat16)
        up_ref[part] = (grad * (value * cdf)).astype(jnp.bfloat16)
    gate_rows_ref[...] = gate_ref[...].T
    up_rows_ref[...] = up_ref[...].T
    input_grads((gate_rows_ref[...], up_rows_ref[...]), in_ref, 0, kept_ref, away_ref, block)


def rest_back_kernel(block, gate_rows_ref, up_rows_ref, in_ref, kept_ref, away_ref):
    first = in_ref.shape[3] - kept_ref.shape[1]
    input_grads((gate_rows_ref[...], up_rows_ref[...]), in_ref, first, kept_ref, away_ref, block)


def hidden_back(rows, gate_pre, up_pre, in_near, down_near):
    count, width = rows.shape
    hidden = down_near.shape[1]
    near_spec = pl.BlockSpec(memory_space=pltpu.VMEM)
    return pl.pallas_call(
        partial(hidden_back_kernel, width // 2),
        in_specs=[near_spec] * 5,
        out_specs=[near_spec] * 6,
        out_shape=(
            pltpu.VMEM((hidden, count), jnp.bfloat16),
            pltpu.VMEM((hidden, count), jnp.bfloat16),
            pltpu.VMEM((count, hidden), jnp.bfloat16),
            pltpu.VMEM((count, hidden), jnp.bfloat16),
            pltpu.VMEM((count // 2, width // 2), jnp.float32),
            pltpu.VMEM((count // 2, width // 2), jnp.bfloat16),
        ),
        compiler_params=pltpu.CompilerParams(vmem_limit_bytes=12 << 20),
        cost_estimate=pl.CostEstimate(
            flops=4 * count * hidden * width,
            bytes_accessed=4 * hidden * width,
            transcendentals=count * hidden,
        ),
        name="hidden_back",
    )(rows, near(gate_pre), near(up_pre), near(in_near), near(down_near))


def rest_back(gate_rows, up_rows, in_near):
    count, hidden = gate_rows.shape
    width = in_near.shape[3]
    near_spec = pl.BlockSpec(memory_space=pltpu.VMEM)
    return pl.pallas_call(
        partial(rest_back_kernel, width // 2),
        in_specs=[near_spec] * 3,
        out_specs=[near_spec] * 2,
        out_shape=(
            pltpu.VMEM((count // 2, width // 2), jnp.float32),
            pltpu.VMEM((count // 2, width // 2), jnp.bfloat16),
        ),
        compiler_params=pltpu.CompilerParams(vmem_limit_bytes=12 << 20),
        cost_estimate=pl.CostEstimate(
            flops=2 * count * hidden * width, bytes_accessed=2 * hidden * width, transcendentals=0
        ),
        name="rest_back",
    )(near(gate_rows), near(up_rows), near(in_near))


def half_kernel(grad_ref, rows_ref, *refs):
    refs[-1][0, 0] = jnp.dot(
        grad_ref[...], rows_ref[...], preferred_element_type=jnp.float32
    ).astype(jnp.bfloat16)


def half_weight_grad(which, grad, rows, partly=None):
    hidden, count = grad.shape
    width = rows.shape[1]
    block = block_of(hidden, 640)
    given = [] if partly is None else [partly]
    return pl.pallas_call(
        half_kernel,
        grid=(hidden // block,),
        in_specs=[
            pl.BlockSpec((block, count), lambda j: (j, 0)),
            pl.BlockSpec((count, width), lambda j: (0, 0)),
        ]
        + [pl.BlockSpec(memory_space=pl.ANY)] * len(given),
        out_specs=pl.BlockSpec((1, 1, block, width), lambda j: (0, which, j, 0)),
        out_shape=jax.ShapeDtypeStruct((1, 2, hidden, width), jnp.bfloat16),
        input_output_aliases={2: 0} if given else {},
        compiler_params=pltpu.CompilerParams(vmem_limit_bytes=20 << 20),
        cost_estimate=pl.CostEstimate(
            flops=2 * count * hidden * width, bytes_accessed=2 * hidden * width, transcendentals=0
        ),
        name="weight_grad_half",
    )(grad, rows, *given)


def aligned_device(
    tokens, out_grad, expert_out, router_probs, expert_index, in_weight, down_weight, router_weight
):
    token_count, width = tokens.shape
    experts = router_probs.shape[1]
    capacity = (5 * token_count + 4 * experts - 1) // (4 * experts)
    groups = lax.axis_size("dp")
    full_width = experts * width
    probs = router_probs.T
    route = expert_index.reshape(1, token_count)
    send, mask = prelude(capacity, route, probs, tokens, out_grad, expert_out)
    got = lax.all_to_all(send, "expert", split_axis=0, concat_axis=0, tiled=True)
    in_near = fetch(in_weight, got)

    def as_rows(value):
        return value.transpose(1, 0, 2).reshape(value.shape[1], full_width)

    row_tokens, all_grads = as_rows(got[:, :capacity]), as_rows(got[:, capacity:])
    first, last = distances()[:-1], distances()[-1:]
    row_tokens = gather_groups(row_tokens, first)
    all_grads = gather_groups(all_grads, first)
    row_tokens = gather_groups(row_tokens, last)
    all_grads = gather_groups(all_grads, last).reshape(groups, capacity + 8, full_width)
    gate_pre, down_near = hidden_pre(0, row_tokens, in_near, down_weight)
    up_pre = hidden_pre(1, row_tokens, in_near)
    row_grads = all_grads[:, :capacity].reshape(groups * capacity, full_width)
    gate_dot = jnp.sum(got[:, 2 * capacity : 2 * capacity + 3].astype(jnp.float32), axis=(0, 1))
    counts = jnp.sum(all_grads[:, capacity + 3, :experts].astype(jnp.float32), axis=0)

    gate_grad, up_grad, gate_rows, up_rows, kept, away = hidden_back(
        row_grads, gate_pre, up_pre, in_near, down_near
    )
    more_kept, more_away = rest_back(gate_rows, up_rows, in_near)
    summed = kept + swap(away, 1).astype(jnp.float32)
    more = more_kept + swap(more_away, 1).astype(jnp.float32)
    summed = reduce_groups(summed, 2).astype(jnp.bfloat16)
    more = reduce_groups(more, 2).astype(jnp.bfloat16)
    going = jnp.concatenate([summed, more], axis=1)
    going = going.reshape(capacity, experts, width).transpose(1, 0, 2)
    returned = lax.all_to_all(going, "expert", split_axis=0, concat_axis=0, tiled=True)
    weight_grad = half_weight_grad(0, gate_grad, row_tokens)
    weight_grad = half_weight_grad(1, up_grad, row_tokens, weight_grad)

    chosen = (lax.broadcasted_iota(jnp.int32, (experts, token_count), 0) == route).astype(jnp.float32)
    prob_grad = chosen * gate_dot[None, :] + aux_coef * experts * counts[:, None] / (
        token_count * groups
    )
    logit_grad = probs * (prob_grad - jnp.sum(probs * prob_grad, axis=0, keepdims=True))
    logit_grad = logit_grad.astype(jnp.bfloat16)
    router_grad = jnp.dot(logit_grad, tokens, preferred_element_type=jnp.float32)
    for distance in distances()[::-1]:
        router_grad = router_grad + swap(router_grad, distance)
    router_term = lax.dot_general(
        logit_grad, router_weight, (((0,), (1,)), ((), ())), preferred_element_type=jnp.float32
    )
    combined = lax.dot_general(
        mask,
        returned.reshape(experts * capacity, width),
        contract_first,
        preferred_element_type=jnp.float32,
    )
    token_grad = (combined + router_term).astype(jnp.bfloat16)
    return (token_grad, weight_grad, router_grad.T)


def per_device(tokens, out_grad, expert_out, router_probs, *rest):
    token_count, width = tokens.shape
    experts = router_probs.shape[1]
    capacity = (5 * token_count + 4 * experts - 1) // (4 * experts)
    aligned = token_count == width and width % 128 == 0 and capacity % 8 == 0 and experts % 8 == 0
    if not aligned:
        return general_device(tokens, out_grad, expert_out, router_probs, *rest)
    return aligned_device(tokens, out_grad, expert_out, router_probs, *rest)


def solution(mesh):
    in_specs = (
        P("dp", "expert"),
        P("dp", "expert"),
        P("dp", "expert"),
        P("dp", None),
        P("dp", None),
        P("expert", None, "dp", None),
        P("expert", "dp", None),
        P("expert", None),
    )
    out_specs = (P("dp", "expert"), P("expert", None, "dp", None), P("expert", None))
    return jax.shard_map(
        per_device, mesh=mesh, in_specs=in_specs, out_specs=out_specs, check_vma=False
    )
```

```python
import math
from functools import partial

import jax
import jax.numpy as jnp
from jax import lax
from jax.experimental import pallas as pl
from jax.experimental.pallas import tpu as pltpu
from jax.sharding import PartitionSpec as P


aux_coef = 0.2
contract_last = (((1,), (1,)), ((), ()))
contract_first = (((0,), (0,)), ((), ()))


def slot_numbers(routes):
    width = routes.shape[1]
    same_expert = routes[:, :, None] == routes[:, None, :]
    position = jnp.arange(width, dtype=jnp.int32)
    before = position[None, :] < position[:, None]
    return jnp.sum((same_expert & before[None]).astype(jnp.int32), axis=2)


def one_hot(routes, slot_ids, experts, capacity):
    expert_hit = routes[..., None] == jnp.arange(experts, dtype=jnp.int32)
    slot_hit = slot_ids[..., None] == jnp.arange(capacity, dtype=jnp.int32)
    return (expert_hit[..., :, None] & slot_hit[..., None, :]).astype(jnp.float32)


def gelu_parts(pre_act, upstream):
    gelu_value, pullback = jax.vjp(partial(jax.nn.gelu, approximate=True), pre_act)
    return (gelu_value, pullback(upstream)[0])


def swap(value, distance):
    size = lax.axis_size("dp")
    return lax.ppermute(value, "dp", [(i, i ^ distance) for i in range(size)])


def distances():
    found, distance = [], lax.axis_size("dp") // 2
    while distance:
        found.append(distance)
        distance //= 2
    return found


def gather_groups(block, given=()):
    for distance in given or distances():
        block = jnp.concatenate([block, swap(block, distance)], axis=0)
    return block


def reduce_groups(total, first=1):
    order = [distance for distance in distances()[::-1] if distance >= first]
    for distance in order:
        half = total.shape[0] // 2
        away = swap(total[half:].astype(jnp.bfloat16), distance)
        total = total[:half] + away.astype(jnp.float32)
    return total


def weight_grad_kernel(gate_ref, up_ref, rows_ref, out_ref):
    rows = rows_ref[...]
    out_ref[0, 0] = lax.dot_general(
        gate_ref[...], rows, contract_first, preferred_element_type=jnp.float32
    ).astype(jnp.bfloat16)
    out_ref[0, 1] = lax.dot_general(
        up_ref[...], rows, contract_first, preferred_element_type=jnp.float32
    ).astype(jnp.bfloat16)


def weight_grads(gate_grad, up_grad, rows):
    count, hidden = gate_grad.shape
    width = rows.shape[1]
    block = 256 if hidden % 256 == 0 else hidden
    return pl.pallas_call(
        weight_grad_kernel,
        grid=(hidden // block,),
        in_specs=[
            pl.BlockSpec((count, block), lambda j: (0, j)),
            pl.BlockSpec((count, block), lambda j: (0, j)),
            pl.BlockSpec((count, width), lambda j: (0, 0)),
        ],
        out_specs=pl.BlockSpec((1, 2, block, width), lambda j: (0, 0, j, 0)),
        out_shape=jax.ShapeDtypeStruct((1, 2, hidden, width), jnp.bfloat16),
        cost_estimate=pl.CostEstimate(
            flops=4 * count * hidden * width,
            bytes_accessed=4 * hidden * width,
            transcendentals=0,
        ),
        name="weight_grads",
    )(gate_grad, up_grad, rows)


def split_float(value):
    high = lax.reduce_precision(value, 8, 7)
    middle = lax.reduce_precision(value - high, 8, 7)
    return jnp.stack([high, middle, value - high - middle]).astype(jnp.bfloat16)


def general_device(
    tokens, out_grad, expert_out, router_probs, expert_index, in_weight, down_weight, router_weight
):
    token_count, feature_width = tokens.shape
    experts = router_probs.shape[1]
    capacity = (5 * token_count + 4 * experts - 1) // (4 * experts)
    groups = lax.axis_size("dp")
    routes = expert_index[:, 0]
    slot_ids = slot_numbers(routes[None, :])[0]
    dispatch_mask = one_hot(routes, slot_ids, experts, capacity)
    mask_half = dispatch_mask.astype(jnp.bfloat16)
    chosen = jnp.sum(dispatch_mask, axis=2)

    def exchange(value):
        return lax.all_to_all(value, "expert", split_axis=0, concat_axis=2, tiled=True)[0]

    send_tokens = jnp.einsum(
        "tec,tf->ecf", mask_half, tokens, preferred_element_type=jnp.float32
    ).astype(jnp.bfloat16)
    got_tokens = exchange(send_tokens)

    gate = jnp.sum(router_probs * chosen, axis=1)
    gated_dy = (gate[:, None] * out_grad.astype(jnp.float32)).astype(jnp.bfloat16)
    send_grads = jnp.einsum(
        "tec,tf->ecf", mask_half, gated_dy, preferred_element_type=jnp.float32
    ).astype(jnp.bfloat16)
    partial_dot = jnp.sum(out_grad.astype(jnp.float32) * expert_out.astype(jnp.float32), axis=1)
    dot_rows = token_count // feature_width
    pieces = split_float(partial_dot).reshape(3 * dot_rows, feature_width)
    local_counts = jnp.sum(chosen, axis=0)
    count_row = jnp.pad(local_counts.astype(jnp.bfloat16)[None], ((0, 0), (0, feature_width - experts)))
    side = jnp.concatenate([pieces, count_row], axis=0)
    side_rows = -(-(capacity + side.shape[0]) // 8) * 8 - capacity
    side = jnp.pad(side, ((0, side_rows - side.shape[0]), (0, 0)))
    send_grads = jnp.concatenate(
        [send_grads, jnp.broadcast_to(side[None], (experts, side_rows, feature_width))], axis=1
    )
    got_grads = exchange(send_grads)

    row_tokens = gather_groups(got_tokens)
    all_grads = gather_groups(got_grads).reshape(groups, capacity + side_rows, -1)
    row_grads = all_grads[:, :capacity].reshape(groups * capacity, -1)
    own_side = got_grads[capacity:].astype(jnp.float32)
    gate_dot = jnp.sum(
        own_side[: 3 * dot_rows].reshape(3, dot_rows, experts, feature_width), axis=(0, 2)
    ).reshape(token_count)
    counts = jnp.sum(all_grads[:, capacity + 3 * dot_rows, :experts].astype(jnp.float32), axis=0)

    gate_weight = in_weight[0, 0]
    up_weight = in_weight[0, 1]
    gate_pre = lax.dot_general(
        row_tokens, gate_weight, contract_last, preferred_element_type=jnp.float32
    )
    up_pre = lax.dot_general(
        row_tokens, up_weight, contract_last, preferred_element_type=jnp.float32
    )
    hidden_grad = lax.dot_general(
        row_grads, down_weight[0], contract_last, preferred_element_type=jnp.float32
    )
    gate_act, gate_back = gelu_parts(gate_pre, hidden_grad * up_pre)
    gate_grad = gate_back.astype(jnp.bfloat16)
    up_grad = (hidden_grad * gate_act).astype(jnp.bfloat16)
    term = jnp.dot(gate_grad, gate_weight, preferred_element_type=jnp.float32)
    term = term + jnp.dot(up_grad, up_weight, preferred_element_type=jnp.float32)
    summed = reduce_groups(term)
    going = summed.astype(jnp.bfloat16).reshape(capacity, experts, feature_width)
    returned = lax.all_to_all(
        going.transpose(1, 0, 2), "expert", split_axis=0, concat_axis=0, tiled=True
    )
    weight_grad = weight_grads(gate_grad, up_grad, row_tokens)

    prob_grad = chosen * gate_dot[:, None] + aux_coef * experts * counts[None, :] / (
        token_count * groups
    )
    logit_grad = router_probs * (
        prob_grad - jnp.sum(router_probs * prob_grad, axis=1, keepdims=True)
    )
    logit_grad = logit_grad.astype(jnp.bfloat16)
    router_grad = lax.dot_general(
        tokens, logit_grad, contract_first, preferred_element_type=jnp.float32
    )
    for distance in distances():
        router_grad = router_grad + swap(router_grad, distance)
    router_term = lax.dot_general(
        logit_grad, router_weight, contract_last, preferred_element_type=jnp.float32
    )
    combined = jnp.einsum(
        "tec,ecf->tf", mask_half, returned, preferred_element_type=jnp.float32
    )
    token_grad = (combined + router_term).astype(jnp.bfloat16)
    return (token_grad, weight_grad, router_grad)


def prelude_kernel(
    capacity,
    route_hbm,
    probs_hbm,
    tokens_hbm,
    grads_hbm,
    expert_out_hbm,
    down_hbm,
    send_ref,
    place_ref,
    down_ref,
    route_ref,
    probs_ref,
    tokens_ref,
    grads_ref,
    expert_out_ref,
    sems,
):
    sources = (route_hbm, probs_hbm, tokens_hbm, grads_hbm, expert_out_hbm)
    targets = (route_ref, probs_ref, tokens_ref, grads_ref, expert_out_ref)
    copies = [
        pltpu.make_async_copy(source, target, sems.at[number])
        for number, (source, target) in enumerate(zip(sources, targets))
    ]
    pieces = sems.shape[0] - len(copies)
    size = down_ref.shape[0] // pieces
    for piece in range(pieces):
        rows = pl.ds(piece * size, size)
        copies.append(
            pltpu.make_async_copy(down_hbm.at[0, rows], down_ref.at[rows], sems.at[len(copies)])
        )
    for copy in copies:
        copy.start()
    experts, count = probs_ref.shape
    width = tokens_ref.shape[1]
    half, full = jnp.bfloat16, jnp.float32
    iota = lambda shape, axis: lax.broadcasted_iota(jnp.int32, shape, axis)
    dot = partial(lax.dot_general, preferred_element_type=full)
    plain = (((1,), (0,)), ((), ()))
    square = (count, count)
    earlier = (iota(square, 0) < iota(square, 1)).astype(full).astype(half)
    copies[0].wait()
    route = route_ref[...]
    hit = iota((experts, count), 0) == route
    before = dot(hit.astype(full).astype(half), earlier, plain)
    slot = jnp.sum(jnp.where(hit, before, 0.0), axis=0, keepdims=True)
    place = iota((experts * capacity, count), 0) == route * capacity + slot.astype(jnp.int32)
    mask = place.astype(full).astype(half)
    place_ref[...] = mask
    copies[1].wait()
    gate = jnp.sum(jnp.where(hit, probs_ref[...], 0.0), axis=0, keepdims=True)
    row_gate = jnp.sum(jnp.where(place, gate, 0.0), axis=1, keepdims=True)
    copies[2].wait()
    rows_x = dot(mask, tokens_ref[...], plain)
    copies[3].wait()
    rows_dy = dot(mask, grads_ref[...], plain) * row_gate
    copies[4].wait()
    product = grads_ref[...].astype(full) * expert_out_ref[...].astype(full)
    high = product.astype(half)
    low = (product - high.astype(full)).astype(half)
    ones = jnp.ones((8, width), half)
    part = dot(ones, high, contract_last) + dot(ones, low, contract_last)
    first = part.astype(half).astype(full)
    second = (part - first).astype(half).astype(full)
    third = part - first - second
    listed = (iota((width, count), 0) == route).astype(full).astype(half)
    counts = dot(jnp.ones((8, count), half), listed, contract_last)
    line = iota((8, width), 0)
    side = jnp.where(line == 3, counts, 0.0)
    for number, piece in enumerate((first, second, third)):
        side = jnp.where(line == number, piece, side)
    side = side.astype(half)
    for expert in range(experts):
        rows = slice(expert * capacity, (expert + 1) * capacity)
        send_ref[expert, :capacity] = rows_x[rows].astype(half)
        send_ref[expert, capacity : 2 * capacity] = rows_dy[rows].astype(half)
        send_ref[expert, 2 * capacity :] = side
    for copy in copies[5:]:
        copy.wait()


def far(value):
    return pltpu.with_memory_space_constraint(value, pltpu.HBM)


def near(value):
    return pltpu.with_memory_space_constraint(value, pltpu.VMEM)


def prelude(capacity, down_weight, *args):
    experts, count = args[1].shape
    width = args[2].shape[1]
    return pl.pallas_call(
        partial(prelude_kernel, capacity),
        in_specs=[pl.BlockSpec(memory_space=pl.ANY)] * (len(args) + 1),
        out_specs=[pl.BlockSpec(memory_space=pltpu.VMEM)] * 3,
        out_shape=(
            jax.ShapeDtypeStruct((experts, 2 * capacity + 8, width), jnp.bfloat16),
            jax.ShapeDtypeStruct((experts * capacity, count), jnp.bfloat16),
            pltpu.VMEM((down_weight.shape[1] // 2, down_weight.shape[2]), down_weight.dtype),
        ),
        scratch_shapes=[pltpu.VMEM(value.shape, value.dtype) for value in args]
        + [pltpu.SemaphoreType.DMA((len(args) + 2,))],
        compiler_params=pltpu.CompilerParams(vmem_limit_bytes=8 << 20),
        name="prelude",
    )(*[far(value) for value in args], far(down_weight))


def fetch_kernel(pieces, source_ref, after_ref, target_ref, sems):
    planes, hidden = source_ref.shape[1:3]
    size = hidden // pieces
    copies = []
    for plane in range(planes):
        for piece in range(pieces):
            where = (0, plane, pl.ds(piece * size, size))
            copies.append(
                pltpu.make_async_copy(
                    source_ref.at[where], target_ref.at[where], sems.at[len(copies)]
                )
            )
    for copy in copies:
        copy.start()
    for copy in copies:
        copy.wait()


def fetch(weight, after):
    pieces = 4
    return pl.pallas_call(
        partial(fetch_kernel, pieces),
        in_specs=[pl.BlockSpec(memory_space=pl.ANY)] * 2,
        out_specs=pl.BlockSpec(memory_space=pltpu.VMEM),
        out_shape=pltpu.VMEM(weight.shape, weight.dtype),
        scratch_shapes=[pltpu.SemaphoreType.DMA((weight.shape[1] * pieces,))],
        compiler_params=pltpu.CompilerParams(vmem_limit_bytes=1 << 20),
        cost_estimate=pl.CostEstimate(
            flops=0, bytes_accessed=2 * weight.size, transcendentals=0
        ),
        name="fetch",
    )(far(weight), after)


def pre_activation(which, rows_ref, in_ref, out_ref):
    rows = rows_ref[...]
    size = in_ref.shape[2] // 2
    for start in (0, size):
        part = slice(start, start + size)
        out_ref[part] = lax.dot_general(
            in_ref[0, which, part], rows, contract_last, preferred_element_type=jnp.float32
        )


def gate_pre_kernel(rows_ref, in_ref, down_hbm, out_ref, down_ref, sems):
    pieces = sems.shape[0]
    half = down_ref.shape[0]
    size = half // pieces
    copies = [
        pltpu.make_async_copy(
            down_hbm.at[0, pl.ds(half + piece * size, size)],
            down_ref.at[pl.ds(piece * size, size)],
            sems.at[piece],
        )
        for piece in range(pieces)
    ]
    for copy in copies:
        copy.start()
    pre_activation(0, rows_ref, in_ref, out_ref)
    for copy in copies:
        copy.wait()


def hidden_pre(which, rows, in_near, down_weight=None):
    count, width = rows.shape
    hidden = in_near.shape[2]
    near_spec = pl.BlockSpec(memory_space=pltpu.VMEM)
    out = pltpu.VMEM((hidden, count), jnp.float32)
    settings = dict(
        compiler_params=pltpu.CompilerParams(vmem_limit_bytes=8 << 20),
        cost_estimate=pl.CostEstimate(
            flops=2 * count * hidden * width, bytes_accessed=2 * hidden * width, transcendentals=0
        ),
    )
    if down_weight is None:
        return pl.pallas_call(
            partial(pre_activation, which),
            in_specs=[near_spec] * 2,
            out_specs=near_spec,
            out_shape=out,
            name="hidden_pre",
            **settings,
        )(rows, near(in_near))
    return pl.pallas_call(
        gate_pre_kernel,
        in_specs=[near_spec] * 2 + [pl.BlockSpec(memory_space=pl.ANY)],
        out_specs=[near_spec] * 2,
        out_shape=(out, pltpu.VMEM((hidden // 2, width), down_weight.dtype)),
        scratch_shapes=[pltpu.SemaphoreType.DMA((4,))],
        name="gate_pre",
        **settings,
    )(rows, near(in_near), far(down_weight))


def block_of(size, wanted):
    return wanted if size % wanted == 0 else size


def input_grads(rows, in_ref, first, kept_ref, away_ref, block):
    half = kept_ref.shape[0]
    for start in range(0, kept_ref.shape[1], block):
        part, columns = slice(start, start + block), slice(first + start, first + start + block)
        total = jnp.dot(rows[0], in_ref[0, 0, :, columns], preferred_element_type=jnp.float32)
        total += jnp.dot(rows[1], in_ref[0, 1, :, columns], preferred_element_type=jnp.float32)
        kept_ref[:, part] = total[:half]
        away_ref[:, part] = total[half:].astype(jnp.bfloat16)


def hidden_back_kernel(
    block,
    rows_ref,
    gate_pre_ref,
    up_pre_ref,
    in_ref,
    down_ref,
    other_ref,
    gate_ref,
    up_ref,
    gate_rows_ref,
    up_rows_ref,
    kept_ref,
    away_ref,
):
    size = down_ref.shape[0]
    rows = rows_ref[...]
    scale, cubic = math.sqrt(2 / math.pi), 0.044715
    for number, weight_ref in enumerate((down_ref, other_ref)):
        part = slice(number * size, (number + 1) * size)
        grad = lax.dot_general(
            weight_ref[...], rows, contract_last, preferred_element_type=jnp.float32
        )
        value, up = gate_pre_ref[part], up_pre_ref[part]
        square = value * value
        bend = jnp.tanh(scale * (value + cubic * (square * value)))
        cdf = 0.5 * (1.0 + bend)
        slope = cdf + (0.5 * scale) * value * (1.0 - bend * bend) * (1.0 + 3 * cubic * square)
        gate_ref[part] = (grad * up * slope).astype(jnp.bfloat16)
        up_ref[part] = (grad * (value * cdf)).astype(jnp.bfloat16)
    gate_rows_ref[...] = gate_ref[...].T
    up_rows_ref[...] = up_ref[...].T
    input_grads((gate_rows_ref[...], up_rows_ref[...]), in_ref, 0, kept_ref, away_ref, block)


def rest_back_kernel(block, gate_rows_ref, up_rows_ref, in_ref, kept_ref, away_ref):
    first = in_ref.shape[3] - kept_ref.shape[1]
    input_grads((gate_rows_ref[...], up_rows_ref[...]), in_ref, first, kept_ref, away_ref, block)


def hidden_back(rows, gate_pre, up_pre, in_near, downs):
    count, width = rows.shape
    hidden = in_near.shape[2]
    near_spec = pl.BlockSpec(memory_space=pltpu.VMEM)
    return pl.pallas_call(
        partial(hidden_back_kernel, width // 2),
        in_specs=[near_spec] * 6,
        out_specs=[near_spec] * 6,
        out_shape=(
            pltpu.VMEM((hidden, count), jnp.bfloat16),
            pltpu.VMEM((hidden, count), jnp.bfloat16),
            pltpu.VMEM((count, hidden), jnp.bfloat16),
            pltpu.VMEM((count, hidden), jnp.bfloat16),
            pltpu.VMEM((count // 2, width // 2), jnp.float32),
            pltpu.VMEM((count // 2, width // 2), jnp.bfloat16),
        ),
        compiler_params=pltpu.CompilerParams(vmem_limit_bytes=12 << 20),
        cost_estimate=pl.CostEstimate(
            flops=4 * count * hidden * width,
            bytes_accessed=4 * hidden * width,
            transcendentals=count * hidden,
        ),
        name="hidden_back",
    )(rows, near(gate_pre), near(up_pre), near(in_near), *map(near, downs))


def rest_back(gate_rows, up_rows, in_near):
    count, hidden = gate_rows.shape
    width = in_near.shape[3]
    near_spec = pl.BlockSpec(memory_space=pltpu.VMEM)
    return pl.pallas_call(
        partial(rest_back_kernel, width // 2),
        in_specs=[near_spec] * 3,
        out_specs=[near_spec] * 2,
        out_shape=(
            pltpu.VMEM((count // 2, width // 2), jnp.float32),
            pltpu.VMEM((count // 2, width // 2), jnp.bfloat16),
        ),
        compiler_params=pltpu.CompilerParams(vmem_limit_bytes=12 << 20),
        cost_estimate=pl.CostEstimate(
            flops=2 * count * hidden * width, bytes_accessed=2 * hidden * width, transcendentals=0
        ),
        name="rest_back",
    )(near(gate_rows), near(up_rows), near(in_near))


def half_kernel(grad_ref, rows_ref, *refs):
    refs[-1][0, 0] = jnp.dot(
        grad_ref[...], rows_ref[...], preferred_element_type=jnp.float32
    ).astype(jnp.bfloat16)


def half_weight_grad(which, grad, rows, partly=None):
    hidden, count = grad.shape
    width = rows.shape[1]
    block = block_of(hidden, 640)
    given = [] if partly is None else [partly]
    return pl.pallas_call(
        half_kernel,
        grid=(hidden // block,),
        in_specs=[
            pl.BlockSpec((block, count), lambda j: (j, 0)),
            pl.BlockSpec((count, width), lambda j: (0, 0)),
        ]
        + [pl.BlockSpec(memory_space=pl.ANY)] * len(given),
        out_specs=pl.BlockSpec((1, 1, block, width), lambda j: (0, which, j, 0)),
        out_shape=jax.ShapeDtypeStruct((1, 2, hidden, width), jnp.bfloat16),
        input_output_aliases={2: 0} if given else {},
        compiler_params=pltpu.CompilerParams(vmem_limit_bytes=20 << 20),
        cost_estimate=pl.CostEstimate(
            flops=2 * count * hidden * width, bytes_accessed=2 * hidden * width, transcendentals=0
        ),
        name="weight_grad_half",
    )(grad, rows, *given)


def aligned_device(
    tokens, out_grad, expert_out, router_probs, expert_index, in_weight, down_weight, router_weight
):
    token_count, width = tokens.shape
    experts = router_probs.shape[1]
    capacity = (5 * token_count + 4 * experts - 1) // (4 * experts)
    groups = lax.axis_size("dp")
    full_width = experts * width
    probs = router_probs.T
    route = expert_index.reshape(1, token_count)
    send, mask, first_down = prelude(
        capacity, down_weight, route, probs, tokens, out_grad, expert_out
    )
    got = lax.all_to_all(send, "expert", split_axis=0, concat_axis=0, tiled=True)
    in_near = fetch(in_weight, got)

    def as_rows(value):
        return value.transpose(1, 0, 2).reshape(value.shape[1], full_width)

    row_tokens, all_grads = as_rows(got[:, :capacity]), as_rows(got[:, capacity:])
    first, last = distances()[:-1], distances()[-1:]
    row_tokens = gather_groups(row_tokens, first)
    all_grads = gather_groups(all_grads, first)
    row_tokens = gather_groups(row_tokens, last)
    all_grads = gather_groups(all_grads, last).reshape(groups, capacity + 8, full_width)
    gate_pre, second_down = hidden_pre(0, row_tokens, in_near, down_weight)
    up_pre = hidden_pre(1, row_tokens, in_near)
    row_grads = all_grads[:, :capacity].reshape(groups * capacity, full_width)
    gate_dot = jnp.sum(got[:, 2 * capacity : 2 * capacity + 3].astype(jnp.float32), axis=(0, 1))
    counts = jnp.sum(all_grads[:, capacity + 3, :experts].astype(jnp.float32), axis=0)

    gate_grad, up_grad, gate_rows, up_rows, kept, away = hidden_back(
        row_grads, gate_pre, up_pre, in_near, (first_down, second_down)
    )
    more_kept, more_away = rest_back(gate_rows, up_rows, in_near)
    summed = kept + swap(away, 1).astype(jnp.float32)
    more = more_kept + swap(more_away, 1).astype(jnp.float32)
    summed = reduce_groups(summed, 2).astype(jnp.bfloat16)
    more = reduce_groups(more, 2).astype(jnp.bfloat16)
    going = jnp.concatenate([summed, more], axis=1)
    going = going.reshape(capacity, experts, width).transpose(1, 0, 2)
    returned = lax.all_to_all(going, "expert", split_axis=0, concat_axis=0, tiled=True)
    weight_grad = half_weight_grad(0, gate_grad, row_tokens)
    weight_grad = half_weight_grad(1, up_grad, row_tokens, weight_grad)

    chosen = (lax.broadcasted_iota(jnp.int32, (experts, token_count), 0) == route).astype(jnp.float32)
    prob_grad = chosen * gate_dot[None, :] + aux_coef * experts * counts[:, None] / (
        token_count * groups
    )
    logit_grad = probs * (prob_grad - jnp.sum(probs * prob_grad, axis=0, keepdims=True))
    logit_grad = logit_grad.astype(jnp.bfloat16)
    router_grad = jnp.dot(logit_grad, tokens, preferred_element_type=jnp.float32)
    for distance in distances()[::-1]:
        router_grad = router_grad + swap(router_grad, distance)
    router_term = lax.dot_general(
        logit_grad, router_weight, (((0,), (1,)), ((), ())), preferred_element_type=jnp.float32
    )
    combined = lax.dot_general(
        mask,
        returned.reshape(experts * capacity, width),
        contract_first,
        preferred_element_type=jnp.float32,
    )
    token_grad = (combined + router_term).astype(jnp.bfloat16)
    return (token_grad, weight_grad, router_grad.T)


def per_device(tokens, out_grad, expert_out, router_probs, *rest):
    token_count, width = tokens.shape
    experts = router_probs.shape[1]
    capacity = (5 * token_count + 4 * experts - 1) // (4 * experts)
    aligned = token_count == width and width % 128 == 0 and capacity % 8 == 0 and experts % 8 == 0
    if not aligned:
        return general_device(tokens, out_grad, expert_out, router_probs, *rest)
    return aligned_device(tokens, out_grad, expert_out, router_probs, *rest)


def solution(mesh):
    in_specs = (
        P("dp", "expert"),
        P("dp", "expert"),
        P("dp", "expert"),
        P("dp", None),
        P("dp", None),
        P("expert", None, "dp", None),
        P("expert", "dp", None),
        P("expert", None),
    )
    out_specs = (P("dp", "expert"), P("expert", None, "dp", None), P("expert", None))
    return jax.shard_map(
        per_device, mesh=mesh, in_specs=in_specs, out_specs=out_specs, check_vma=False
    )
```

```python
import math
from functools import partial

import jax
import jax.numpy as jnp
from jax import lax
from jax.experimental import pallas as pl
from jax.experimental.pallas import tpu as pltpu
from jax.sharding import PartitionSpec as P


aux_coef = 0.2
contract_last = (((1,), (1,)), ((), ()))
contract_first = (((0,), (0,)), ((), ()))


def slot_numbers(routes):
    width = routes.shape[1]
    same_expert = routes[:, :, None] == routes[:, None, :]
    position = jnp.arange(width, dtype=jnp.int32)
    before = position[None, :] < position[:, None]
    return jnp.sum((same_expert & before[None]).astype(jnp.int32), axis=2)


def one_hot(routes, slot_ids, experts, capacity):
    expert_hit = routes[..., None] == jnp.arange(experts, dtype=jnp.int32)
    slot_hit = slot_ids[..., None] == jnp.arange(capacity, dtype=jnp.int32)
    return (expert_hit[..., :, None] & slot_hit[..., None, :]).astype(jnp.float32)


def gelu_parts(pre_act, upstream):
    gelu_value, pullback = jax.vjp(partial(jax.nn.gelu, approximate=True), pre_act)
    return (gelu_value, pullback(upstream)[0])


def swap(value, distance):
    size = lax.axis_size("dp")
    return lax.ppermute(value, "dp", [(i, i ^ distance) for i in range(size)])


def distances():
    found, distance = [], lax.axis_size("dp") // 2
    while distance:
        found.append(distance)
        distance //= 2
    return found


def gather_groups(block, given=()):
    for distance in given or distances():
        block = jnp.concatenate([block, swap(block, distance)], axis=0)
    return block


def reduce_groups(total, first=1):
    order = [distance for distance in distances()[::-1] if distance >= first]
    for distance in order:
        half = total.shape[0] // 2
        away = swap(total[half:].astype(jnp.bfloat16), distance)
        total = total[:half] + away.astype(jnp.float32)
    return total


def weight_grad_kernel(gate_ref, up_ref, rows_ref, out_ref):
    rows = rows_ref[...]
    out_ref[0, 0] = lax.dot_general(
        gate_ref[...], rows, contract_first, preferred_element_type=jnp.float32
    ).astype(jnp.bfloat16)
    out_ref[0, 1] = lax.dot_general(
        up_ref[...], rows, contract_first, preferred_element_type=jnp.float32
    ).astype(jnp.bfloat16)


def weight_grads(gate_grad, up_grad, rows):
    count, hidden = gate_grad.shape
    width = rows.shape[1]
    block = 256 if hidden % 256 == 0 else hidden
    return pl.pallas_call(
        weight_grad_kernel,
        grid=(hidden // block,),
        in_specs=[
            pl.BlockSpec((count, block), lambda j: (0, j)),
            pl.BlockSpec((count, block), lambda j: (0, j)),
            pl.BlockSpec((count, width), lambda j: (0, 0)),
        ],
        out_specs=pl.BlockSpec((1, 2, block, width), lambda j: (0, 0, j, 0)),
        out_shape=jax.ShapeDtypeStruct((1, 2, hidden, width), jnp.bfloat16),
        cost_estimate=pl.CostEstimate(
            flops=4 * count * hidden * width,
            bytes_accessed=4 * hidden * width,
            transcendentals=0,
        ),
        name="weight_grads",
    )(gate_grad, up_grad, rows)


def split_float(value):
    high = lax.reduce_precision(value, 8, 7)
    middle = lax.reduce_precision(value - high, 8, 7)
    return jnp.stack([high, middle, value - high - middle]).astype(jnp.bfloat16)


def general_device(
    tokens, out_grad, expert_out, router_probs, expert_index, in_weight, down_weight, router_weight
):
    token_count, feature_width = tokens.shape
    experts = router_probs.shape[1]
    capacity = (5 * token_count + 4 * experts - 1) // (4 * experts)
    groups = lax.axis_size("dp")
    routes = expert_index[:, 0]
    slot_ids = slot_numbers(routes[None, :])[0]
    dispatch_mask = one_hot(routes, slot_ids, experts, capacity)
    mask_half = dispatch_mask.astype(jnp.bfloat16)
    chosen = jnp.sum(dispatch_mask, axis=2)

    def exchange(value):
        return lax.all_to_all(value, "expert", split_axis=0, concat_axis=2, tiled=True)[0]

    send_tokens = jnp.einsum(
        "tec,tf->ecf", mask_half, tokens, preferred_element_type=jnp.float32
    ).astype(jnp.bfloat16)
    got_tokens = exchange(send_tokens)

    gate = jnp.sum(router_probs * chosen, axis=1)
    gated_dy = (gate[:, None] * out_grad.astype(jnp.float32)).astype(jnp.bfloat16)
    send_grads = jnp.einsum(
        "tec,tf->ecf", mask_half, gated_dy, preferred_element_type=jnp.float32
    ).astype(jnp.bfloat16)
    partial_dot = jnp.sum(out_grad.astype(jnp.float32) * expert_out.astype(jnp.float32), axis=1)
    dot_rows = token_count // feature_width
    pieces = split_float(partial_dot).reshape(3 * dot_rows, feature_width)
    local_counts = jnp.sum(chosen, axis=0)
    count_row = jnp.pad(local_counts.astype(jnp.bfloat16)[None], ((0, 0), (0, feature_width - experts)))
    side = jnp.concatenate([pieces, count_row], axis=0)
    side_rows = -(-(capacity + side.shape[0]) // 8) * 8 - capacity
    side = jnp.pad(side, ((0, side_rows - side.shape[0]), (0, 0)))
    send_grads = jnp.concatenate(
        [send_grads, jnp.broadcast_to(side[None], (experts, side_rows, feature_width))], axis=1
    )
    got_grads = exchange(send_grads)

    row_tokens = gather_groups(got_tokens)
    all_grads = gather_groups(got_grads).reshape(groups, capacity + side_rows, -1)
    row_grads = all_grads[:, :capacity].reshape(groups * capacity, -1)
    own_side = got_grads[capacity:].astype(jnp.float32)
    gate_dot = jnp.sum(
        own_side[: 3 * dot_rows].reshape(3, dot_rows, experts, feature_width), axis=(0, 2)
    ).reshape(token_count)
    counts = jnp.sum(all_grads[:, capacity + 3 * dot_rows, :experts].astype(jnp.float32), axis=0)

    gate_weight = in_weight[0, 0]
    up_weight = in_weight[0, 1]
    gate_pre = lax.dot_general(
        row_tokens, gate_weight, contract_last, preferred_element_type=jnp.float32
    )
    up_pre = lax.dot_general(
        row_tokens, up_weight, contract_last, preferred_element_type=jnp.float32
    )
    hidden_grad = lax.dot_general(
        row_grads, down_weight[0], contract_last, preferred_element_type=jnp.float32
    )
    gate_act, gate_back = gelu_parts(gate_pre, hidden_grad * up_pre)
    gate_grad = gate_back.astype(jnp.bfloat16)
    up_grad = (hidden_grad * gate_act).astype(jnp.bfloat16)
    term = jnp.dot(gate_grad, gate_weight, preferred_element_type=jnp.float32)
    term = term + jnp.dot(up_grad, up_weight, preferred_element_type=jnp.float32)
    summed = reduce_groups(term)
    going = summed.astype(jnp.bfloat16).reshape(capacity, experts, feature_width)
    returned = lax.all_to_all(
        going.transpose(1, 0, 2), "expert", split_axis=0, concat_axis=0, tiled=True
    )
    weight_grad = weight_grads(gate_grad, up_grad, row_tokens)

    prob_grad = chosen * gate_dot[:, None] + aux_coef * experts * counts[None, :] / (
        token_count * groups
    )
    logit_grad = router_probs * (
        prob_grad - jnp.sum(router_probs * prob_grad, axis=1, keepdims=True)
    )
    logit_grad = logit_grad.astype(jnp.bfloat16)
    router_grad = lax.dot_general(
        tokens, logit_grad, contract_first, preferred_element_type=jnp.float32
    )
    for distance in distances():
        router_grad = router_grad + swap(router_grad, distance)
    router_term = lax.dot_general(
        logit_grad, router_weight, contract_last, preferred_element_type=jnp.float32
    )
    combined = jnp.einsum(
        "tec,ecf->tf", mask_half, returned, preferred_element_type=jnp.float32
    )
    token_grad = (combined + router_term).astype(jnp.bfloat16)
    return (token_grad, weight_grad, router_grad)


def prelude_kernel(
    capacity,
    route_hbm,
    probs_hbm,
    tokens_hbm,
    grads_hbm,
    expert_out_hbm,
    down_hbm,
    send_ref,
    place_ref,
    down_ref,
    route_ref,
    probs_ref,
    tokens_ref,
    grads_ref,
    expert_out_ref,
    sems,
):
    sources = (route_hbm, probs_hbm, tokens_hbm, grads_hbm, expert_out_hbm)
    targets = (route_ref, probs_ref, tokens_ref, grads_ref, expert_out_ref)
    copies = [
        pltpu.make_async_copy(source, target, sems.at[number])
        for number, (source, target) in enumerate(zip(sources, targets))
    ]
    pieces = sems.shape[0] - len(copies)
    size = down_ref.shape[0] // pieces
    for piece in range(pieces):
        rows = pl.ds(piece * size, size)
        copies.append(
            pltpu.make_async_copy(down_hbm.at[0, rows], down_ref.at[rows], sems.at[len(copies)])
        )
    for copy in copies:
        copy.start()
    experts, count = probs_ref.shape
    width = tokens_ref.shape[1]
    half, full = jnp.bfloat16, jnp.float32
    iota = lambda shape, axis: lax.broadcasted_iota(jnp.int32, shape, axis)
    dot = partial(lax.dot_general, preferred_element_type=full)
    plain = (((1,), (0,)), ((), ()))
    square = (count, count)
    earlier = (iota(square, 0) < iota(square, 1)).astype(full).astype(half)
    copies[0].wait()
    route = route_ref[...]
    hit = iota((experts, count), 0) == route
    before = dot(hit.astype(full).astype(half), earlier, plain)
    slot = jnp.sum(jnp.where(hit, before, 0.0), axis=0, keepdims=True)
    place = iota((experts * capacity, count), 0) == route * capacity + slot.astype(jnp.int32)
    mask = place.astype(full).astype(half)
    own = lax.axis_index("expert")
    turned = iota((experts * capacity, count), 0) == (route ^ own) * capacity + slot.astype(jnp.int32)
    place_ref[...] = turned.astype(full).astype(half)
    copies[1].wait()
    gate = jnp.sum(jnp.where(hit, probs_ref[...], 0.0), axis=0, keepdims=True)
    row_gate = jnp.sum(jnp.where(place, gate, 0.0), axis=1, keepdims=True)
    copies[2].wait()
    rows_x = dot(mask, tokens_ref[...], plain)
    copies[3].wait()
    rows_dy = dot(mask, grads_ref[...], plain) * row_gate
    copies[4].wait()
    product = grads_ref[...].astype(full) * expert_out_ref[...].astype(full)
    high = product.astype(half)
    low = (product - high.astype(full)).astype(half)
    ones = jnp.ones((8, width), half)
    part = dot(ones, high, contract_last) + dot(ones, low, contract_last)
    first = part.astype(half).astype(full)
    second = (part - first).astype(half).astype(full)
    third = part - first - second
    listed = (iota((width, count), 0) == route).astype(full).astype(half)
    counts = dot(jnp.ones((8, count), half), listed, contract_last)
    line = iota((8, width), 0)
    side = jnp.where(line == 3, counts, 0.0)
    for number, piece in enumerate((first, second, third)):
        side = jnp.where(line == number, piece, side)
    side = side.astype(half)
    for expert in range(experts):
        rows = slice(expert * capacity, (expert + 1) * capacity)
        send_ref[expert, :capacity] = rows_x[rows].astype(half)
        send_ref[expert, capacity : 2 * capacity] = rows_dy[rows].astype(half)
        send_ref[expert, 2 * capacity :] = side
    for copy in copies[5:]:
        copy.wait()


def far(value):
    return pltpu.with_memory_space_constraint(value, pltpu.HBM)


def near(value):
    return pltpu.with_memory_space_constraint(value, pltpu.VMEM)


def prelude(capacity, down_weight, *args):
    experts, count = args[1].shape
    width = args[2].shape[1]
    return pl.pallas_call(
        partial(prelude_kernel, capacity),
        in_specs=[pl.BlockSpec(memory_space=pl.ANY)] * (len(args) + 1),
        out_specs=[pl.BlockSpec(memory_space=pltpu.VMEM)] * 3,
        out_shape=(
            jax.ShapeDtypeStruct((experts, 2 * capacity + 8, width), jnp.bfloat16),
            jax.ShapeDtypeStruct((experts * capacity, count), jnp.bfloat16),
            pltpu.VMEM((down_weight.shape[1] // 2, down_weight.shape[2]), down_weight.dtype),
        ),
        scratch_shapes=[pltpu.VMEM(value.shape, value.dtype) for value in args]
        + [pltpu.SemaphoreType.DMA((len(args) + 2,))],
        compiler_params=pltpu.CompilerParams(vmem_limit_bytes=8 << 20),
        name="prelude",
    )(*[far(value) for value in args], far(down_weight))


def fetch_kernel(pieces, source_ref, after_ref, target_ref, sems):
    planes, hidden = source_ref.shape[1:3]
    size = hidden // pieces
    copies = []
    for plane in range(planes):
        for piece in range(pieces):
            where = (0, plane, pl.ds(piece * size, size))
            copies.append(
                pltpu.make_async_copy(
                    source_ref.at[where], target_ref.at[where], sems.at[len(copies)]
                )
            )
    for copy in copies:
        copy.start()
    for copy in copies:
        copy.wait()


def fetch(weight, after):
    pieces = 4
    return pl.pallas_call(
        partial(fetch_kernel, pieces),
        in_specs=[pl.BlockSpec(memory_space=pl.ANY)] * 2,
        out_specs=pl.BlockSpec(memory_space=pltpu.VMEM),
        out_shape=pltpu.VMEM(weight.shape, weight.dtype),
        scratch_shapes=[pltpu.SemaphoreType.DMA((weight.shape[1] * pieces,))],
        compiler_params=pltpu.CompilerParams(vmem_limit_bytes=1 << 20),
        cost_estimate=pl.CostEstimate(
            flops=0, bytes_accessed=2 * weight.size, transcendentals=0
        ),
        name="fetch",
    )(far(weight), after)


def pre_activation(which, rows_ref, in_ref, out_ref):
    rows = rows_ref[...]
    size = in_ref.shape[2] // 2
    for start in (0, size):
        part = slice(start, start + size)
        out_ref[part] = lax.dot_general(
            in_ref[0, which, part], rows, contract_last, preferred_element_type=jnp.float32
        )


def gate_pre_kernel(rows_ref, in_ref, down_hbm, out_ref, down_ref, sems):
    pieces = sems.shape[0]
    half = down_ref.shape[0]
    size = half // pieces
    copies = [
        pltpu.make_async_copy(
            down_hbm.at[0, pl.ds(half + piece * size, size)],
            down_ref.at[pl.ds(piece * size, size)],
            sems.at[piece],
        )
        for piece in range(pieces)
    ]
    for copy in copies:
        copy.start()
    pre_activation(0, rows_ref, in_ref, out_ref)
    for copy in copies:
        copy.wait()


def hidden_pre(which, rows, in_near, down_weight=None):
    count, width = rows.shape
    hidden = in_near.shape[2]
    near_spec = pl.BlockSpec(memory_space=pltpu.VMEM)
    out = pltpu.VMEM((hidden, count), jnp.float32)
    settings = dict(
        compiler_params=pltpu.CompilerParams(vmem_limit_bytes=8 << 20),
        cost_estimate=pl.CostEstimate(
            flops=2 * count * hidden * width, bytes_accessed=2 * hidden * width, transcendentals=0
        ),
    )
    if down_weight is None:
        return pl.pallas_call(
            partial(pre_activation, which),
            in_specs=[near_spec] * 2,
            out_specs=near_spec,
            out_shape=out,
            name="hidden_pre",
            **settings,
        )(rows, near(in_near))
    return pl.pallas_call(
        gate_pre_kernel,
        in_specs=[near_spec] * 2 + [pl.BlockSpec(memory_space=pl.ANY)],
        out_specs=[near_spec] * 2,
        out_shape=(out, pltpu.VMEM((hidden // 2, width), down_weight.dtype)),
        scratch_shapes=[pltpu.SemaphoreType.DMA((4,))],
        name="gate_pre",
        **settings,
    )(rows, near(in_near), far(down_weight))


def block_of(size, wanted):
    return wanted if size % wanted == 0 else size


def input_grads(rows, in_ref, first, kept_ref, away_ref, block):
    half = kept_ref.shape[0]
    for start in range(0, kept_ref.shape[1], block):
        part, columns = slice(start, start + block), slice(first + start, first + start + block)
        total = jnp.dot(rows[0], in_ref[0, 0, :, columns], preferred_element_type=jnp.float32)
        total += jnp.dot(rows[1], in_ref[0, 1, :, columns], preferred_element_type=jnp.float32)
        kept_ref[:, part] = total[:half]
        away_ref[:, part] = total[half:].astype(jnp.bfloat16)


def hidden_back_kernel(
    block,
    rows_ref,
    gate_pre_ref,
    up_pre_ref,
    in_ref,
    down_ref,
    other_ref,
    gate_ref,
    up_ref,
    gate_rows_ref,
    up_rows_ref,
    kept_ref,
    away_ref,
):
    size = down_ref.shape[0]
    rows = rows_ref[...]
    scale, cubic = math.sqrt(2 / math.pi), 0.044715
    for number, weight_ref in enumerate((down_ref, other_ref)):
        part = slice(number * size, (number + 1) * size)
        grad = lax.dot_general(
            weight_ref[...], rows, contract_last, preferred_element_type=jnp.float32
        )
        value, up = gate_pre_ref[part], up_pre_ref[part]
        square = value * value
        bend = jnp.tanh(scale * (value + cubic * (square * value)))
        cdf = 0.5 * (1.0 + bend)
        slope = cdf + (0.5 * scale) * value * (1.0 - bend * bend) * (1.0 + 3 * cubic * square)
        gate_ref[part] = (grad * up * slope).astype(jnp.bfloat16)
        up_ref[part] = (grad * (value * cdf)).astype(jnp.bfloat16)
    gate_rows_ref[...] = gate_ref[...].T
    up_rows_ref[...] = up_ref[...].T
    input_grads((gate_rows_ref[...], up_rows_ref[...]), in_ref, 0, kept_ref, away_ref, block)


def rest_back_kernel(block, gate_rows_ref, up_rows_ref, in_ref, kept_ref, away_ref):
    first = in_ref.shape[3] - kept_ref.shape[1]
    input_grads((gate_rows_ref[...], up_rows_ref[...]), in_ref, first, kept_ref, away_ref, block)


def hidden_back(rows, gate_pre, up_pre, in_near, downs):
    count, width = rows.shape
    hidden = in_near.shape[2]
    near_spec = pl.BlockSpec(memory_space=pltpu.VMEM)
    return pl.pallas_call(
        partial(hidden_back_kernel, width // 2),
        in_specs=[near_spec] * 6,
        out_specs=[near_spec] * 6,
        out_shape=(
            pltpu.VMEM((hidden, count), jnp.bfloat16),
            pltpu.VMEM((hidden, count), jnp.bfloat16),
            pltpu.VMEM((count, hidden), jnp.bfloat16),
            pltpu.VMEM((count, hidden), jnp.bfloat16),
            pltpu.VMEM((count // 2, width // 2), jnp.float32),
            pltpu.VMEM((count // 2, width // 2), jnp.bfloat16),
        ),
        compiler_params=pltpu.CompilerParams(vmem_limit_bytes=12 << 20),
        cost_estimate=pl.CostEstimate(
            flops=4 * count * hidden * width,
            bytes_accessed=4 * hidden * width,
            transcendentals=count * hidden,
        ),
        name="hidden_back",
    )(rows, near(gate_pre), near(up_pre), near(in_near), *map(near, downs))


def rest_back(gate_rows, up_rows, in_near):
    count, hidden = gate_rows.shape
    width = in_near.shape[3]
    near_spec = pl.BlockSpec(memory_space=pltpu.VMEM)
    return pl.pallas_call(
        partial(rest_back_kernel, width // 2),
        in_specs=[near_spec] * 3,
        out_specs=[near_spec] * 2,
        out_shape=(
            pltpu.VMEM((count // 2, width // 2), jnp.float32),
            pltpu.VMEM((count // 2, width // 2), jnp.bfloat16),
        ),
        compiler_params=pltpu.CompilerParams(vmem_limit_bytes=12 << 20),
        cost_estimate=pl.CostEstimate(
            flops=2 * count * hidden * width, bytes_accessed=2 * hidden * width, transcendentals=0
        ),
        name="rest_back",
    )(near(gate_rows), near(up_rows), near(in_near))


def pack_kernel(rows_ref, own_ref, odd_ref, even_ref):
    own = lax.axis_index("expert")
    width = own_ref.shape[1]
    for step in range(rows_ref.shape[1] // width):
        block = pl.ds(pl.multiple_of((own ^ step) * width, width), width)
        target = own_ref if step == 0 else (odd_ref if step % 2 else even_ref).at[(step - 1) // 2]
        target[...] = rows_ref[:, block]


def pack(rows, experts):
    capacity, width = rows.shape[0], rows.shape[1] // experts
    near_spec = pl.BlockSpec(memory_space=pltpu.VMEM)
    return pl.pallas_call(
        pack_kernel,
        in_specs=[near_spec],
        out_specs=[near_spec] * 3,
        out_shape=(
            pltpu.VMEM((capacity, width), rows.dtype),
            pltpu.VMEM((experts // 2, capacity, width), rows.dtype),
            pltpu.VMEM((experts // 2 - 1, capacity, width), rows.dtype),
        ),
        compiler_params=pltpu.CompilerParams(vmem_limit_bytes=4 << 20),
        cost_estimate=pl.CostEstimate(
            flops=0, bytes_accessed=4 * rows.size, transcendentals=0
        ),
        name="pack",
    )(near(rows))


def across(value, distance):
    size = lax.axis_size("expert")
    return lax.ppermute(value, "expert", [(i, i ^ distance) for i in range(size)])


def half_kernel(grad_ref, rows_ref, *refs):
    refs[-1][0, 0] = jnp.dot(
        grad_ref[...], rows_ref[...], preferred_element_type=jnp.float32
    ).astype(jnp.bfloat16)


def half_weight_grad(which, grad, rows, partly=None):
    hidden, count = grad.shape
    width = rows.shape[1]
    block = block_of(hidden, 640)
    given = [] if partly is None else [partly]
    return pl.pallas_call(
        half_kernel,
        grid=(hidden // block,),
        in_specs=[
            pl.BlockSpec((block, count), lambda j: (j, 0)),
            pl.BlockSpec((count, width), lambda j: (0, 0)),
        ]
        + [pl.BlockSpec(memory_space=pl.ANY)] * len(given),
        out_specs=pl.BlockSpec((1, 1, block, width), lambda j: (0, which, j, 0)),
        out_shape=jax.ShapeDtypeStruct((1, 2, hidden, width), jnp.bfloat16),
        input_output_aliases={2: 0} if given else {},
        compiler_params=pltpu.CompilerParams(vmem_limit_bytes=20 << 20),
        cost_estimate=pl.CostEstimate(
            flops=2 * count * hidden * width, bytes_accessed=2 * hidden * width, transcendentals=0
        ),
        name="weight_grad_half",
    )(grad, rows, *given)


def aligned_device(
    tokens, out_grad, expert_out, router_probs, expert_index, in_weight, down_weight, router_weight
):
    token_count, width = tokens.shape
    experts = router_probs.shape[1]
    capacity = (5 * token_count + 4 * experts - 1) // (4 * experts)
    groups = lax.axis_size("dp")
    full_width = experts * width
    probs = router_probs.T
    route = expert_index.reshape(1, token_count)
    send, mask, first_down = prelude(
        capacity, down_weight, route, probs, tokens, out_grad, expert_out
    )
    got = lax.all_to_all(send, "expert", split_axis=0, concat_axis=0, tiled=True)
    in_near = fetch(in_weight, got)

    def as_rows(value):
        return value.transpose(1, 0, 2).reshape(value.shape[1], full_width)

    row_tokens, all_grads = as_rows(got[:, :capacity]), as_rows(got[:, capacity:])
    first, last = distances()[:-1], distances()[-1:]
    row_tokens = gather_groups(row_tokens, first)
    all_grads = gather_groups(all_grads, first)
    row_tokens = gather_groups(row_tokens, last)
    all_grads = gather_groups(all_grads, last).reshape(groups, capacity + 8, full_width)
    gate_pre, second_down = hidden_pre(0, row_tokens, in_near, down_weight)
    up_pre = hidden_pre(1, row_tokens, in_near)
    row_grads = all_grads[:, :capacity].reshape(groups * capacity, full_width)
    gate_dot = jnp.sum(got[:, 2 * capacity : 2 * capacity + 3].astype(jnp.float32), axis=(0, 1))
    counts = jnp.sum(all_grads[:, capacity + 3, :experts].astype(jnp.float32), axis=0)

    gate_grad, up_grad, gate_rows, up_rows, kept, away = hidden_back(
        row_grads, gate_pre, up_pre, in_near, (first_down, second_down)
    )
    more_kept, more_away = rest_back(gate_rows, up_rows, in_near)
    summed = kept + swap(away, 1).astype(jnp.float32)
    more = more_kept + swap(more_away, 1).astype(jnp.float32)
    summed = reduce_groups(summed, 2).astype(jnp.bfloat16)
    more = reduce_groups(more, 2).astype(jnp.bfloat16)
    going = jnp.concatenate([summed, more], axis=1)
    own, odd, even = pack(going, experts)
    neighbours = across(odd, 1)
    returned = [jnp.stack([own, neighbours[0]])]
    for step in range(1, experts // 2):
        returned.append(across(jnp.stack([even[step - 1], neighbours[step]]), 2 * step))
    returned = jnp.concatenate(returned, axis=0)
    weight_grad = half_weight_grad(0, gate_grad, row_tokens)
    weight_grad = half_weight_grad(1, up_grad, row_tokens, weight_grad)

    chosen = (lax.broadcasted_iota(jnp.int32, (experts, token_count), 0) == route).astype(jnp.float32)
    prob_grad = chosen * gate_dot[None, :] + aux_coef * experts * counts[:, None] / (
        token_count * groups
    )
    logit_grad = probs * (prob_grad - jnp.sum(probs * prob_grad, axis=0, keepdims=True))
    logit_grad = logit_grad.astype(jnp.bfloat16)
    router_grad = jnp.dot(logit_grad, tokens, preferred_element_type=jnp.float32)
    for distance in distances():
        router_grad = router_grad + swap(router_grad, distance)
    router_term = lax.dot_general(
        logit_grad, router_weight, (((0,), (1,)), ((), ())), preferred_element_type=jnp.float32
    )
    combined = lax.dot_general(
        mask,
        returned.reshape(experts * capacity, width),
        contract_first,
        preferred_element_type=jnp.float32,
    )
    token_grad = (combined + router_term).astype(jnp.bfloat16)
    return (token_grad, weight_grad, router_grad.T)


def per_device(tokens, out_grad, expert_out, router_probs, *rest):
    token_count, width = tokens.shape
    experts = router_probs.shape[1]
    capacity = (5 * token_count + 4 * experts - 1) // (4 * experts)
    aligned = token_count == width and width % 128 == 0 and capacity % 8 == 0
    aligned = aligned and experts % 8 == 0 and experts & (experts - 1) == 0
    if not aligned:
        return general_device(tokens, out_grad, expert_out, router_probs, *rest)
    return aligned_device(tokens, out_grad, expert_out, router_probs, *rest)


def solution(mesh):
    in_specs = (
        P("dp", "expert"),
        P("dp", "expert"),
        P("dp", "expert"),
        P("dp", None),
        P("dp", None),
        P("expert", None, "dp", None),
        P("expert", "dp", None),
        P("expert", None),
    )
    out_specs = (P("dp", "expert"), P("expert", None, "dp", None), P("expert", None))
    return jax.shard_map(
        per_device, mesh=mesh, in_specs=in_specs, out_specs=out_specs, check_vma=False
    )
```

```python
import math
from functools import partial

import jax
import jax.numpy as jnp
from jax import lax
from jax.experimental import pallas as pl
from jax.experimental.pallas import tpu as pltpu
from jax.sharding import PartitionSpec as P


aux_coef = 0.2
contract_last = (((1,), (1,)), ((), ()))
contract_first = (((0,), (0,)), ((), ()))


def slot_numbers(routes):
    width = routes.shape[1]
    same_expert = routes[:, :, None] == routes[:, None, :]
    position = jnp.arange(width, dtype=jnp.int32)
    before = position[None, :] < position[:, None]
    return jnp.sum((same_expert & before[None]).astype(jnp.int32), axis=2)


def one_hot(routes, slot_ids, experts, capacity):
    expert_hit = routes[..., None] == jnp.arange(experts, dtype=jnp.int32)
    slot_hit = slot_ids[..., None] == jnp.arange(capacity, dtype=jnp.int32)
    return (expert_hit[..., :, None] & slot_hit[..., None, :]).astype(jnp.float32)


def gelu_parts(pre_act, upstream):
    gelu_value, pullback = jax.vjp(partial(jax.nn.gelu, approximate=True), pre_act)
    return (gelu_value, pullback(upstream)[0])


def swap(value, distance):
    size = lax.axis_size("dp")
    return lax.ppermute(value, "dp", [(i, i ^ distance) for i in range(size)])


def distances():
    found, distance = [], lax.axis_size("dp") // 2
    while distance:
        found.append(distance)
        distance //= 2
    return found


def gather_groups(block, given=()):
    for distance in given or distances():
        block = jnp.concatenate([block, swap(block, distance)], axis=0)
    return block


def reduce_groups(total, first=1):
    order = [distance for distance in distances()[::-1] if distance >= first]
    for distance in order:
        half = total.shape[0] // 2
        away = swap(total[half:].astype(jnp.bfloat16), distance)
        total = total[:half] + away.astype(jnp.float32)
    return total


def weight_grad_kernel(gate_ref, up_ref, rows_ref, out_ref):
    rows = rows_ref[...]
    out_ref[0, 0] = lax.dot_general(
        gate_ref[...], rows, contract_first, preferred_element_type=jnp.float32
    ).astype(jnp.bfloat16)
    out_ref[0, 1] = lax.dot_general(
        up_ref[...], rows, contract_first, preferred_element_type=jnp.float32
    ).astype(jnp.bfloat16)


def weight_grads(gate_grad, up_grad, rows):
    count, hidden = gate_grad.shape
    width = rows.shape[1]
    block = 256 if hidden % 256 == 0 else hidden
    return pl.pallas_call(
        weight_grad_kernel,
        grid=(hidden // block,),
        in_specs=[
            pl.BlockSpec((count, block), lambda j: (0, j)),
            pl.BlockSpec((count, block), lambda j: (0, j)),
            pl.BlockSpec((count, width), lambda j: (0, 0)),
        ],
        out_specs=pl.BlockSpec((1, 2, block, width), lambda j: (0, 0, j, 0)),
        out_shape=jax.ShapeDtypeStruct((1, 2, hidden, width), jnp.bfloat16),
        cost_estimate=pl.CostEstimate(
            flops=4 * count * hidden * width,
            bytes_accessed=4 * hidden * width,
            transcendentals=0,
        ),
        name="weight_grads",
    )(gate_grad, up_grad, rows)


def split_float(value):
    high = lax.reduce_precision(value, 8, 7)
    middle = lax.reduce_precision(value - high, 8, 7)
    return jnp.stack([high, middle, value - high - middle]).astype(jnp.bfloat16)


def general_device(
    tokens, out_grad, expert_out, router_probs, expert_index, in_weight, down_weight, router_weight
):
    token_count, feature_width = tokens.shape
    experts = router_probs.shape[1]
    capacity = (5 * token_count + 4 * experts - 1) // (4 * experts)
    groups = lax.axis_size("dp")
    routes = expert_index[:, 0]
    slot_ids = slot_numbers(routes[None, :])[0]
    dispatch_mask = one_hot(routes, slot_ids, experts, capacity)
    mask_half = dispatch_mask.astype(jnp.bfloat16)
    chosen = jnp.sum(dispatch_mask, axis=2)

    def exchange(value):
        return lax.all_to_all(value, "expert", split_axis=0, concat_axis=2, tiled=True)[0]

    send_tokens = jnp.einsum(
        "tec,tf->ecf", mask_half, tokens, preferred_element_type=jnp.float32
    ).astype(jnp.bfloat16)
    got_tokens = exchange(send_tokens)

    gate = jnp.sum(router_probs * chosen, axis=1)
    gated_dy = (gate[:, None] * out_grad.astype(jnp.float32)).astype(jnp.bfloat16)
    send_grads = jnp.einsum(
        "tec,tf->ecf", mask_half, gated_dy, preferred_element_type=jnp.float32
    ).astype(jnp.bfloat16)
    partial_dot = jnp.sum(out_grad.astype(jnp.float32) * expert_out.astype(jnp.float32), axis=1)
    dot_rows = token_count // feature_width
    pieces = split_float(partial_dot).reshape(3 * dot_rows, feature_width)
    local_counts = jnp.sum(chosen, axis=0)
    count_row = jnp.pad(local_counts.astype(jnp.bfloat16)[None], ((0, 0), (0, feature_width - experts)))
    side = jnp.concatenate([pieces, count_row], axis=0)
    side_rows = -(-(capacity + side.shape[0]) // 8) * 8 - capacity
    side = jnp.pad(side, ((0, side_rows - side.shape[0]), (0, 0)))
    send_grads = jnp.concatenate(
        [send_grads, jnp.broadcast_to(side[None], (experts, side_rows, feature_width))], axis=1
    )
    got_grads = exchange(send_grads)

    row_tokens = gather_groups(got_tokens)
    all_grads = gather_groups(got_grads).reshape(groups, capacity + side_rows, -1)
    row_grads = all_grads[:, :capacity].reshape(groups * capacity, -1)
    own_side = got_grads[capacity:].astype(jnp.float32)
    gate_dot = jnp.sum(
        own_side[: 3 * dot_rows].reshape(3, dot_rows, experts, feature_width), axis=(0, 2)
    ).reshape(token_count)
    counts = jnp.sum(all_grads[:, capacity + 3 * dot_rows, :experts].astype(jnp.float32), axis=0)

    gate_weight = in_weight[0, 0]
    up_weight = in_weight[0, 1]
    gate_pre = lax.dot_general(
        row_tokens, gate_weight, contract_last, preferred_element_type=jnp.float32
    )
    up_pre = lax.dot_general(
        row_tokens, up_weight, contract_last, preferred_element_type=jnp.float32
    )
    hidden_grad = lax.dot_general(
        row_grads, down_weight[0], contract_last, preferred_element_type=jnp.float32
    )
    gate_act, gate_back = gelu_parts(gate_pre, hidden_grad * up_pre)
    gate_grad = gate_back.astype(jnp.bfloat16)
    up_grad = (hidden_grad * gate_act).astype(jnp.bfloat16)
    term = jnp.dot(gate_grad, gate_weight, preferred_element_type=jnp.float32)
    term = term + jnp.dot(up_grad, up_weight, preferred_element_type=jnp.float32)
    summed = reduce_groups(term)
    going = summed.astype(jnp.bfloat16).reshape(capacity, experts, feature_width)
    returned = lax.all_to_all(
        going.transpose(1, 0, 2), "expert", split_axis=0, concat_axis=0, tiled=True
    )
    weight_grad = weight_grads(gate_grad, up_grad, row_tokens)

    prob_grad = chosen * gate_dot[:, None] + aux_coef * experts * counts[None, :] / (
        token_count * groups
    )
    logit_grad = router_probs * (
        prob_grad - jnp.sum(router_probs * prob_grad, axis=1, keepdims=True)
    )
    logit_grad = logit_grad.astype(jnp.bfloat16)
    router_grad = lax.dot_general(
        tokens, logit_grad, contract_first, preferred_element_type=jnp.float32
    )
    for distance in distances():
        router_grad = router_grad + swap(router_grad, distance)
    router_term = lax.dot_general(
        logit_grad, router_weight, contract_last, preferred_element_type=jnp.float32
    )
    combined = jnp.einsum(
        "tec,ecf->tf", mask_half, returned, preferred_element_type=jnp.float32
    )
    token_grad = (combined + router_term).astype(jnp.bfloat16)
    return (token_grad, weight_grad, router_grad)


def prelude_kernel(
    capacity,
    route_hbm,
    probs_hbm,
    tokens_hbm,
    grads_hbm,
    expert_out_hbm,
    down_hbm,
    send_ref,
    place_ref,
    down_ref,
    route_ref,
    probs_ref,
    tokens_ref,
    grads_ref,
    expert_out_ref,
    sems,
):
    sources = (route_hbm, probs_hbm, tokens_hbm, grads_hbm, expert_out_hbm)
    targets = (route_ref, probs_ref, tokens_ref, grads_ref, expert_out_ref)
    copies = [
        pltpu.make_async_copy(source, target, sems.at[number])
        for number, (source, target) in enumerate(zip(sources, targets))
    ]
    pieces = sems.shape[0] - len(copies)
    half = down_ref.shape[0]
    size = half // pieces
    for piece in range(pieces):
        copies.append(
            pltpu.make_async_copy(
                down_hbm.at[0, pl.ds(half + piece * size, size)],
                down_ref.at[pl.ds(piece * size, size)],
                sems.at[len(copies)],
            )
        )
    for copy in copies:
        copy.start()
    experts, count = probs_ref.shape
    width = tokens_ref.shape[1]
    half, full = jnp.bfloat16, jnp.float32
    iota = lambda shape, axis: lax.broadcasted_iota(jnp.int32, shape, axis)
    dot = partial(lax.dot_general, preferred_element_type=full)
    plain = (((1,), (0,)), ((), ()))
    square = (count, count)
    earlier = (iota(square, 0) < iota(square, 1)).astype(full).astype(half)
    copies[0].wait()
    route = route_ref[...]
    hit = iota((experts, count), 0) == route
    before = dot(hit.astype(full).astype(half), earlier, plain)
    slot = jnp.sum(jnp.where(hit, before, 0.0), axis=0, keepdims=True)
    place = iota((experts * capacity, count), 0) == route * capacity + slot.astype(jnp.int32)
    mask = place.astype(full).astype(half)
    place_ref[...] = mask
    copies[1].wait()
    gate = jnp.sum(jnp.where(hit, probs_ref[...], 0.0), axis=0, keepdims=True)
    row_gate = jnp.sum(jnp.where(place, gate, 0.0), axis=1, keepdims=True)
    copies[2].wait()
    rows_x = dot(mask, tokens_ref[...], plain)
    copies[3].wait()
    rows_dy = dot(mask, grads_ref[...], plain) * row_gate
    copies[4].wait()
    product = grads_ref[...].astype(full) * expert_out_ref[...].astype(full)
    high = product.astype(half)
    low = (product - high.astype(full)).astype(half)
    ones = jnp.ones((8, width), half)
    part = dot(ones, high, contract_last) + dot(ones, low, contract_last)
    first = part.astype(half).astype(full)
    second = (part - first).astype(half).astype(full)
    third = part - first - second
    listed = (iota((width, count), 0) == route).astype(full).astype(half)
    counts = dot(jnp.ones((8, count), half), listed, contract_last)
    line = iota((8, width), 0)
    side = jnp.where(line == 3, counts, 0.0)
    for number, piece in enumerate((first, second, third)):
        side = jnp.where(line == number, piece, side)
    side = side.astype(half)
    for expert in range(experts):
        rows = slice(expert * capacity, (expert + 1) * capacity)
        send_ref[expert, :capacity] = rows_x[rows].astype(half)
        send_ref[expert, capacity : 2 * capacity] = rows_dy[rows].astype(half)
        send_ref[expert, 2 * capacity :] = side
    for copy in copies[5:]:
        copy.wait()


def far(value):
    return pltpu.with_memory_space_constraint(value, pltpu.HBM)


def near(value):
    return pltpu.with_memory_space_constraint(value, pltpu.VMEM)


def prelude(capacity, down_weight, *args):
    experts, count = args[1].shape
    width = args[2].shape[1]
    return pl.pallas_call(
        partial(prelude_kernel, capacity),
        in_specs=[pl.BlockSpec(memory_space=pl.ANY)] * (len(args) + 1),
        out_specs=[pl.BlockSpec(memory_space=pltpu.VMEM)] * 3,
        out_shape=(
            jax.ShapeDtypeStruct((experts, 2 * capacity + 8, width), jnp.bfloat16),
            jax.ShapeDtypeStruct((experts * capacity, count), jnp.bfloat16),
            pltpu.VMEM((down_weight.shape[1] // 2, down_weight.shape[2]), down_weight.dtype),
        ),
        scratch_shapes=[pltpu.VMEM(value.shape, value.dtype) for value in args]
        + [pltpu.SemaphoreType.DMA((len(args) + 2,))],
        compiler_params=pltpu.CompilerParams(vmem_limit_bytes=8 << 20),
        name="prelude",
    )(*[far(value) for value in args], far(down_weight))


def fetch_kernel(pieces, source_ref, after_ref, target_ref, sems):
    planes, hidden = source_ref.shape[1:3]
    size = hidden // pieces
    copies = []
    for plane in range(planes):
        for piece in range(pieces):
            where = (0, plane, pl.ds(piece * size, size))
            copies.append(
                pltpu.make_async_copy(
                    source_ref.at[where], target_ref.at[where], sems.at[len(copies)]
                )
            )
    for copy in copies:
        copy.start()
    for copy in copies:
        copy.wait()


def fetch(weight, after):
    pieces = 4
    return pl.pallas_call(
        partial(fetch_kernel, pieces),
        in_specs=[pl.BlockSpec(memory_space=pl.ANY)] * 2,
        out_specs=pl.BlockSpec(memory_space=pltpu.VMEM),
        out_shape=pltpu.VMEM(weight.shape, weight.dtype),
        scratch_shapes=[pltpu.SemaphoreType.DMA((weight.shape[1] * pieces,))],
        compiler_params=pltpu.CompilerParams(vmem_limit_bytes=1 << 20),
        cost_estimate=pl.CostEstimate(
            flops=0, bytes_accessed=2 * weight.size, transcendentals=0
        ),
        name="fetch",
    )(far(weight), after)


def pre_activation(which, rows_ref, in_ref, out_ref):
    rows = rows_ref[...]
    size = in_ref.shape[2] // 2
    for start in (0, size):
        part = slice(start, start + size)
        out_ref[part] = lax.dot_general(
            in_ref[0, which, part], rows, contract_last, preferred_element_type=jnp.float32
        )


def gate_pre_kernel(rows_ref, in_ref, down_hbm, out_ref, down_ref, sems):
    pieces = sems.shape[0]
    size = down_ref.shape[0] // pieces
    copies = [
        pltpu.make_async_copy(
            down_hbm.at[0, pl.ds(piece * size, size)],
            down_ref.at[pl.ds(piece * size, size)],
            sems.at[piece],
        )
        for piece in range(pieces)
    ]
    for copy in copies:
        copy.start()
    pre_activation(0, rows_ref, in_ref, out_ref)
    for copy in copies:
        copy.wait()


def hidden_pre(which, rows, in_near, down_weight=None):
    count, width = rows.shape
    hidden = in_near.shape[2]
    near_spec = pl.BlockSpec(memory_space=pltpu.VMEM)
    out = pltpu.VMEM((hidden, count), jnp.float32)
    settings = dict(
        compiler_params=pltpu.CompilerParams(vmem_limit_bytes=8 << 20),
        cost_estimate=pl.CostEstimate(
            flops=2 * count * hidden * width, bytes_accessed=2 * hidden * width, transcendentals=0
        ),
    )
    if down_weight is None:
        return pl.pallas_call(
            partial(pre_activation, which),
            in_specs=[near_spec] * 2,
            out_specs=near_spec,
            out_shape=out,
            name="hidden_pre",
            **settings,
        )(rows, near(in_near))
    return pl.pallas_call(
        gate_pre_kernel,
        in_specs=[near_spec] * 2 + [pl.BlockSpec(memory_space=pl.ANY)],
        out_specs=[near_spec] * 2,
        out_shape=(out, pltpu.VMEM((hidden // 2, width), down_weight.dtype)),
        scratch_shapes=[pltpu.SemaphoreType.DMA((4,))],
        name="gate_pre",
        **settings,
    )(rows, near(in_near), far(down_weight))


def block_of(size, wanted):
    return wanted if size % wanted == 0 else size


def input_grads(rows, in_ref, first, kept_ref, away_ref, block):
    half = kept_ref.shape[0]
    for start in range(0, kept_ref.shape[1], block):
        part, columns = slice(start, start + block), slice(first + start, first + start + block)
        total = jnp.dot(rows[0], in_ref[0, 0, :, columns], preferred_element_type=jnp.float32)
        total += jnp.dot(rows[1], in_ref[0, 1, :, columns], preferred_element_type=jnp.float32)
        kept_ref[:, part] = total[:half]
        away_ref[:, part] = total[half:].astype(jnp.bfloat16)


def hidden_back_kernel(
    block,
    rows_ref,
    gate_pre_ref,
    up_pre_ref,
    in_ref,
    down_ref,
    other_ref,
    gate_ref,
    up_ref,
    gate_rows_ref,
    up_rows_ref,
    kept_ref,
    away_ref,
):
    size = down_ref.shape[0]
    rows = rows_ref[...]
    scale, cubic = math.sqrt(2 / math.pi), 0.044715
    for number, weight_ref in enumerate((down_ref, other_ref)):
        part = slice(number * size, (number + 1) * size)
        grad = lax.dot_general(
            weight_ref[...], rows, contract_last, preferred_element_type=jnp.float32
        )
        value, up = gate_pre_ref[part], up_pre_ref[part]
        square = value * value
        bend = jnp.tanh(scale * (value + cubic * (square * value)))
        cdf = 0.5 * (1.0 + bend)
        slope = cdf + (0.5 * scale) * value * (1.0 - bend * bend) * (1.0 + 3 * cubic * square)
        gate_ref[part] = (grad * up * slope).astype(jnp.bfloat16)
        up_ref[part] = (grad * (value * cdf)).astype(jnp.bfloat16)
    gate_rows_ref[...] = gate_ref[...].T
    up_rows_ref[...] = up_ref[...].T
    input_grads((gate_rows_ref[...], up_rows_ref[...]), in_ref, 0, kept_ref, away_ref, block)


def rest_back_kernel(block, gate_rows_ref, up_rows_ref, in_ref, kept_ref, away_ref):
    first = in_ref.shape[3] - kept_ref.shape[1]
    input_grads((gate_rows_ref[...], up_rows_ref[...]), in_ref, first, kept_ref, away_ref, block)


def hidden_back(rows, gate_pre, up_pre, in_near, downs):
    count, width = rows.shape
    hidden = in_near.shape[2]
    near_spec = pl.BlockSpec(memory_space=pltpu.VMEM)
    return pl.pallas_call(
        partial(hidden_back_kernel, width // 2),
        in_specs=[near_spec] * 6,
        out_specs=[near_spec] * 6,
        out_shape=(
            pltpu.VMEM((hidden, count), jnp.bfloat16),
            pltpu.VMEM((hidden, count), jnp.bfloat16),
            pltpu.VMEM((count, hidden), jnp.bfloat16),
            pltpu.VMEM((count, hidden), jnp.bfloat16),
            pltpu.VMEM((count // 2, width // 2), jnp.float32),
            pltpu.VMEM((count // 2, width // 2), jnp.bfloat16),
        ),
        compiler_params=pltpu.CompilerParams(vmem_limit_bytes=12 << 20),
        cost_estimate=pl.CostEstimate(
            flops=4 * count * hidden * width,
            bytes_accessed=4 * hidden * width,
            transcendentals=count * hidden,
        ),
        name="hidden_back",
    )(rows, near(gate_pre), near(up_pre), near(in_near), *map(near, downs))


def rest_back(gate_rows, up_rows, in_near):
    count, hidden = gate_rows.shape
    width = in_near.shape[3]
    near_spec = pl.BlockSpec(memory_space=pltpu.VMEM)
    return pl.pallas_call(
        partial(rest_back_kernel, width // 2),
        in_specs=[near_spec] * 3,
        out_specs=[near_spec] * 2,
        out_shape=(
            pltpu.VMEM((count // 2, width // 2), jnp.float32),
            pltpu.VMEM((count // 2, width // 2), jnp.bfloat16),
        ),
        compiler_params=pltpu.CompilerParams(vmem_limit_bytes=12 << 20),
        cost_estimate=pl.CostEstimate(
            flops=2 * count * hidden * width, bytes_accessed=2 * hidden * width, transcendentals=0
        ),
        name="rest_back",
    )(near(gate_rows), near(up_rows), near(in_near))


def half_kernel(grad_ref, rows_ref, *refs):
    refs[-1][0, 0] = jnp.dot(
        grad_ref[...], rows_ref[...], preferred_element_type=jnp.float32
    ).astype(jnp.bfloat16)


def half_weight_grad(which, grad, rows, partly=None):
    hidden, count = grad.shape
    width = rows.shape[1]
    block = block_of(hidden, 640)
    given = [] if partly is None else [partly]
    return pl.pallas_call(
        half_kernel,
        grid=(hidden // block,),
        in_specs=[
            pl.BlockSpec((block, count), lambda j: (j, 0)),
            pl.BlockSpec((count, width), lambda j: (0, 0)),
        ]
        + [pl.BlockSpec(memory_space=pl.ANY)] * len(given),
        out_specs=pl.BlockSpec((1, 1, block, width), lambda j: (0, which, j, 0)),
        out_shape=jax.ShapeDtypeStruct((1, 2, hidden, width), jnp.bfloat16),
        input_output_aliases={2: 0} if given else {},
        compiler_params=pltpu.CompilerParams(vmem_limit_bytes=20 << 20),
        cost_estimate=pl.CostEstimate(
            flops=2 * count * hidden * width, bytes_accessed=2 * hidden * width, transcendentals=0
        ),
        name="weight_grad_half",
    )(grad, rows, *given)


def aligned_device(
    tokens, out_grad, expert_out, router_probs, expert_index, in_weight, down_weight, router_weight
):
    token_count, width = tokens.shape
    experts = router_probs.shape[1]
    capacity = (5 * token_count + 4 * experts - 1) // (4 * experts)
    groups = lax.axis_size("dp")
    full_width = experts * width
    probs = router_probs.T
    route = expert_index.reshape(1, token_count)
    send, mask, second_down = prelude(
        capacity, down_weight, route, probs, tokens, out_grad, expert_out
    )
    got = lax.all_to_all(send, "expert", split_axis=0, concat_axis=0, tiled=True)
    in_near = fetch(in_weight, got)

    def as_rows(value):
        return value.transpose(1, 0, 2).reshape(value.shape[1], full_width)

    row_tokens, all_grads = as_rows(got[:, :capacity]), as_rows(got[:, capacity:])
    first, last = distances()[:-1], distances()[-1:]
    row_tokens = gather_groups(row_tokens, first)
    all_grads = gather_groups(all_grads, first)
    row_tokens = gather_groups(row_tokens, last)
    all_grads = gather_groups(all_grads, last).reshape(groups, capacity + 8, full_width)
    gate_pre, first_down = hidden_pre(0, row_tokens, in_near, down_weight)
    up_pre = hidden_pre(1, row_tokens, in_near)
    row_grads = all_grads[:, :capacity].reshape(groups * capacity, full_width)
    gate_dot = jnp.sum(got[:, 2 * capacity : 2 * capacity + 3].astype(jnp.float32), axis=(0, 1))
    counts = jnp.sum(all_grads[:, capacity + 3, :experts].astype(jnp.float32), axis=0)

    gate_grad, up_grad, gate_rows, up_rows, kept, away = hidden_back(
        row_grads, gate_pre, up_pre, in_near, (first_down, second_down)
    )
    more_kept, more_away = rest_back(gate_rows, up_rows, in_near)
    summed = kept + swap(away, 1).astype(jnp.float32)
    more = more_kept + swap(more_away, 1).astype(jnp.float32)
    going = reduce_groups(jnp.concatenate([summed, more], axis=1), 2).astype(jnp.bfloat16)
    going = going.reshape(capacity, experts, width).transpose(1, 0, 2)
    returned = lax.all_to_all(going, "expert", split_axis=0, concat_axis=0, tiled=True)
    weight_grad = half_weight_grad(0, gate_grad, row_tokens)
    weight_grad = half_weight_grad(1, up_grad, row_tokens, weight_grad)

    chosen = (lax.broadcasted_iota(jnp.int32, (experts, token_count), 0) == route).astype(jnp.float32)
    prob_grad = chosen * gate_dot[None, :] + aux_coef * experts * counts[:, None] / (
        token_count * groups
    )
    logit_grad = probs * (prob_grad - jnp.sum(probs * prob_grad, axis=0, keepdims=True))
    logit_grad = logit_grad.astype(jnp.bfloat16)
    router_grad = jnp.dot(logit_grad, tokens, preferred_element_type=jnp.float32)
    for distance in distances()[::-1]:
        router_grad = router_grad + swap(router_grad, distance)
    router_term = lax.dot_general(
        logit_grad, router_weight, (((0,), (1,)), ((), ())), preferred_element_type=jnp.float32
    )
    combined = lax.dot_general(
        mask,
        returned.reshape(experts * capacity, width),
        contract_first,
        preferred_element_type=jnp.float32,
    )
    token_grad = (combined + router_term).astype(jnp.bfloat16)
    return (token_grad, weight_grad, router_grad.T)


def per_device(tokens, out_grad, expert_out, router_probs, *rest):
    token_count, width = tokens.shape
    experts = router_probs.shape[1]
    capacity = (5 * token_count + 4 * experts - 1) // (4 * experts)
    aligned = token_count == width and width % 128 == 0 and capacity % 8 == 0 and experts % 8 == 0
    if not aligned:
        return general_device(tokens, out_grad, expert_out, router_probs, *rest)
    return aligned_device(tokens, out_grad, expert_out, router_probs, *rest)


def solution(mesh):
    in_specs = (
        P("dp", "expert"),
        P("dp", "expert"),
        P("dp", "expert"),
        P("dp", None),
        P("dp", None),
        P("expert", None, "dp", None),
        P("expert", "dp", None),
        P("expert", None),
    )
    out_specs = (P("dp", "expert"), P("expert", None, "dp", None), P("expert", None))
    return jax.shard_map(
        per_device, mesh=mesh, in_specs=in_specs, out_specs=out_specs, check_vma=False
    )
```

```python
import math
from functools import partial

import jax
import jax.numpy as jnp
from jax import lax
from jax.experimental import pallas as pl
from jax.experimental.pallas import tpu as pltpu
from jax.sharding import PartitionSpec as P


aux_coef = 0.2
contract_last = (((1,), (1,)), ((), ()))
contract_first = (((0,), (0,)), ((), ()))


def slot_numbers(routes):
    width = routes.shape[1]
    same_expert = routes[:, :, None] == routes[:, None, :]
    position = jnp.arange(width, dtype=jnp.int32)
    before = position[None, :] < position[:, None]
    return jnp.sum((same_expert & before[None]).astype(jnp.int32), axis=2)


def one_hot(routes, slot_ids, experts, capacity):
    expert_hit = routes[..., None] == jnp.arange(experts, dtype=jnp.int32)
    slot_hit = slot_ids[..., None] == jnp.arange(capacity, dtype=jnp.int32)
    return (expert_hit[..., :, None] & slot_hit[..., None, :]).astype(jnp.float32)


def gelu_parts(pre_act, upstream):
    gelu_value, pullback = jax.vjp(partial(jax.nn.gelu, approximate=True), pre_act)
    return (gelu_value, pullback(upstream)[0])


def swap(value, distance):
    size = lax.axis_size("dp")
    return lax.ppermute(value, "dp", [(i, i ^ distance) for i in range(size)])


def distances():
    found, distance = [], lax.axis_size("dp") // 2
    while distance:
        found.append(distance)
        distance //= 2
    return found


def gather_groups(block, given=()):
    for distance in given or distances():
        block = jnp.concatenate([block, swap(block, distance)], axis=0)
    return block


def reduce_groups(total, first=1):
    order = [distance for distance in distances()[::-1] if distance >= first]
    for distance in order:
        half = total.shape[0] // 2
        away = swap(total[half:].astype(jnp.bfloat16), distance)
        total = total[:half] + away.astype(jnp.float32)
    return total


def weight_grad_kernel(gate_ref, up_ref, rows_ref, out_ref):
    rows = rows_ref[...]
    out_ref[0, 0] = lax.dot_general(
        gate_ref[...], rows, contract_first, preferred_element_type=jnp.float32
    ).astype(jnp.bfloat16)
    out_ref[0, 1] = lax.dot_general(
        up_ref[...], rows, contract_first, preferred_element_type=jnp.float32
    ).astype(jnp.bfloat16)


def weight_grads(gate_grad, up_grad, rows):
    count, hidden = gate_grad.shape
    width = rows.shape[1]
    block = 256 if hidden % 256 == 0 else hidden
    return pl.pallas_call(
        weight_grad_kernel,
        grid=(hidden // block,),
        in_specs=[
            pl.BlockSpec((count, block), lambda j: (0, j)),
            pl.BlockSpec((count, block), lambda j: (0, j)),
            pl.BlockSpec((count, width), lambda j: (0, 0)),
        ],
        out_specs=pl.BlockSpec((1, 2, block, width), lambda j: (0, 0, j, 0)),
        out_shape=jax.ShapeDtypeStruct((1, 2, hidden, width), jnp.bfloat16),
        cost_estimate=pl.CostEstimate(
            flops=4 * count * hidden * width,
            bytes_accessed=4 * hidden * width,
            transcendentals=0,
        ),
        name="weight_grads",
    )(gate_grad, up_grad, rows)


def split_float(value):
    high = lax.reduce_precision(value, 8, 7)
    middle = lax.reduce_precision(value - high, 8, 7)
    return jnp.stack([high, middle, value - high - middle]).astype(jnp.bfloat16)


def general_device(
    tokens, out_grad, expert_out, router_probs, expert_index, in_weight, down_weight, router_weight
):
    token_count, feature_width = tokens.shape
    experts = router_probs.shape[1]
    capacity = (5 * token_count + 4 * experts - 1) // (4 * experts)
    groups = lax.axis_size("dp")
    routes = expert_index[:, 0]
    slot_ids = slot_numbers(routes[None, :])[0]
    dispatch_mask = one_hot(routes, slot_ids, experts, capacity)
    mask_half = dispatch_mask.astype(jnp.bfloat16)
    chosen = jnp.sum(dispatch_mask, axis=2)

    def exchange(value):
        return lax.all_to_all(value, "expert", split_axis=0, concat_axis=2, tiled=True)[0]

    send_tokens = jnp.einsum(
        "tec,tf->ecf", mask_half, tokens, preferred_element_type=jnp.float32
    ).astype(jnp.bfloat16)
    got_tokens = exchange(send_tokens)

    gate = jnp.sum(router_probs * chosen, axis=1)
    gated_dy = (gate[:, None] * out_grad.astype(jnp.float32)).astype(jnp.bfloat16)
    send_grads = jnp.einsum(
        "tec,tf->ecf", mask_half, gated_dy, preferred_element_type=jnp.float32
    ).astype(jnp.bfloat16)
    partial_dot = jnp.sum(out_grad.astype(jnp.float32) * expert_out.astype(jnp.float32), axis=1)
    dot_rows = token_count // feature_width
    pieces = split_float(partial_dot).reshape(3 * dot_rows, feature_width)
    local_counts = jnp.sum(chosen, axis=0)
    count_row = jnp.pad(local_counts.astype(jnp.bfloat16)[None], ((0, 0), (0, feature_width - experts)))
    side = jnp.concatenate([pieces, count_row], axis=0)
    side_rows = -(-(capacity + side.shape[0]) // 8) * 8 - capacity
    side = jnp.pad(side, ((0, side_rows - side.shape[0]), (0, 0)))
    send_grads = jnp.concatenate(
        [send_grads, jnp.broadcast_to(side[None], (experts, side_rows, feature_width))], axis=1
    )
    got_grads = exchange(send_grads)

    row_tokens = gather_groups(got_tokens)
    all_grads = gather_groups(got_grads).reshape(groups, capacity + side_rows, -1)
    row_grads = all_grads[:, :capacity].reshape(groups * capacity, -1)
    own_side = got_grads[capacity:].astype(jnp.float32)
    gate_dot = jnp.sum(
        own_side[: 3 * dot_rows].reshape(3, dot_rows, experts, feature_width), axis=(0, 2)
    ).reshape(token_count)
    counts = jnp.sum(all_grads[:, capacity + 3 * dot_rows, :experts].astype(jnp.float32), axis=0)

    gate_weight = in_weight[0, 0]
    up_weight = in_weight[0, 1]
    gate_pre = lax.dot_general(
        row_tokens, gate_weight, contract_last, preferred_element_type=jnp.float32
    )
    up_pre = lax.dot_general(
        row_tokens, up_weight, contract_last, preferred_element_type=jnp.float32
    )
    hidden_grad = lax.dot_general(
        row_grads, down_weight[0], contract_last, preferred_element_type=jnp.float32
    )
    gate_act, gate_back = gelu_parts(gate_pre, hidden_grad * up_pre)
    gate_grad = gate_back.astype(jnp.bfloat16)
    up_grad = (hidden_grad * gate_act).astype(jnp.bfloat16)
    term = jnp.dot(gate_grad, gate_weight, preferred_element_type=jnp.float32)
    term = term + jnp.dot(up_grad, up_weight, preferred_element_type=jnp.float32)
    summed = reduce_groups(term)
    going = summed.astype(jnp.bfloat16).reshape(capacity, experts, feature_width)
    returned = lax.all_to_all(
        going.transpose(1, 0, 2), "expert", split_axis=0, concat_axis=0, tiled=True
    )
    weight_grad = weight_grads(gate_grad, up_grad, row_tokens)

    prob_grad = chosen * gate_dot[:, None] + aux_coef * experts * counts[None, :] / (
        token_count * groups
    )
    logit_grad = router_probs * (
        prob_grad - jnp.sum(router_probs * prob_grad, axis=1, keepdims=True)
    )
    logit_grad = logit_grad.astype(jnp.bfloat16)
    router_grad = lax.dot_general(
        tokens, logit_grad, contract_first, preferred_element_type=jnp.float32
    )
    for distance in distances():
        router_grad = router_grad + swap(router_grad, distance)
    router_term = lax.dot_general(
        logit_grad, router_weight, contract_last, preferred_element_type=jnp.float32
    )
    combined = jnp.einsum(
        "tec,ecf->tf", mask_half, returned, preferred_element_type=jnp.float32
    )
    token_grad = (combined + router_term).astype(jnp.bfloat16)
    return (token_grad, weight_grad, router_grad)


def prelude_kernel(
    capacity,
    route_hbm,
    probs_hbm,
    tokens_hbm,
    grads_hbm,
    expert_out_hbm,
    down_hbm,
    send_ref,
    place_ref,
    down_ref,
    route_ref,
    probs_ref,
    tokens_ref,
    grads_ref,
    expert_out_ref,
    sems,
):
    sources = (route_hbm, probs_hbm, tokens_hbm, grads_hbm, expert_out_hbm)
    targets = (route_ref, probs_ref, tokens_ref, grads_ref, expert_out_ref)
    copies = [
        pltpu.make_async_copy(source, target, sems.at[number])
        for number, (source, target) in enumerate(zip(sources, targets))
    ]
    pieces = sems.shape[0] - len(copies)
    half = down_ref.shape[0]
    size = half // pieces
    for piece in range(pieces):
        copies.append(
            pltpu.make_async_copy(
                down_hbm.at[0, pl.ds(half + piece * size, size)],
                down_ref.at[pl.ds(piece * size, size)],
                sems.at[len(copies)],
            )
        )
    for copy in copies:
        copy.start()
    experts, count = probs_ref.shape
    width = tokens_ref.shape[1]
    half, full = jnp.bfloat16, jnp.float32
    iota = lambda shape, axis: lax.broadcasted_iota(jnp.int32, shape, axis)
    dot = partial(lax.dot_general, preferred_element_type=full)
    plain = (((1,), (0,)), ((), ()))
    square = (count, count)
    earlier = (iota(square, 0) < iota(square, 1)).astype(full).astype(half)
    copies[0].wait()
    route = route_ref[...]
    hit = iota((experts, count), 0) == route
    before = dot(hit.astype(full).astype(half), earlier, plain)
    slot = jnp.sum(jnp.where(hit, before, 0.0), axis=0, keepdims=True)
    place = iota((experts * capacity, count), 0) == route * capacity + slot.astype(jnp.int32)
    mask = place.astype(full).astype(half)
    place_ref[...] = mask
    copies[1].wait()
    gate = jnp.sum(jnp.where(hit, probs_ref[...], 0.0), axis=0, keepdims=True)
    row_gate = jnp.sum(jnp.where(place, gate, 0.0), axis=1, keepdims=True)
    copies[2].wait()
    rows_x = dot(mask, tokens_ref[...], plain)
    copies[3].wait()
    rows_dy = dot(mask, grads_ref[...], plain) * row_gate
    copies[4].wait()
    product = grads_ref[...].astype(full) * expert_out_ref[...].astype(full)
    high = product.astype(half)
    low = (product - high.astype(full)).astype(half)
    ones = jnp.ones((8, width), half)
    part = dot(ones, high, contract_last) + dot(ones, low, contract_last)
    first = part.astype(half).astype(full)
    second = (part - first).astype(half).astype(full)
    third = part - first - second
    listed = (iota((width, count), 0) == route).astype(full).astype(half)
    counts = dot(jnp.ones((8, count), half), listed, contract_last)
    line = iota((8, width), 0)
    side = jnp.where(line == 3, counts, 0.0)
    for number, piece in enumerate((first, second, third)):
        side = jnp.where(line == number, piece, side)
    side = side.astype(half)
    for expert in range(experts):
        rows = slice(expert * capacity, (expert + 1) * capacity)
        send_ref[expert, :capacity] = rows_x[rows].astype(half)
        send_ref[expert, capacity : 2 * capacity] = rows_dy[rows].astype(half)
        send_ref[expert, 2 * capacity :] = side
    for copy in copies[5:]:
        copy.wait()


def far(value):
    return pltpu.with_memory_space_constraint(value, pltpu.HBM)


def near(value):
    return pltpu.with_memory_space_constraint(value, pltpu.VMEM)


def prelude(capacity, down_weight, *args):
    experts, count = args[1].shape
    width = args[2].shape[1]
    return pl.pallas_call(
        partial(prelude_kernel, capacity),
        in_specs=[pl.BlockSpec(memory_space=pl.ANY)] * (len(args) + 1),
        out_specs=[pl.BlockSpec(memory_space=pltpu.VMEM)] * 3,
        out_shape=(
            jax.ShapeDtypeStruct((experts, 2 * capacity + 8, width), jnp.bfloat16),
            jax.ShapeDtypeStruct((experts * capacity, count), jnp.bfloat16),
            pltpu.VMEM((down_weight.shape[1] // 2, down_weight.shape[2]), down_weight.dtype),
        ),
        scratch_shapes=[pltpu.VMEM(value.shape, value.dtype) for value in args]
        + [pltpu.SemaphoreType.DMA((len(args) + 2,))],
        compiler_params=pltpu.CompilerParams(vmem_limit_bytes=8 << 20),
        name="prelude",
    )(*[far(value) for value in args], far(down_weight))


def fetch_kernel(pieces, source_ref, after_ref, target_ref, sems):
    planes, hidden = source_ref.shape[1:3]
    size = hidden // pieces
    copies = []
    for plane in range(planes):
        for piece in range(pieces):
            where = (0, plane, pl.ds(piece * size, size))
            copies.append(
                pltpu.make_async_copy(
                    source_ref.at[where], target_ref.at[where], sems.at[len(copies)]
                )
            )
    for copy in copies:
        copy.start()
    for copy in copies:
        copy.wait()


def fetch(weight, after):
    pieces = 4
    return pl.pallas_call(
        partial(fetch_kernel, pieces),
        in_specs=[pl.BlockSpec(memory_space=pl.ANY)] * 2,
        out_specs=pl.BlockSpec(memory_space=pltpu.VMEM),
        out_shape=pltpu.VMEM(weight.shape, weight.dtype),
        scratch_shapes=[pltpu.SemaphoreType.DMA((weight.shape[1] * pieces,))],
        compiler_params=pltpu.CompilerParams(vmem_limit_bytes=1 << 20),
        cost_estimate=pl.CostEstimate(
            flops=0, bytes_accessed=2 * weight.size, transcendentals=0
        ),
        name="fetch",
    )(far(weight), after)


def pre_activation(which, rows, in_ref, part):
    return lax.dot_general(
        in_ref[0, which, part], rows, contract_last, preferred_element_type=jnp.float32
    )


def up_pre_kernel(rows_ref, in_ref, gate_pre_ref, gate_factor_ref, up_factor_ref):
    rows = rows_ref[...]
    size = in_ref.shape[2] // 4
    scale, cubic = math.sqrt(2 / math.pi), 0.044715
    for start in range(0, 4 * size, size):
        part = slice(start, start + size)
        value = gate_pre_ref[part]
        square = value * value
        bend = jnp.tanh(scale * (value + cubic * (square * value)))
        cdf = 0.5 * (1.0 + bend)
        slope = cdf + (0.5 * scale) * value * (1.0 - bend * bend) * (1.0 + 3 * cubic * square)
        up_factor_ref[part] = value * cdf
        gate_factor_ref[part] = slope * pre_activation(1, rows, in_ref, part)


def gate_pre_kernel(rows_ref, in_ref, down_hbm, out_ref, down_ref, sems):
    pieces = sems.shape[0]
    step = down_ref.shape[0] // pieces
    copies = [
        pltpu.make_async_copy(
            down_hbm.at[0, pl.ds(piece * step, step)],
            down_ref.at[pl.ds(piece * step, step)],
            sems.at[piece],
        )
        for piece in range(pieces)
    ]
    for copy in copies:
        copy.start()
    rows = rows_ref[...]
    size = in_ref.shape[2] // 2
    for start in (0, size):
        part = slice(start, start + size)
        out_ref[part] = pre_activation(0, rows, in_ref, part)
    for copy in copies:
        copy.wait()


def hidden_pre(rows, in_near, down_weight=None, gate_pre=None):
    count, width = rows.shape
    hidden = in_near.shape[2]
    near_spec = pl.BlockSpec(memory_space=pltpu.VMEM)
    out = pltpu.VMEM((hidden, count), jnp.float32)
    settings = dict(
        out_specs=[near_spec] * 2,
        compiler_params=pltpu.CompilerParams(vmem_limit_bytes=8 << 20),
        cost_estimate=pl.CostEstimate(
            flops=2 * count * hidden * width, bytes_accessed=2 * hidden * width, transcendentals=0
        ),
    )
    if gate_pre is not None:
        return pl.pallas_call(
            up_pre_kernel,
            in_specs=[near_spec] * 3,
            out_shape=(out, out),
            name="up_pre",
            **settings,
        )(rows, near(in_near), near(gate_pre))
    return pl.pallas_call(
        gate_pre_kernel,
        in_specs=[near_spec] * 2 + [pl.BlockSpec(memory_space=pl.ANY)],
        out_shape=(out, pltpu.VMEM((hidden // 2, width), down_weight.dtype)),
        scratch_shapes=[pltpu.SemaphoreType.DMA((4,))],
        name="gate_pre",
        **settings,
    )(rows, near(in_near), far(down_weight))


def block_of(size, wanted):
    return wanted if size % wanted == 0 else size


def input_grads(rows, in_ref, first, kept_ref, away_ref, block):
    half = kept_ref.shape[0]
    for start in range(0, kept_ref.shape[1], block):
        part, columns = slice(start, start + block), slice(first + start, first + start + block)
        total = jnp.dot(rows[0], in_ref[0, 0, :, columns], preferred_element_type=jnp.float32)
        total += jnp.dot(rows[1], in_ref[0, 1, :, columns], preferred_element_type=jnp.float32)
        kept_ref[:, part] = total[:half]
        away_ref[:, part] = total[half:].astype(jnp.bfloat16)


def hidden_back_kernel(
    block,
    rows_ref,
    gate_factor_ref,
    up_factor_ref,
    in_ref,
    down_ref,
    other_ref,
    gate_ref,
    up_ref,
    gate_rows_ref,
    up_rows_ref,
    kept_ref,
    away_ref,
):
    size = down_ref.shape[0]
    rows = rows_ref[...]
    for number, weight_ref in enumerate((down_ref, other_ref)):
        part = slice(number * size, (number + 1) * size)
        grad = lax.dot_general(
            weight_ref[...], rows, contract_last, preferred_element_type=jnp.float32
        )
        gate_ref[part] = (grad * gate_factor_ref[part]).astype(jnp.bfloat16)
        up_ref[part] = (grad * up_factor_ref[part]).astype(jnp.bfloat16)
    gate_rows_ref[...] = gate_ref[...].T
    up_rows_ref[...] = up_ref[...].T
    input_grads((gate_rows_ref[...], up_rows_ref[...]), in_ref, 0, kept_ref, away_ref, block)


def rest_back_kernel(block, gate_rows_ref, up_rows_ref, in_ref, kept_ref, away_ref):
    first = in_ref.shape[3] - kept_ref.shape[1]
    input_grads((gate_rows_ref[...], up_rows_ref[...]), in_ref, first, kept_ref, away_ref, block)


def hidden_back(rows, gate_factor, up_factor, in_near, downs):
    count, width = rows.shape
    hidden = in_near.shape[2]
    near_spec = pl.BlockSpec(memory_space=pltpu.VMEM)
    return pl.pallas_call(
        partial(hidden_back_kernel, width // 2),
        in_specs=[near_spec] * 6,
        out_specs=[near_spec] * 6,
        out_shape=(
            pltpu.VMEM((hidden, count), jnp.bfloat16),
            pltpu.VMEM((hidden, count), jnp.bfloat16),
            pltpu.VMEM((count, hidden), jnp.bfloat16),
            pltpu.VMEM((count, hidden), jnp.bfloat16),
            pltpu.VMEM((count // 2, width // 2), jnp.float32),
            pltpu.VMEM((count // 2, width // 2), jnp.bfloat16),
        ),
        compiler_params=pltpu.CompilerParams(vmem_limit_bytes=12 << 20),
        cost_estimate=pl.CostEstimate(
            flops=4 * count * hidden * width,
            bytes_accessed=4 * hidden * width,
            transcendentals=count * hidden,
        ),
        name="hidden_back",
    )(rows, near(gate_factor), near(up_factor), near(in_near), *map(near, downs))


def rest_back(gate_rows, up_rows, in_near):
    count, hidden = gate_rows.shape
    width = in_near.shape[3]
    near_spec = pl.BlockSpec(memory_space=pltpu.VMEM)
    return pl.pallas_call(
        partial(rest_back_kernel, width // 2),
        in_specs=[near_spec] * 3,
        out_specs=[near_spec] * 2,
        out_shape=(
            pltpu.VMEM((count // 2, width // 2), jnp.float32),
            pltpu.VMEM((count // 2, width // 2), jnp.bfloat16),
        ),
        compiler_params=pltpu.CompilerParams(vmem_limit_bytes=12 << 20),
        cost_estimate=pl.CostEstimate(
            flops=2 * count * hidden * width, bytes_accessed=2 * hidden * width, transcendentals=0
        ),
        name="rest_back",
    )(near(gate_rows), near(up_rows), near(in_near))


def half_kernel(grad_ref, rows_ref, *refs):
    refs[-1][0, 0] = jnp.dot(
        grad_ref[...], rows_ref[...], preferred_element_type=jnp.float32
    ).astype(jnp.bfloat16)


def half_weight_grad(which, grad, rows, partly=None):
    hidden, count = grad.shape
    width = rows.shape[1]
    block = block_of(hidden, 640)
    given = [] if partly is None else [partly]
    return pl.pallas_call(
        half_kernel,
        grid=(hidden // block,),
        in_specs=[
            pl.BlockSpec((block, count), lambda j: (j, 0)),
            pl.BlockSpec((count, width), lambda j: (0, 0)),
        ]
        + [pl.BlockSpec(memory_space=pl.ANY)] * len(given),
        out_specs=pl.BlockSpec((1, 1, block, width), lambda j: (0, which, j, 0)),
        out_shape=jax.ShapeDtypeStruct((1, 2, hidden, width), jnp.bfloat16),
        input_output_aliases={2: 0} if given else {},
        compiler_params=pltpu.CompilerParams(vmem_limit_bytes=20 << 20),
        cost_estimate=pl.CostEstimate(
            flops=2 * count * hidden * width, bytes_accessed=2 * hidden * width, transcendentals=0
        ),
        name="weight_grad_half",
    )(grad, rows, *given)


def aligned_device(
    tokens, out_grad, expert_out, router_probs, expert_index, in_weight, down_weight, router_weight
):
    token_count, width = tokens.shape
    experts = router_probs.shape[1]
    capacity = (5 * token_count + 4 * experts - 1) // (4 * experts)
    groups = lax.axis_size("dp")
    full_width = experts * width
    probs = router_probs.T
    route = expert_index.reshape(1, token_count)
    send, mask, second_down = prelude(
        capacity, down_weight, route, probs, tokens, out_grad, expert_out
    )
    got = lax.all_to_all(send, "expert", split_axis=0, concat_axis=0, tiled=True)
    in_near = fetch(in_weight, got)

    def as_rows(value):
        return value.transpose(1, 0, 2).reshape(value.shape[1], full_width)

    row_tokens, all_grads = as_rows(got[:, :capacity]), as_rows(got[:, capacity:])
    first, last = distances()[:-1], distances()[-1:]
    row_tokens = gather_groups(row_tokens, first)
    all_grads = gather_groups(all_grads, first)
    row_tokens = gather_groups(row_tokens, last)
    all_grads = gather_groups(all_grads, last).reshape(groups, capacity + 8, full_width)
    gate_pre, first_down = hidden_pre(row_tokens, in_near, down_weight)
    gate_factor, up_factor = hidden_pre(row_tokens, in_near, gate_pre=gate_pre)
    row_grads = all_grads[:, :capacity].reshape(groups * capacity, full_width)
    gate_dot = jnp.sum(got[:, 2 * capacity : 2 * capacity + 3].astype(jnp.float32), axis=(0, 1))
    counts = jnp.sum(all_grads[:, capacity + 3, :experts].astype(jnp.float32), axis=0)

    gate_grad, up_grad, gate_rows, up_rows, kept, away = hidden_back(
        row_grads, gate_factor, up_factor, in_near, (first_down, second_down)
    )
    more_kept, more_away = rest_back(gate_rows, up_rows, in_near)
    summed = kept + swap(away, 1).astype(jnp.float32)
    more = more_kept + swap(more_away, 1).astype(jnp.float32)
    going = reduce_groups(jnp.concatenate([summed, more], axis=1), 2).astype(jnp.bfloat16)
    going = going.reshape(capacity, experts, width).transpose(1, 0, 2)
    returned = lax.all_to_all(going, "expert", split_axis=0, concat_axis=0, tiled=True)
    weight_grad = half_weight_grad(0, gate_grad, row_tokens)
    weight_grad = half_weight_grad(1, up_grad, row_tokens, weight_grad)

    chosen = (lax.broadcasted_iota(jnp.int32, (experts, token_count), 0) == route).astype(jnp.float32)
    prob_grad = chosen * gate_dot[None, :] + aux_coef * experts * counts[:, None] / (
        token_count * groups
    )
    logit_grad = probs * (prob_grad - jnp.sum(probs * prob_grad, axis=0, keepdims=True))
    logit_grad = logit_grad.astype(jnp.bfloat16)
    router_grad = jnp.dot(logit_grad, tokens, preferred_element_type=jnp.float32)
    for distance in distances()[::-1]:
        router_grad = router_grad + swap(router_grad, distance)
    router_term = lax.dot_general(
        logit_grad, router_weight, (((0,), (1,)), ((), ())), preferred_element_type=jnp.float32
    )
    combined = lax.dot_general(
        mask,
        returned.reshape(experts * capacity, width),
        contract_first,
        preferred_element_type=jnp.float32,
    )
    token_grad = (combined + router_term).astype(jnp.bfloat16)
    return (token_grad, weight_grad, router_grad.T)


def per_device(tokens, out_grad, expert_out, router_probs, *rest):
    token_count, width = tokens.shape
    experts = router_probs.shape[1]
    capacity = (5 * token_count + 4 * experts - 1) // (4 * experts)
    aligned = token_count == width and width % 128 == 0 and capacity % 8 == 0 and experts % 8 == 0
    if not aligned:
        return general_device(tokens, out_grad, expert_out, router_probs, *rest)
    return aligned_device(tokens, out_grad, expert_out, router_probs, *rest)


def solution(mesh):
    in_specs = (
        P("dp", "expert"),
        P("dp", "expert"),
        P("dp", "expert"),
        P("dp", None),
        P("dp", None),
        P("expert", None, "dp", None),
        P("expert", "dp", None),
        P("expert", None),
    )
    out_specs = (P("dp", "expert"), P("expert", None, "dp", None), P("expert", None))
    return jax.shard_map(
        per_device, mesh=mesh, in_specs=in_specs, out_specs=out_specs, check_vma=False
    )
```

```python
import math
from functools import partial

import jax
import jax.numpy as jnp
from jax import lax
from jax.experimental import pallas as pl
from jax.experimental.pallas import tpu as pltpu
from jax.sharding import PartitionSpec as P


aux_coef = 0.2
contract_last = (((1,), (1,)), ((), ()))
contract_first = (((0,), (0,)), ((), ()))


def slot_numbers(routes):
    width = routes.shape[1]
    same_expert = routes[:, :, None] == routes[:, None, :]
    position = jnp.arange(width, dtype=jnp.int32)
    before = position[None, :] < position[:, None]
    return jnp.sum((same_expert & before[None]).astype(jnp.int32), axis=2)


def one_hot(routes, slot_ids, experts, capacity):
    expert_hit = routes[..., None] == jnp.arange(experts, dtype=jnp.int32)
    slot_hit = slot_ids[..., None] == jnp.arange(capacity, dtype=jnp.int32)
    return (expert_hit[..., :, None] & slot_hit[..., None, :]).astype(jnp.float32)


def gelu_parts(pre_act, upstream):
    gelu_value, pullback = jax.vjp(partial(jax.nn.gelu, approximate=True), pre_act)
    return (gelu_value, pullback(upstream)[0])


def swap(value, distance):
    size = lax.axis_size("dp")
    return lax.ppermute(value, "dp", [(i, i ^ distance) for i in range(size)])


def distances():
    found, distance = [], lax.axis_size("dp") // 2
    while distance:
        found.append(distance)
        distance //= 2
    return found


def gather_groups(block, given=()):
    for distance in given or distances():
        block = jnp.concatenate([block, swap(block, distance)], axis=0)
    return block


def reduce_groups(total, first=1):
    order = [distance for distance in distances()[::-1] if distance >= first]
    for distance in order:
        half = total.shape[0] // 2
        away = swap(total[half:].astype(jnp.bfloat16), distance)
        total = total[:half] + away.astype(jnp.float32)
    return total


def weight_grad_kernel(gate_ref, up_ref, rows_ref, out_ref):
    rows = rows_ref[...]
    out_ref[0, 0] = lax.dot_general(
        gate_ref[...], rows, contract_first, preferred_element_type=jnp.float32
    ).astype(jnp.bfloat16)
    out_ref[0, 1] = lax.dot_general(
        up_ref[...], rows, contract_first, preferred_element_type=jnp.float32
    ).astype(jnp.bfloat16)


def weight_grads(gate_grad, up_grad, rows):
    count, hidden = gate_grad.shape
    width = rows.shape[1]
    block = 256 if hidden % 256 == 0 else hidden
    return pl.pallas_call(
        weight_grad_kernel,
        grid=(hidden // block,),
        in_specs=[
            pl.BlockSpec((count, block), lambda j: (0, j)),
            pl.BlockSpec((count, block), lambda j: (0, j)),
            pl.BlockSpec((count, width), lambda j: (0, 0)),
        ],
        out_specs=pl.BlockSpec((1, 2, block, width), lambda j: (0, 0, j, 0)),
        out_shape=jax.ShapeDtypeStruct((1, 2, hidden, width), jnp.bfloat16),
        cost_estimate=pl.CostEstimate(
            flops=4 * count * hidden * width,
            bytes_accessed=4 * hidden * width,
            transcendentals=0,
        ),
        name="weight_grads",
    )(gate_grad, up_grad, rows)


def split_float(value):
    high = lax.reduce_precision(value, 8, 7)
    middle = lax.reduce_precision(value - high, 8, 7)
    return jnp.stack([high, middle, value - high - middle]).astype(jnp.bfloat16)


def general_device(
    tokens, out_grad, expert_out, router_probs, expert_index, in_weight, down_weight, router_weight
):
    token_count, feature_width = tokens.shape
    experts = router_probs.shape[1]
    capacity = (5 * token_count + 4 * experts - 1) // (4 * experts)
    groups = lax.axis_size("dp")
    routes = expert_index[:, 0]
    slot_ids = slot_numbers(routes[None, :])[0]
    dispatch_mask = one_hot(routes, slot_ids, experts, capacity)
    mask_half = dispatch_mask.astype(jnp.bfloat16)
    chosen = jnp.sum(dispatch_mask, axis=2)

    def exchange(value):
        return lax.all_to_all(value, "expert", split_axis=0, concat_axis=2, tiled=True)[0]

    send_tokens = jnp.einsum(
        "tec,tf->ecf", mask_half, tokens, preferred_element_type=jnp.float32
    ).astype(jnp.bfloat16)
    got_tokens = exchange(send_tokens)

    gate = jnp.sum(router_probs * chosen, axis=1)
    gated_dy = (gate[:, None] * out_grad.astype(jnp.float32)).astype(jnp.bfloat16)
    send_grads = jnp.einsum(
        "tec,tf->ecf", mask_half, gated_dy, preferred_element_type=jnp.float32
    ).astype(jnp.bfloat16)
    partial_dot = jnp.sum(out_grad.astype(jnp.float32) * expert_out.astype(jnp.float32), axis=1)
    dot_rows = token_count // feature_width
    pieces = split_float(partial_dot).reshape(3 * dot_rows, feature_width)
    local_counts = jnp.sum(chosen, axis=0)
    count_row = jnp.pad(local_counts.astype(jnp.bfloat16)[None], ((0, 0), (0, feature_width - experts)))
    side = jnp.concatenate([pieces, count_row], axis=0)
    side_rows = -(-(capacity + side.shape[0]) // 8) * 8 - capacity
    side = jnp.pad(side, ((0, side_rows - side.shape[0]), (0, 0)))
    send_grads = jnp.concatenate(
        [send_grads, jnp.broadcast_to(side[None], (experts, side_rows, feature_width))], axis=1
    )
    got_grads = exchange(send_grads)

    row_tokens = gather_groups(got_tokens)
    all_grads = gather_groups(got_grads).reshape(groups, capacity + side_rows, -1)
    row_grads = all_grads[:, :capacity].reshape(groups * capacity, -1)
    own_side = got_grads[capacity:].astype(jnp.float32)
    gate_dot = jnp.sum(
        own_side[: 3 * dot_rows].reshape(3, dot_rows, experts, feature_width), axis=(0, 2)
    ).reshape(token_count)
    counts = jnp.sum(all_grads[:, capacity + 3 * dot_rows, :experts].astype(jnp.float32), axis=0)

    gate_weight = in_weight[0, 0]
    up_weight = in_weight[0, 1]
    gate_pre = lax.dot_general(
        row_tokens, gate_weight, contract_last, preferred_element_type=jnp.float32
    )
    up_pre = lax.dot_general(
        row_tokens, up_weight, contract_last, preferred_element_type=jnp.float32
    )
    hidden_grad = lax.dot_general(
        row_grads, down_weight[0], contract_last, preferred_element_type=jnp.float32
    )
    gate_act, gate_back = gelu_parts(gate_pre, hidden_grad * up_pre)
    gate_grad = gate_back.astype(jnp.bfloat16)
    up_grad = (hidden_grad * gate_act).astype(jnp.bfloat16)
    term = jnp.dot(gate_grad, gate_weight, preferred_element_type=jnp.float32)
    term = term + jnp.dot(up_grad, up_weight, preferred_element_type=jnp.float32)
    summed = reduce_groups(term)
    going = summed.astype(jnp.bfloat16).reshape(capacity, experts, feature_width)
    returned = lax.all_to_all(
        going.transpose(1, 0, 2), "expert", split_axis=0, concat_axis=0, tiled=True
    )
    weight_grad = weight_grads(gate_grad, up_grad, row_tokens)

    prob_grad = chosen * gate_dot[:, None] + aux_coef * experts * counts[None, :] / (
        token_count * groups
    )
    logit_grad = router_probs * (
        prob_grad - jnp.sum(router_probs * prob_grad, axis=1, keepdims=True)
    )
    logit_grad = logit_grad.astype(jnp.bfloat16)
    router_grad = lax.dot_general(
        tokens, logit_grad, contract_first, preferred_element_type=jnp.float32
    )
    for distance in distances():
        router_grad = router_grad + swap(router_grad, distance)
    router_term = lax.dot_general(
        logit_grad, router_weight, contract_last, preferred_element_type=jnp.float32
    )
    combined = jnp.einsum(
        "tec,ecf->tf", mask_half, returned, preferred_element_type=jnp.float32
    )
    token_grad = (combined + router_term).astype(jnp.bfloat16)
    return (token_grad, weight_grad, router_grad)


def prelude_kernel(
    capacity,
    route_hbm,
    probs_hbm,
    tokens_hbm,
    grads_hbm,
    expert_out_hbm,
    down_hbm,
    send_ref,
    place_ref,
    down_ref,
    route_ref,
    probs_ref,
    tokens_ref,
    grads_ref,
    expert_out_ref,
    sems,
):
    sources = (route_hbm, probs_hbm, tokens_hbm, grads_hbm, expert_out_hbm)
    targets = (route_ref, probs_ref, tokens_ref, grads_ref, expert_out_ref)
    copies = [
        pltpu.make_async_copy(source, target, sems.at[number])
        for number, (source, target) in enumerate(zip(sources, targets))
    ]
    pieces = sems.shape[0] - len(copies)
    half = down_ref.shape[0]
    size = half // pieces
    for piece in range(pieces):
        copies.append(
            pltpu.make_async_copy(
                down_hbm.at[0, pl.ds(half + piece * size, size)],
                down_ref.at[pl.ds(piece * size, size)],
                sems.at[len(copies)],
            )
        )
    for copy in copies:
        copy.start()
    experts, count = probs_ref.shape
    width = tokens_ref.shape[1]
    half, full = jnp.bfloat16, jnp.float32
    iota = lambda shape, axis: lax.broadcasted_iota(jnp.int32, shape, axis)
    dot = partial(lax.dot_general, preferred_element_type=full)
    plain = (((1,), (0,)), ((), ()))
    square = (count, count)
    earlier = (iota(square, 0) < iota(square, 1)).astype(full).astype(half)
    copies[0].wait()
    route = route_ref[...]
    hit = iota((experts, count), 0) == route
    before = dot(hit.astype(full).astype(half), earlier, plain)
    slot = jnp.sum(jnp.where(hit, before, 0.0), axis=0, keepdims=True)
    place = iota((experts * capacity, count), 0) == route * capacity + slot.astype(jnp.int32)
    mask = place.astype(full).astype(half)
    place_ref[...] = mask
    copies[1].wait()
    gate = jnp.sum(jnp.where(hit, probs_ref[...], 0.0), axis=0, keepdims=True)
    row_gate = jnp.sum(jnp.where(place, gate, 0.0), axis=1, keepdims=True)
    copies[2].wait()
    rows_x = dot(mask, tokens_ref[...], plain)
    copies[3].wait()
    rows_dy = dot(mask, grads_ref[...], plain) * row_gate
    copies[4].wait()
    product = grads_ref[...].astype(full) * expert_out_ref[...].astype(full)
    high = product.astype(half)
    low = (product - high.astype(full)).astype(half)
    ones = jnp.ones((8, width), half)
    part = dot(ones, high, contract_last) + dot(ones, low, contract_last)
    first = part.astype(half).astype(full)
    second = (part - first).astype(half).astype(full)
    third = part - first - second
    listed = (iota((width, count), 0) == route).astype(full).astype(half)
    counts = dot(jnp.ones((8, count), half), listed, contract_last)
    line = iota((8, width), 0)
    side = jnp.where(line == 3, counts, 0.0)
    for number, piece in enumerate((first, second, third)):
        side = jnp.where(line == number, piece, side)
    side = side.astype(half)
    for expert in range(experts):
        rows = slice(expert * capacity, (expert + 1) * capacity)
        send_ref[expert, :capacity] = rows_x[rows].astype(half)
        send_ref[expert, capacity : 2 * capacity] = rows_dy[rows].astype(half)
        send_ref[expert, 2 * capacity :] = side
    for copy in copies[5:]:
        copy.wait()


def far(value):
    return pltpu.with_memory_space_constraint(value, pltpu.HBM)


def near(value):
    return pltpu.with_memory_space_constraint(value, pltpu.VMEM)


def prelude(capacity, down_weight, *args):
    experts, count = args[1].shape
    width = args[2].shape[1]
    return pl.pallas_call(
        partial(prelude_kernel, capacity),
        in_specs=[pl.BlockSpec(memory_space=pl.ANY)] * (len(args) + 1),
        out_specs=[pl.BlockSpec(memory_space=pltpu.VMEM)] * 3,
        out_shape=(
            jax.ShapeDtypeStruct((experts, 2 * capacity + 8, width), jnp.bfloat16),
            jax.ShapeDtypeStruct((experts * capacity, count), jnp.bfloat16),
            pltpu.VMEM((down_weight.shape[1] // 2, down_weight.shape[2]), down_weight.dtype),
        ),
        scratch_shapes=[pltpu.VMEM(value.shape, value.dtype) for value in args]
        + [pltpu.SemaphoreType.DMA((len(args) + 2,))],
        compiler_params=pltpu.CompilerParams(vmem_limit_bytes=8 << 20),
        name="prelude",
    )(*[far(value) for value in args], far(down_weight))


def fetch_kernel(pieces, source_ref, after_ref, target_ref, sems):
    planes, hidden = source_ref.shape[1:3]
    size = hidden // pieces
    copies = []
    for plane in range(planes):
        for piece in range(pieces):
            where = (0, plane, pl.ds(piece * size, size))
            copies.append(
                pltpu.make_async_copy(
                    source_ref.at[where], target_ref.at[where], sems.at[len(copies)]
                )
            )
    for copy in copies:
        copy.start()
    for copy in copies:
        copy.wait()


def fetch(weight, after):
    pieces = 4
    return pl.pallas_call(
        partial(fetch_kernel, pieces),
        in_specs=[pl.BlockSpec(memory_space=pl.ANY)] * 2,
        out_specs=pl.BlockSpec(memory_space=pltpu.VMEM),
        out_shape=pltpu.VMEM(weight.shape, weight.dtype),
        scratch_shapes=[pltpu.SemaphoreType.DMA((weight.shape[1] * pieces,))],
        compiler_params=pltpu.CompilerParams(vmem_limit_bytes=1 << 20),
        cost_estimate=pl.CostEstimate(
            flops=0, bytes_accessed=2 * weight.size, transcendentals=0
        ),
        name="fetch",
    )(far(weight), after)


def pre_activation(which, rows, in_ref, part):
    return lax.dot_general(
        in_ref[0, which, part], rows, contract_last, preferred_element_type=jnp.float32
    )


def up_pre_kernel(rows_ref, in_ref, gate_pre_ref, gate_factor_ref, up_factor_ref):
    rows = rows_ref[...]
    size = in_ref.shape[2] // 4
    scale, cubic = math.sqrt(2 / math.pi), 0.044715
    for start in range(0, 4 * size, size):
        part = slice(start, start + size)
        value = gate_pre_ref[part]
        square = value * value
        bend = jnp.tanh(scale * (value + cubic * (square * value)))
        cdf = 0.5 * (1.0 + bend)
        slope = cdf + (0.5 * scale) * value * (1.0 - bend * bend) * (1.0 + 3 * cubic * square)
        up_factor_ref[part] = value * cdf
        gate_factor_ref[part] = slope * pre_activation(1, rows, in_ref, part)


def gate_pre_kernel(rows_ref, in_ref, down_hbm, out_ref, down_ref, sems):
    pieces = sems.shape[0]
    step = down_ref.shape[0] // pieces
    copies = [
        pltpu.make_async_copy(
            down_hbm.at[0, pl.ds(piece * step, step)],
            down_ref.at[pl.ds(piece * step, step)],
            sems.at[piece],
        )
        for piece in range(pieces)
    ]
    for copy in copies:
        copy.start()
    rows = rows_ref[...]
    size = in_ref.shape[2] // 2
    for start in (0, size):
        part = slice(start, start + size)
        out_ref[part] = pre_activation(0, rows, in_ref, part)
    for copy in copies:
        copy.wait()


def hidden_pre(rows, in_near, down_weight=None, gate_pre=None):
    count, width = rows.shape
    hidden = in_near.shape[2]
    near_spec = pl.BlockSpec(memory_space=pltpu.VMEM)
    out = pltpu.VMEM((hidden, count), jnp.float32)
    settings = dict(
        out_specs=[near_spec] * 2,
        compiler_params=pltpu.CompilerParams(vmem_limit_bytes=8 << 20),
        cost_estimate=pl.CostEstimate(
            flops=2 * count * hidden * width, bytes_accessed=2 * hidden * width, transcendentals=0
        ),
    )
    if gate_pre is not None:
        return pl.pallas_call(
            up_pre_kernel,
            in_specs=[near_spec] * 3,
            out_shape=(out, out),
            name="up_pre",
            **settings,
        )(rows, near(in_near), near(gate_pre))
    return pl.pallas_call(
        gate_pre_kernel,
        in_specs=[near_spec] * 2 + [pl.BlockSpec(memory_space=pl.ANY)],
        out_shape=(out, pltpu.VMEM((hidden // 2, width), down_weight.dtype)),
        scratch_shapes=[pltpu.SemaphoreType.DMA((4,))],
        name="gate_pre",
        **settings,
    )(rows, near(in_near), far(down_weight))


def block_of(size, wanted):
    return wanted if size % wanted == 0 else size


def input_grads(rows, in_ref, first, kept_ref, away_ref, block):
    half = kept_ref.shape[0]
    for start in range(0, kept_ref.shape[1], block):
        part, columns = slice(start, start + block), slice(first + start, first + start + block)
        total = jnp.dot(rows[0], in_ref[0, 0, :, columns], preferred_element_type=jnp.float32)
        total += jnp.dot(rows[1], in_ref[0, 1, :, columns], preferred_element_type=jnp.float32)
        kept_ref[:, part] = total[:half]
        away_ref[:, part] = total[half:].astype(jnp.bfloat16)


def hidden_back_kernel(
    block,
    rows_ref,
    gate_factor_ref,
    up_factor_ref,
    in_ref,
    down_ref,
    other_ref,
    gate_ref,
    up_ref,
    gate_rows_ref,
    up_rows_ref,
    kept_ref,
    away_ref,
):
    size = down_ref.shape[0]
    rows = rows_ref[...]
    for number, weight_ref in enumerate((down_ref, other_ref)):
        part = slice(number * size, (number + 1) * size)
        grad = lax.dot_general(
            weight_ref[...], rows, contract_last, preferred_element_type=jnp.float32
        )
        gate_ref[part] = (grad * gate_factor_ref[part]).astype(jnp.bfloat16)
        up_ref[part] = (grad * up_factor_ref[part]).astype(jnp.bfloat16)
    gate_rows_ref[...] = gate_ref[...].T
    up_rows_ref[...] = up_ref[...].T
    input_grads((gate_rows_ref[...], up_rows_ref[...]), in_ref, 0, kept_ref, away_ref, block)


def rest_back_kernel(block, gate_rows_ref, up_rows_ref, in_ref, kept_ref, away_ref):
    first = in_ref.shape[3] - kept_ref.shape[1]
    input_grads((gate_rows_ref[...], up_rows_ref[...]), in_ref, first, kept_ref, away_ref, block)


def hidden_back(rows, gate_factor, up_factor, in_near, downs):
    count, width = rows.shape
    hidden = in_near.shape[2]
    near_spec = pl.BlockSpec(memory_space=pltpu.VMEM)
    return pl.pallas_call(
        partial(hidden_back_kernel, width // 2),
        in_specs=[near_spec] * 6,
        out_specs=[near_spec] * 6,
        out_shape=(
            pltpu.VMEM((hidden, count), jnp.bfloat16),
            pltpu.VMEM((hidden, count), jnp.bfloat16),
            pltpu.VMEM((count, hidden), jnp.bfloat16),
            pltpu.VMEM((count, hidden), jnp.bfloat16),
            pltpu.VMEM((count // 2, width // 2), jnp.float32),
            pltpu.VMEM((count // 2, width // 2), jnp.bfloat16),
        ),
        compiler_params=pltpu.CompilerParams(vmem_limit_bytes=12 << 20),
        cost_estimate=pl.CostEstimate(
            flops=4 * count * hidden * width,
            bytes_accessed=4 * hidden * width,
            transcendentals=count * hidden,
        ),
        name="hidden_back",
    )(rows, near(gate_factor), near(up_factor), near(in_near), *map(near, downs))


def rest_back(gate_rows, up_rows, in_near):
    count, hidden = gate_rows.shape
    width = in_near.shape[3]
    near_spec = pl.BlockSpec(memory_space=pltpu.VMEM)
    return pl.pallas_call(
        partial(rest_back_kernel, width // 2),
        in_specs=[near_spec] * 3,
        out_specs=[near_spec] * 2,
        out_shape=(
            pltpu.VMEM((count // 2, width // 2), jnp.float32),
            pltpu.VMEM((count // 2, width // 2), jnp.bfloat16),
        ),
        compiler_params=pltpu.CompilerParams(vmem_limit_bytes=12 << 20),
        cost_estimate=pl.CostEstimate(
            flops=2 * count * hidden * width, bytes_accessed=2 * hidden * width, transcendentals=0
        ),
        name="rest_back",
    )(near(gate_rows), near(up_rows), near(in_near))


def finish_kernel(mask_ref, rows_ref, term_ref, out_ref):
    combined = lax.dot_general(
        mask_ref[...], rows_ref[...], contract_first, preferred_element_type=jnp.float32
    )
    out_ref[...] = (combined + term_ref[...]).astype(jnp.bfloat16)


def finish(mask, rows, term):
    return pl.pallas_call(
        finish_kernel,
        out_shape=jax.ShapeDtypeStruct(term.shape, jnp.bfloat16),
        compiler_params=pltpu.CompilerParams(vmem_limit_bytes=4 << 20),
        name="finish",
    )(mask, rows, term)


def half_kernel(grad_ref, rows_ref, *refs):
    refs[-1][0, 0] = jnp.dot(
        grad_ref[...], rows_ref[...], preferred_element_type=jnp.float32
    ).astype(jnp.bfloat16)


def half_weight_grad(which, grad, rows, partly=None):
    hidden, count = grad.shape
    width = rows.shape[1]
    block = block_of(hidden, 640)
    given = [] if partly is None else [partly]
    return pl.pallas_call(
        half_kernel,
        grid=(hidden // block,),
        in_specs=[
            pl.BlockSpec((block, count), lambda j: (j, 0)),
            pl.BlockSpec((count, width), lambda j: (0, 0)),
        ]
        + [pl.BlockSpec(memory_space=pl.ANY)] * len(given),
        out_specs=pl.BlockSpec((1, 1, block, width), lambda j: (0, which, j, 0)),
        out_shape=jax.ShapeDtypeStruct((1, 2, hidden, width), jnp.bfloat16),
        input_output_aliases={2: 0} if given else {},
        compiler_params=pltpu.CompilerParams(vmem_limit_bytes=20 << 20),
        cost_estimate=pl.CostEstimate(
            flops=2 * count * hidden * width, bytes_accessed=2 * hidden * width, transcendentals=0
        ),
        name="weight_grad_half",
    )(grad, rows, *given)


def aligned_device(
    tokens, out_grad, expert_out, router_probs, expert_index, in_weight, down_weight, router_weight
):
    token_count, width = tokens.shape
    experts = router_probs.shape[1]
    capacity = (5 * token_count + 4 * experts - 1) // (4 * experts)
    groups = lax.axis_size("dp")
    full_width = experts * width
    probs = router_probs.T
    route = expert_index.reshape(1, token_count)
    send, mask, second_down = prelude(
        capacity, down_weight, route, probs, tokens, out_grad, expert_out
    )
    got = lax.all_to_all(send, "expert", split_axis=0, concat_axis=0, tiled=True)
    in_near = fetch(in_weight, got)

    def as_rows(value):
        return value.transpose(1, 0, 2).reshape(value.shape[1], full_width)

    row_tokens, all_grads = as_rows(got[:, :capacity]), as_rows(got[:, capacity:])
    first, last = distances()[:-1], distances()[-1:]
    row_tokens = gather_groups(row_tokens, first)
    all_grads = gather_groups(all_grads, first)
    row_tokens = gather_groups(row_tokens, last)
    all_grads = gather_groups(all_grads, last).reshape(groups, capacity + 8, full_width)
    gate_pre, first_down = hidden_pre(row_tokens, in_near, down_weight)
    gate_factor, up_factor = hidden_pre(row_tokens, in_near, gate_pre=gate_pre)
    row_grads = all_grads[:, :capacity].reshape(groups * capacity, full_width)
    gate_dot = jnp.sum(got[:, 2 * capacity : 2 * capacity + 3].astype(jnp.float32), axis=(0, 1))
    counts = jnp.sum(all_grads[:, capacity + 3, :experts].astype(jnp.float32), axis=0)

    gate_grad, up_grad, gate_rows, up_rows, kept, away = hidden_back(
        row_grads, gate_factor, up_factor, in_near, (first_down, second_down)
    )
    more_kept, more_away = rest_back(gate_rows, up_rows, in_near)
    summed = kept + swap(away, 1).astype(jnp.float32)
    more = more_kept + swap(more_away, 1).astype(jnp.float32)
    going = reduce_groups(jnp.concatenate([summed, more], axis=1), 2).astype(jnp.bfloat16)
    going = going.reshape(capacity, experts, width).transpose(1, 0, 2)
    returned = lax.all_to_all(going, "expert", split_axis=0, concat_axis=0, tiled=True)
    weight_grad = half_weight_grad(0, gate_grad, row_tokens)
    weight_grad = half_weight_grad(1, up_grad, row_tokens, weight_grad)

    chosen = (lax.broadcasted_iota(jnp.int32, (experts, token_count), 0) == route).astype(jnp.float32)
    prob_grad = chosen * gate_dot[None, :] + aux_coef * experts * counts[:, None] / (
        token_count * groups
    )
    logit_grad = probs * (prob_grad - jnp.sum(probs * prob_grad, axis=0, keepdims=True))
    logit_grad = logit_grad.astype(jnp.bfloat16)
    router_grad = jnp.dot(logit_grad, tokens, preferred_element_type=jnp.float32)
    for distance in distances()[::-1]:
        router_grad = router_grad + swap(router_grad, distance)
    router_term = lax.dot_general(
        logit_grad, router_weight, (((0,), (1,)), ((), ())), preferred_element_type=jnp.float32
    )
    token_grad = finish(mask, returned.reshape(experts * capacity, width), router_term)
    return (token_grad, weight_grad, router_grad.T)


def per_device(tokens, out_grad, expert_out, router_probs, *rest):
    token_count, width = tokens.shape
    experts = router_probs.shape[1]
    capacity = (5 * token_count + 4 * experts - 1) // (4 * experts)
    aligned = token_count == width and width % 128 == 0 and capacity % 8 == 0 and experts % 8 == 0
    if not aligned:
        return general_device(tokens, out_grad, expert_out, router_probs, *rest)
    return aligned_device(tokens, out_grad, expert_out, router_probs, *rest)


def solution(mesh):
    in_specs = (
        P("dp", "expert"),
        P("dp", "expert"),
        P("dp", "expert"),
        P("dp", None),
        P("dp", None),
        P("expert", None, "dp", None),
        P("expert", "dp", None),
        P("expert", None),
    )
    out_specs = (P("dp", "expert"), P("expert", None, "dp", None), P("expert", None))
    return jax.shard_map(
        per_device, mesh=mesh, in_specs=in_specs, out_specs=out_specs, check_vma=False
    )
```
